32 devices in a mesh: wave: 4 (over y, x), row: 8 (over z, core).
Axes of the slice: x: 2, y: 2, z: 4, core: 2. Of those that a mesh axis runs over, the one named last changes fastest.
Arguments:
- plane_waves: float32 [2, 4, 2048, 2048], P(None, 'wave', 'row'), may hold values from -6 to 6
- transmission: float32 [1, 2, 2048, 2048], P(None, None, 'row')
- wave_index: int32 [4, 2], P('wave'), may hold values from -32 to 31
- wave_weight: float32 [4], P('wave'), may hold values from 0.3 to 3
- wave_phase: float32 [4], P('wave'), may hold values from -3.140625 to 3.140625
- probe_pos: int32 [64, 2], replicated, may hold values from 0 to 2047, as said below
Outputs:
- diffraction: float32 [64, 128, 128], P('row', 'wave')
The draws below stay inside these ranges and needn't reach their ends.
Inputs may be any that keep to these rules, and one draw needn't show every extreme that they name: `probe_pos`: the probes numbered j * 8 to (j + 1) * 8 - 1 have their grid row (first entry) in j * 256 to (j + 1) * 256 - 1; the second entry is the grid column.
All inputs are finite; a program needn't handle non-finite values.
Results may differ from the reference program's by a relative error of at most 0.0003.
Values sent between devices are 32-bit elements; how exact they have to be, the bound alone decides.
No kernel may reach another device: no remote copies, remote signals or barrier semaphores. Data moves between devices by JAX's collectives and lax.ppermute only.
A program may use at most 128 MiB of HBM per device.

```python
import math
import jax
import jax.numpy as jnp
from jax import lax

GRID = 2048
FACTOR = 16
WINDOW = 128
HALF = 64
SLICES = 1
WAVES = 4
ROWS_DEV = 256
PROBES_DEV = 8
PROBES = 64


def draw_transmission(key, part):
    key_amp, key_shift = jax.random.split(key)
    amplitude = jax.random.uniform(key_amp, (SLICES, GRID, GRID), jnp.float32, 0.75, 1.0)
    phase_shift = jax.random.uniform(key_shift, (SLICES, GRID, GRID), jnp.float32, -1.2, 1.2)
    return jnp.stack((amplitude * jnp.cos(phase_shift), amplitude * jnp.sin(phase_shift)), axis=1)


def draw_probe_pos(key, part):
    subkeys = jax.random.split(key, 4)
    block_count = PROBES // PROBES_DEV
    numbers = jnp.arange(PROBES, dtype=jnp.int32)
    owner_block = numbers // PROBES_DEV
    within = numbers % PROBES_DEV
    grid_rows = owner_block * ROWS_DEV + jax.random.randint(subkeys[0], (PROBES,), 0, ROWS_DEV, dtype=jnp.int32)
    grid_cols = jax.random.randint(subkeys[1], (PROBES,), 0, GRID, dtype=jnp.int32)
    first_slot = jax.random.randint(subkeys[2], (block_count,), 0, PROBES_DEV, dtype=jnp.int32)
    second_slot = (first_slot + 1 + jax.random.randint(subkeys[3], (block_count,), 0, PROBES_DEV - 1, dtype=jnp.int32)) % PROBES_DEV
    is_first = within == first_slot[owner_block]
    is_second = within == second_slot[owner_block]
    grid_rows = jnp.where(is_first, owner_block * ROWS_DEV, grid_rows)
    grid_rows = jnp.where(is_second, owner_block * ROWS_DEV + ROWS_DEV - 1, grid_rows)
    grid_cols = jnp.where(is_first, 0, grid_cols)
    grid_cols = jnp.where(is_second, GRID - 1, grid_cols)
    return jnp.stack((grid_rows, grid_cols), axis=1)


def plant(values, own_key, smallest, high):
    place = [jax.random.randint(jax.random.fold_in(own_key, axis), (), 0, length) for axis, length in enumerate(values.shape)]
    longest = values.shape.index(max(values.shape))
    neighbour = place[:longest] + [(place[longest] + 1) % values.shape[longest]] + place[longest + 1:]
    return values.at[tuple(place)].set(smallest).at[tuple(neighbour)].set(high)


def shard_levels(key, dims, cuts, low, high):
    factor_of = 1.0
    for dim, parts in cuts:
        steps = jax.random.uniform(jax.random.fold_in(jax.random.fold_in(key, 6), dim), (parts,), jnp.float32, low / len(cuts), high / len(cuts))
        factor_of = factor_of * jnp.repeat(jnp.exp(steps), dims[dim] // parts).reshape((-1,) + (1,) * (len(dims) - 1 - dim))
    return factor_of


def gaussian(rng, shape, spread, bound, cuts=(), held_as=jnp.bfloat16):
    values = jax.random.normal(rng, shape, jnp.float32) * spread
    if len(cuts) > 0:
        values = shard_levels(rng, shape, cuts, -0.22, 0.18) * values
    return jnp.clip(values, min=-bound, max=bound).astype(held_as)


def setup_inputs(seed: int = 0) -> dict:
    streams_of = jax.random.split(jax.random.key(seed), 7)
    return {
        "plane_waves": gaussian(streams_of[0], (2, WAVES, GRID, GRID), 1.0, 6.0, ((1, 4), (2, 8)), jnp.float32),
        "transmission": draw_transmission(jax.random.fold_in(streams_of[6], 71), 0),
        "wave_index": plant(jax.random.randint(streams_of[2], (WAVES, 2), -(WINDOW // 4), WINDOW // 4), jax.random.fold_in(streams_of[2], 1), -(WINDOW // 4), (WINDOW // 4) - 1).astype(jnp.int32),
        "wave_weight": jnp.clip(jnp.exp(math.log(3.0) - 2.3025851 * jax.random.uniform(streams_of[3], (WAVES,), jnp.float32) ** shard_levels(streams_of[3], (WAVES,), ((0, 4),), -0.2, 0.2)), 0.3, 3.0),
        "wave_phase": jnp.clip(jax.random.uniform(streams_of[4], (WAVES,), jnp.float32, -3.140625, 3.140625), -3.140625, 3.140625),
        "probe_pos": draw_probe_pos(jax.random.fold_in(streams_of[6], 71), 0),
    }


FRESNEL = 0.1
EXACT_PRECISION = lax.Precision.HIGHEST


def propagator_parts():
    indices = jnp.arange(GRID, dtype=jnp.int32)
    frequency = jnp.where(indices < GRID // 2, indices, indices - GRID)
    radius = frequency[:, None] * frequency[:, None] + frequency[None, :] * frequency[None, :]
    phase_angle = radius.astype(jnp.float32) * (math.pi * FRESNEL / GRID)
    inside = 9 * radius <= GRID * GRID
    return jnp.where(inside, jnp.cos(phase_angle), 0.0), jnp.where(inside, -jnp.sin(phase_angle), 0.0)


def coefficients(positions, wave_index, wave_weight, wave_phase):
    grid_rows = positions[:, 0:1]
    grid_cols = positions[:, 1:2]
    turns = (FACTOR * (grid_rows * wave_index[None, :, 0] + grid_cols * wave_index[None, :, 1])) % GRID
    angles = wave_phase[None, :] - turns.astype(jnp.float32) * (2.0 * math.pi / GRID)
    return wave_weight[None, :] * jnp.cos(angles), wave_weight[None, :] * jnp.sin(angles)


def reference(plane_waves, transmission, wave_index, wave_weight, wave_phase, probe_pos):
    prop_re, prop_im = propagator_parts()
    propagator = lax.complex(prop_re, prop_im)
    layers = lax.complex(transmission[:, 0], transmission[:, 1])

    def advance(halves):
        field = lax.complex(halves[0], halves[1])
        for slice_index in range(SLICES):
            field = field * layers[slice_index]
            field = jnp.fft.ifft2(propagator * jnp.fft.fft2(field))
        return jnp.real(field), jnp.imag(field)

    exit_re, exit_im = lax.map(advance, (plane_waves[0], plane_waves[1]))
    padded = jnp.pad(jnp.stack((exit_re, exit_im)), ((0, 0), (0, 0), (HALF, HALF), (HALF, HALF)), mode="wrap")
    coef_re, coef_im = coefficients(probe_pos, wave_index, wave_weight, wave_phase)

    def probe_image(item):
        row_start, col_start, weight_re, weight_im = item
        zero_index = jnp.zeros((), jnp.int32)
        window_cut = lax.dynamic_slice(padded, (zero_index, zero_index, row_start.astype(jnp.int32), col_start.astype(jnp.int32)), (2, WAVES, WINDOW, WINDOW))
        real_part = jnp.einsum("w,wij->ij", weight_re, window_cut[0], precision=EXACT_PRECISION) - jnp.einsum("w,wij->ij", weight_im, window_cut[1], precision=EXACT_PRECISION)
        imag_part = jnp.einsum("w,wij->ij", weight_re, window_cut[1], precision=EXACT_PRECISION) + jnp.einsum("w,wij->ij", weight_im, window_cut[0], precision=EXACT_PRECISION)
        spectrum = jnp.fft.fft2(lax.complex(real_part, imag_part))
        spec_re = jnp.real(spectrum)
        spec_im = jnp.imag(spectrum)
        return (spec_re * spec_re + spec_im * spec_im) / (WINDOW * WINDOW * WAVES)

    return lax.map(probe_image, (probe_pos[:, 0], probe_pos[:, 1], coef_re, coef_im))
```

```python
import functools
import math

import jax
import jax.numpy as jnp
import numpy as np
from jax import lax
from jax.experimental import pallas as pl
from jax.experimental.pallas import tpu as pltpu
from jax.sharding import PartitionSpec as P

GRID = 2048
FACTOR = 16
WINDOW = 128
HALF = 64
FRESNEL = 0.1

BAND = math.isqrt(GRID * GRID // 9)
FOLD = GRID // 2
KX_PAD = 384
KY_PAD = 344
ROWS_EXT = GRID + WINDOW
COLS_EXT = FOLD + WINDOW
AHEAD = 8


def angles_of(first, second):
    return (2.0 * math.pi / GRID) * (np.outer(first, second) % GRID)


def cos_sin(first, freq):
    step = 64
    unit = 2.0 * math.pi / GRID
    coarse = jnp.arange(0, first, step, dtype=jnp.int32)
    fine = jnp.arange(step, dtype=jnp.int32)
    a = (coarse[:, None] * freq[None, :] % GRID).astype(jnp.float32)[:, None] * unit
    b = (fine[:, None] * freq[None, :] % GRID).astype(jnp.float32)[None] * unit
    shape = (first, freq.shape[0])
    cos_t = jnp.cos(a) * jnp.cos(b) - jnp.sin(a) * jnp.sin(b)
    sin_t = jnp.sin(a) * jnp.cos(b) + jnp.cos(a) * jnp.sin(b)
    return cos_t.reshape(shape), sin_t.reshape(shape)


def column_table(parity):
    freq = 2 * jnp.arange(KX_PAD, dtype=jnp.int32) + parity
    return jnp.concatenate(cos_sin(COLS_EXT, freq), axis=1)


def row_tables():
    tables = []
    for parity in (0, 1):
        freq = 2 * jnp.arange(KY_PAD, dtype=jnp.int32) + parity
        tables.append(jnp.concatenate(cos_sin(FOLD, freq), axis=1))
    return tables


def dot(left, right):
    return jnp.dot(left, right, precision=lax.Precision.HIGH)


def propagator_block(parity):
    ky = np.concatenate([2 * np.arange(KY_PAD) + q for q in (0, 0, 1, 1)])
    ky = jnp.asarray(ky.astype(np.int32))[:, None]
    kx = (2 * jnp.arange(KX_PAD, dtype=jnp.int32) + parity)[None, :]
    scale = math.pi * FRESNEL / GRID
    angle_y = (ky * ky).astype(jnp.float32) * scale
    angle_x = (kx * kx).astype(jnp.float32) * scale
    cos_y, sin_y = jnp.cos(angle_y), jnp.sin(angle_y)
    cos_x, sin_x = jnp.cos(angle_x), jnp.sin(angle_x)
    inside = 9 * (ky * ky + kx * kx) <= GRID * GRID
    weight = jnp.where(ky == 0, 1.0, 2.0) * jnp.where(kx == 0, 1.0, 2.0) / (GRID * GRID)
    weight = jnp.where(inside, weight, 0.0)
    real_part = weight * (cos_y * cos_x - sin_y * sin_x)
    imag_part = -weight * (sin_y * cos_x + cos_y * sin_x)
    return jnp.concatenate([real_part] * 2, 1), jnp.concatenate([imag_part] * 2, 1)


def coefficients(positions, wave_index, wave_weight, wave_phase):
    turns = (
        FACTOR * (positions[:, 0] * wave_index[0, 0] + positions[:, 1] * wave_index[0, 1])
    ) % GRID
    angles = wave_phase[0] - turns.astype(jnp.float32) * (2.0 * math.pi / GRID)
    return wave_weight[0] * jnp.cos(angles), wave_weight[0] * jnp.sin(angles)


def window_kernel(row_ref, col_ref, re_ref, im_ref, field_ref, out_ref, held, sems):
    slot = pl.program_id(0)
    count = pl.num_programs(0)

    def fetch(index, buffer, side):
        row = pl.multiple_of(row_ref[index] // 8 * 8, 8)
        col = pl.multiple_of((col_ref[index] // WINDOW + side) * WINDOW, WINDOW)
        return pltpu.make_async_copy(
            field_ref.at[:, pl.ds(row, WINDOW + 8), pl.ds(col, WINDOW)],
            held.at[buffer, side],
            sems.at[buffer, side],
        )

    @pl.when(slot == 0)
    def _():
        for ahead in range(AHEAD):
            fetch(ahead, ahead, 0).start()
            fetch(ahead, ahead, 1).start()

    fetch(slot, slot % AHEAD, 0).wait()
    fetch(slot, slot % AHEAD, 1).wait()
    row_shift = row_ref[slot] % 8
    col_shift = col_ref[slot] % WINDOW

    lane = lax.broadcasted_iota(jnp.int32, (WINDOW, WINDOW), 1)

    def cut(part):
        back = lax.rem(WINDOW - col_shift, WINDOW)
        sides = [
            pltpu.roll(held[slot % AHEAD, side, part, pl.ds(row_shift, WINDOW)], back, 1)
            for side in (0, 1)
        ]
        return jnp.where(lane < WINDOW - col_shift, sides[0], sides[1])

    real_part, imag_part = cut(0), cut(1)
    weight_re, weight_im = re_ref[slot], im_ref[slot]
    out_ref[0, 0] = weight_re * real_part - weight_im * imag_part
    out_ref[0, 1] = weight_re * imag_part + weight_im * real_part

    @pl.when(slot + AHEAD < count)
    def _():
        fetch(slot + AHEAD, slot % AHEAD, 0).start()
        fetch(slot + AHEAD, slot % AHEAD, 1).start()


def cut_windows(field, rows, cols, weight_re, weight_im):
    count = rows.shape[0]
    return pl.pallas_call(
        window_kernel,
        out_shape=jax.ShapeDtypeStruct((count, 2, WINDOW, WINDOW), jnp.float32),
        grid_spec=pltpu.PrefetchScalarGridSpec(
            num_scalar_prefetch=4,
            grid=(count,),
            in_specs=[pl.BlockSpec(memory_space=pl.ANY)],
            out_specs=pl.BlockSpec((1, 2, WINDOW, WINDOW), lambda i, *_: (i, 0, 0, 0)),
            scratch_shapes=[
                pltpu.VMEM((AHEAD, 2, 2, WINDOW + 8, WINDOW), jnp.float32),
                pltpu.SemaphoreType.DMA((AHEAD, 2)),
            ],
        ),
        name="cut_windows",
    )(rows, cols, weight_re, weight_im, field)


def flip(block, axis, bit):
    count = lax.axis_size(axis)
    return lax.ppermute(block, axis, [(i, i ^ bit) for i in range(count)])


def shards(plane_waves, transmission, wave_index, wave_weight, wave_phase, probe_pos):
    rows_here = plane_waves.shape[2]
    row_count = lax.axis_size("row")
    wave_count = lax.axis_size("wave")
    row_rank = lax.axis_index("row")
    wave_rank = lax.axis_index("wave")
    parity = row_rank % 2
    sign = 1.0 - 2.0 * parity.astype(jnp.float32)

    wave_re, wave_im = plane_waves[0, 0], plane_waves[1, 0]
    trans_re, trans_im = transmission[0, 0], transmission[0, 1]
    field = jnp.concatenate(
        [wave_re * trans_re - wave_im * trans_im, wave_re * trans_im + wave_im * trans_re]
    )
    low, high = field[:, :FOLD], field[:, FOLD:]
    mine = low + sign * high
    theirs = flip(low - sign * high, "row", 1)

    table_x, inverse_y = lax.optimization_barrier((column_table(parity), row_tables()))
    forward_x = table_x[:FOLD]
    forward_y = jnp.concatenate([table[: 2 * rows_here] for table in inverse_y], axis=1)

    def inverse_x(block):
        return lax.dot_general(
            block, table_x, (((1,), (1,)), ((), ())), precision=lax.Precision.HIGH
        )

    def side_by_side(block):
        return jnp.concatenate([block[:rows_here], block[rows_here:]], axis=1)

    mine = side_by_side(dot(mine, forward_x))
    theirs = side_by_side(dot(theirs, forward_x))
    spectrum = jnp.where(
        parity == 0, jnp.concatenate([mine, theirs]), jnp.concatenate([theirs, mine])
    )
    spectrum = lax.dot_general(
        forward_y, spectrum, (((0,), (0,)), ((), ())), precision=lax.Precision.HIGH
    )
    prop_re, prop_im = propagator_block(parity)
    half = 2 * KX_PAD
    spec_re, spec_im = spectrum[:, :half], spectrum[:, half:]
    spectrum = jnp.concatenate(
        [prop_re * spec_re - prop_im * spec_im, prop_re * spec_im + prop_im * spec_re], axis=1
    )
    even = dot(inverse_y[0], spectrum[: 2 * KY_PAD])
    odd = dot(inverse_y[1], spectrum[2 * KY_PAD :])
    top = even + odd
    rows = jnp.concatenate([top, even - odd, top[:WINDOW]])
    field = jnp.stack([inverse_x(rows[:, :half]), inverse_x(rows[:, half:])])

    own = probe_pos.shape[0] // (row_count * wave_count)
    slots = jnp.arange(row_count * wave_count * own, dtype=jnp.int32)
    slot_row = (slots // (wave_count * own)) ^ row_rank
    slot_wave = (slots // own % wave_count) ^ wave_rank
    positions = probe_pos[(slot_row * wave_count + slot_wave) * own + slots % own]
    chip_row = (row_rank // 2) * (2 * rows_here)
    row_starts = (positions[:, 0] - HALF - chip_row) % GRID
    col_starts = (positions[:, 1] - HALF) % GRID
    weight_re, weight_im = coefficients(positions, wave_index, wave_weight, wave_phase)
    wrapped = jnp.where(col_starts >= FOLD, sign, 1.0)
    parts = cut_windows(
        field, row_starts, col_starts % FOLD, weight_re * wrapped, weight_im * wrapped
    )

    wave_bits = wave_count.bit_length() - 1
    parts = parts.reshape((row_count // 2, 2) + (2,) * wave_bits + (own, 2, WINDOW, WINDOW))
    parts = parts[:, 0] + flip(parts[:, 1], "row", 1)
    groups = []
    middle = row_count // 4
    for group, order in (
        (parts[:middle], range(wave_bits)),
        (parts[middle:], range(wave_bits - 1, -1, -1)),
    ):
        left = list(range(wave_bits))
        for place in order:
            dim = 1 + left.index(place)
            left.remove(place)
            keep = lax.index_in_dim(group, 0, dim, False)
            send = lax.index_in_dim(group, 1, dim, False)
            group = keep + flip(send, "wave", wave_count >> (1 + place))
        groups.append(group)
    parts = jnp.concatenate(groups)
    bit = 2
    while bit < row_count:
        parts = parts.reshape((-1, 2) + parts.shape[1:])
        parts = parts[:, 0] + flip(parts[:, 1], "row", bit)
        bit *= 2
    window = parts[0]

    angle = angles_of(np.arange(WINDOW), FACTOR * np.arange(WINDOW))
    cos_t = jnp.asarray(np.cos(angle).astype(np.float32))
    sin_t = jnp.asarray(np.sin(angle).astype(np.float32))

    def one_dft(formula, halves):
        def term(table, value):
            return jnp.einsum(formula, table, value, precision=lax.Precision.HIGHEST)

        return (
            term(cos_t, halves[0]) + term(sin_t, halves[1]),
            term(cos_t, halves[1]) - term(sin_t, halves[0]),
        )

    halves = one_dft("ki,pij->pkj", (window[:, 0], window[:, 1]))
    halves = one_dft("kj,pij->pik", halves)
    total_waves = plane_waves.shape[1] * wave_count
    power = (halves[0] * halves[0] + halves[1] * halves[1]) / (WINDOW * WINDOW * total_waves)
    return lax.all_to_all(power, "wave", split_axis=1, concat_axis=0, tiled=True)


def solution(mesh):
    return jax.shard_map(
        shards,
        mesh=mesh,
        in_specs=(
            P(None, "wave", "row", None),
            P(None, None, "row", None),
            P("wave", None),
            P("wave"),
            P("wave"),
            P(),
        ),
        out_specs=P("row", "wave", None),
        check_vma=False,
    )
```

```python
import functools
import math

import jax
import jax.numpy as jnp
import numpy as np
from jax import lax
from jax.experimental import pallas as pl
from jax.experimental.pallas import tpu as pltpu
from jax.sharding import PartitionSpec as P

GRID = 2048
FACTOR = 16
WINDOW = 128
HALF = 64
FRESNEL = 0.1

BAND = math.isqrt(GRID * GRID // 9)
FOLD = GRID // 2
KX_PAD = 384
KY_PAD = 384
KX_TILES = 4 * KX_PAD // 256
COL_TILES = FOLD // 256


def angles_of(first, second):
    return (2.0 * math.pi / GRID) * (np.outer(first, second) % GRID)


def cos_sin(first, start, stride, second):
    step = 64
    unit = 2.0 * math.pi / GRID
    coarse = start + stride * jnp.arange(0, first, step, dtype=jnp.int32)
    fine = stride * jnp.arange(step, dtype=jnp.int32)
    a = (coarse[:, None] * second[None, :] % GRID).astype(jnp.float32)[:, None] * unit
    b = (fine[:, None] * second[None, :] % GRID).astype(jnp.float32)[None] * unit
    shape = (first, second.shape[0])
    cos_t = jnp.cos(a) * jnp.cos(b) - jnp.sin(a) * jnp.sin(b)
    sin_t = jnp.sin(a) * jnp.cos(b) + jnp.cos(a) * jnp.sin(b)
    return cos_t.reshape(shape), sin_t.reshape(shape)


def column_table(parity):
    freq = 2 * jnp.arange(KX_PAD, dtype=jnp.int32) + parity
    return jnp.concatenate(cos_sin(FOLD, 0, 1, freq), axis=1)


def column_table_inverse(parity):
    cols = jnp.arange(FOLD, dtype=jnp.int32)
    return jnp.concatenate(cos_sin(KX_PAD, parity, 2, cols), axis=0)


def row_table(start, count):
    tables = []
    for parity in (0, 1):
        freq = 2 * jnp.arange(KY_PAD, dtype=jnp.int32) + parity
        tables += cos_sin(count, start, 1, freq)
    return jnp.concatenate(tables, axis=1)


def table_halves(table):
    high = lax.reduce_precision(table, 8, 7)
    return high.astype(jnp.bfloat16), (table - high).astype(jnp.bfloat16)


def dot(left, right):
    return jnp.dot(left, right, precision=lax.Precision.HIGH)


def propagator_block(parity):
    ky = np.concatenate([2 * np.arange(KY_PAD) + q for q in (0, 0, 1, 1)])
    ky = jnp.asarray(ky.astype(np.int32))[:, None]
    kx = (2 * jnp.arange(KX_PAD, dtype=jnp.int32) + parity)[None, :]
    scale = math.pi * FRESNEL / GRID
    angle_y = (ky * ky).astype(jnp.float32) * scale
    angle_x = (kx * kx).astype(jnp.float32) * scale
    cos_y, sin_y = jnp.cos(angle_y), jnp.sin(angle_y)
    cos_x, sin_x = jnp.cos(angle_x), jnp.sin(angle_x)
    inside = 9 * (ky * ky + kx * kx) <= GRID * GRID
    weight = jnp.where(ky == 0, 1.0, 2.0) * jnp.where(kx == 0, 1.0, 2.0) / (GRID * GRID)
    weight = jnp.where(inside, weight, 0.0)
    real_part = weight * (cos_y * cos_x - sin_y * sin_x)
    imag_part = -weight * (sin_y * cos_x + cos_y * sin_x)
    return jnp.concatenate([real_part] * 2, 1), jnp.concatenate([imag_part] * 2, 1)


def coefficients(positions, wave_index, wave_weight, wave_phase):
    turns = (
        FACTOR * (positions[:, 0] * wave_index[0, 0] + positions[:, 1] * wave_index[0, 1])
    ) % GRID
    angles = wave_phase[0] - turns.astype(jnp.float32) * (2.0 * math.pi / GRID)
    return wave_weight[0] * jnp.cos(angles), wave_weight[0] * jnp.sin(angles)


def halves_of(value):
    high = value.astype(jnp.bfloat16)
    return high, (value - high.astype(jnp.float32)).astype(jnp.bfloat16)


def dot3(left, right):
    def term(first, second):
        return jnp.dot(first, second, preferred_element_type=jnp.float32)

    return term(left[0], right[0]) + term(left[0], right[1]) + term(left[1], right[0])


def row_kernel(spec_ref, table_hi, table_lo, out_hi, out_lo):
    spec = halves_of(spec_ref[...])
    half = 2 * KY_PAD
    sums = []
    for part in (0, 1):
        rows = slice(part * half, (part + 1) * half)
        sums.append(
            dot3((table_hi[:, rows], table_lo[:, rows]), (spec[0][rows], spec[1][rows]))
        )
    count = table_hi.shape[0]
    for part, value in enumerate((sums[0] + sums[1], sums[0] - sums[1])):
        high, low = halves_of(value)
        out_hi[0, part * count : (part + 1) * count] = high
        out_lo[0, part * count : (part + 1) * count] = low


def inverse_rows(spectrum, table):
    count = table[0].shape[0]
    depth = 4 * KY_PAD
    whole = pl.BlockSpec((count, depth), lambda j: (0, 0), pipeline_mode=pl.Buffered(1))
    out = jax.ShapeDtypeStruct((2, 2 * count, 2 * KX_PAD), jnp.bfloat16)
    tile = pl.BlockSpec((1, 2 * count, 256), lambda j: (j // 3, 0, j % 3))
    return pl.pallas_call(
        row_kernel,
        out_shape=(out, out),
        grid=(KX_TILES,),
        in_specs=[pl.BlockSpec((depth, 256), lambda j: (0, j)), whole, whole],
        out_specs=(tile, tile),
        cost_estimate=pl.CostEstimate(
            flops=6 * count * depth * 4 * KX_PAD,
            bytes_accessed=4 * depth * (4 * KX_PAD + count) + 8 * count * 4 * KX_PAD,
            transcendentals=0,
        ),
        name="inverse_rows",
    )(spectrum, *table)


def column_kernel(
    row_ref, col_ref, re_ref, im_ref, sign_ref, rows_hi, rows_lo, table_hi, table_lo,
    keep_ref, send_ref, field,
):
    step = pl.program_id(0)

    @pl.when(step < 2 * COL_TILES)
    def _():
        part = step // COL_TILES
        tile = step % COL_TILES
        value = dot3((rows_hi[0], rows_lo[0]), (table_hi[...], table_lo[...]))
        field[part, 2 * tile] = value[:, :WINDOW]
        field[part, 2 * tile + 1] = value[:, WINDOW:]

        @pl.when(tile == 0)
        def _():
            field[part, 2 * COL_TILES] = value[:, :WINDOW] * sign_ref[0]

    @pl.when(step == 2 * COL_TILES)
    def _():
        lane = lax.broadcasted_iota(jnp.int32, (WINDOW, WINDOW), 1)

        def one(index, out_ref, place):
            row, col = row_ref[index], col_ref[index]
            shift = col % WINDOW
            back = lax.rem(WINDOW - shift, WINDOW)

            def cut(part):
                sides = [
                    pltpu.roll(field[part, col // WINDOW + side, pl.ds(row, WINDOW)], back, 1)
                    for side in (0, 1)
                ]
                return jnp.where(lane < WINDOW - shift, sides[0], sides[1])

            real_part, imag_part = cut(0), cut(1)
            weight_re, weight_im = re_ref[index], im_ref[index]
            out_ref[place, 0] = weight_re * real_part - weight_im * imag_part
            out_ref[place, 1] = weight_re * imag_part + weight_im * real_part

        count = keep_ref.shape[0]

        @pl.loop(0, count)
        def _(place):
            one(place, keep_ref, place)
            one(count + place, send_ref, place)


def inverse_columns(rows, table, sign, row_starts, col_starts, weight_re, weight_im):
    count = row_starts.shape[0] // 2
    height = rows[0].shape[1]
    depth = 2 * KX_PAD
    last = 2 * COL_TILES - 1
    rows_spec = pl.BlockSpec(
        (1, height, depth), lambda i, *_: (jnp.minimum(i, last) // COL_TILES, 0, 0)
    )
    table_spec = pl.BlockSpec(
        (depth, 256), lambda i, *_: (0, jnp.minimum(i, last) % COL_TILES)
    )
    out = jax.ShapeDtypeStruct((count, 2, WINDOW, WINDOW), jnp.float32)
    out_spec = pl.BlockSpec(
        (count, 2, WINDOW, WINDOW), lambda i, *_: (0, 0, 0, 0), pipeline_mode=pl.Buffered(1)
    )
    return pl.pallas_call(
        column_kernel,
        out_shape=(out, out),
        grid_spec=pltpu.PrefetchScalarGridSpec(
            num_scalar_prefetch=5,
            grid=(2 * COL_TILES + 1,),
            in_specs=[rows_spec, rows_spec, table_spec, table_spec],
            out_specs=(out_spec, out_spec),
            scratch_shapes=[
                pltpu.VMEM((2, 2 * COL_TILES + 1, height, WINDOW), jnp.float32)
            ],
        ),
        cost_estimate=pl.CostEstimate(
            flops=12 * height * depth * FOLD,
            bytes_accessed=8 * height * depth + 16 * count * WINDOW * WINDOW,
            transcendentals=0,
        ),
        name="inverse_columns",
    )(row_starts, col_starts, weight_re, weight_im, sign[None], *rows, *table)


def flip(block, axis, bit):
    count = lax.axis_size(axis)
    return lax.ppermute(block, axis, [(i, i ^ bit) for i in range(count)])


def shards(plane_waves, transmission, wave_index, wave_weight, wave_phase, probe_pos):
    rows_here = plane_waves.shape[2]
    row_count = lax.axis_size("row")
    wave_count = lax.axis_size("wave")
    row_rank = lax.axis_index("row")
    wave_rank = lax.axis_index("wave")
    parity = row_rank % 2
    sign = 1.0 - 2.0 * parity.astype(jnp.float32)

    wave_re, wave_im = plane_waves[0, 0], plane_waves[1, 0]
    trans_re, trans_im = transmission[0, 0], transmission[0, 1]
    field = jnp.concatenate(
        [wave_re * trans_re - wave_im * trans_im, wave_re * trans_im + wave_im * trans_re]
    )
    low, high = field[:, :FOLD], field[:, FOLD:]
    mine = low + sign * high
    theirs = flip(low - sign * high, "row", 1)

    chip_rows = 2 * rows_here
    chips = row_count // 2
    groups = []
    for odd in (0, 1):
        pieces = [
            row_table(chip_rows * away - HALF, chip_rows + WINDOW)
            for away in range(odd, chips // 2, 2)
        ]
        groups.append(table_halves(jnp.concatenate(pieces)))
    forward_x, forward_y, inverse_x, groups = lax.optimization_barrier(
        (
            column_table(parity),
            row_table(0, chip_rows),
            table_halves(column_table_inverse(parity)),
            groups,
        )
    )

    def side_by_side(block):
        return jnp.concatenate([block[:rows_here], block[rows_here:]], axis=1)

    mine = side_by_side(dot(mine, forward_x))
    theirs = side_by_side(dot(theirs, forward_x))
    spectrum = jnp.where(
        parity == 0, jnp.concatenate([mine, theirs]), jnp.concatenate([theirs, mine])
    )
    spectrum = lax.dot_general(
        forward_y, spectrum, (((0,), (0,)), ((), ())), precision=lax.Precision.HIGH
    )
    prop_re, prop_im = propagator_block(parity)
    half = 2 * KX_PAD
    spec_re, spec_im = spectrum[:, :half], spectrum[:, half:]
    spectrum = jnp.concatenate(
        [prop_re * spec_re - prop_im * spec_im, prop_re * spec_im + prop_im * spec_re], axis=1
    )

    own = probe_pos.shape[0] // (row_count * wave_count)
    far = chips // 2
    slots = jnp.arange(2 * far * 2 * wave_count * own, dtype=jnp.int32)
    slot_probe = slots % own
    slot_wave = slots // own % wave_count ^ wave_rank
    slot_far = slots // (own * wave_count) % far
    slot_core = slots // (own * wave_count * far) % 2
    slot_odd = slots // (own * wave_count * far * 2)
    slot_row = ((slot_far * 2 + slot_odd) * 2 + slot_core) ^ row_rank
    positions = probe_pos[(slot_row * wave_count + slot_wave) * own + slot_probe]
    away = (slot_row // 2 - row_rank // 2) % chips
    segments = far // 2
    segment = away // far * segments + away % far // 2
    row_starts = segment * (chip_rows + WINDOW) + positions[:, 0] % chip_rows
    col_starts = (positions[:, 1] - HALF) % GRID
    weight_re, weight_im = coefficients(positions, wave_index, wave_weight, wave_phase)
    wrapped = jnp.where(col_starts >= FOLD, sign, 1.0)
    lists = (row_starts, col_starts % FOLD, weight_re * wrapped, weight_im * wrapped)

    wave_bits = wave_count.bit_length() - 1

    def partial_sums(odd):
        rows = inverse_rows(spectrum, groups[odd])
        picked = [member.reshape(2, -1)[odd] for member in lists]
        keep, send = inverse_columns(rows, inverse_x, sign, *picked)
        return keep, flip(send, "row", 1)

    def over_waves(keep, arrived):
        shape = (far,) + (2,) * wave_bits + (own, 2, WINDOW, WINDOW)
        parts = keep.reshape(shape) + arrived.reshape(shape)
        sums = []
        for part, order in (
            (parts[: far // 2], range(wave_bits)),
            (parts[far // 2 :], range(wave_bits - 1, -1, -1)),
        ):
            left = list(range(wave_bits))
            for place in order:
                dim = 1 + left.index(place)
                left.remove(place)
                stay = lax.index_in_dim(part, 0, dim, False)
                send = lax.index_in_dim(part, 1, dim, False)
                part = stay + flip(send, "wave", wave_count >> (1 + place))
            sums.append(part)
        return sums

    odd_sums = over_waves(*partial_sums(1))
    even_sums = over_waves(*partial_sums(0))
    parts = [
        even + flip(odd, "row", 2) for even, odd in zip(even_sums, odd_sums)
    ]
    bit = row_count // 2
    parts = parts[0] + flip(parts[1], "row", bit)
    while bit > 4:
        bit //= 2
        parts = parts.reshape((2, -1) + parts.shape[1:])
        parts = parts[0] + flip(parts[1], "row", bit)
    window = parts[0]

    angle = angles_of(np.arange(WINDOW), FACTOR * np.arange(WINDOW))
    cos_t = jnp.asarray(np.cos(angle).astype(np.float32))
    sin_t = jnp.asarray(np.sin(angle).astype(np.float32))

    def one_dft(formula, halves):
        def term(table, value):
            return jnp.einsum(formula, table, value, precision=lax.Precision.HIGHEST)

        return (
            term(cos_t, halves[0]) + term(sin_t, halves[1]),
            term(cos_t, halves[1]) - term(sin_t, halves[0]),
        )

    halves = one_dft("ki,pij->pkj", (window[:, 0], window[:, 1]))
    halves = one_dft("kj,pij->pik", halves)
    total_waves = plane_waves.shape[1] * wave_count
    power = (halves[0] * halves[0] + halves[1] * halves[1]) / (WINDOW * WINDOW * total_waves)
    return lax.all_to_all(power, "wave", split_axis=1, concat_axis=0, tiled=True)


def solution(mesh):
    return jax.shard_map(
        shards,
        mesh=mesh,
        in_specs=(
            P(None, "wave", "row", None),
            P(None, None, "row", None),
            P("wave", None),
            P("wave"),
            P("wave"),
            P(),
        ),
        out_specs=P("row", "wave", None),
        check_vma=False,
    )
```

```python
import functools
import math

import jax
import jax.numpy as jnp
import numpy as np
from jax import lax
from jax.experimental import pallas as pl
from jax.experimental.pallas import tpu as pltpu
from jax.sharding import PartitionSpec as P

GRID = 2048
FACTOR = 16
WINDOW = 128
HALF = 64
FRESNEL = 0.1

BAND = math.isqrt(GRID * GRID // 9)
FOLD = GRID // 2
BLOCKS = 3
LANES = 128
PAIR = 2 * LANES
DEPTH = BLOCKS * PAIR
FREQS = BLOCKS * LANES
FINE = 64
COL_TILES = FOLD // PAIR


def angles_of(first, second):
    return (2.0 * math.pi / GRID) * (np.outer(first, second) % GRID)


def cos_sin(first, second):
    angle = angles_of(first, second)
    return np.stack([np.cos(angle), np.sin(angle)]).astype(np.float32)


def freqs(parity):
    return 2 * np.arange(FREQS) + parity


def both(function):
    return np.stack([function(freqs(0)), function(freqs(1))])


def halves_of(value):
    high = value.astype(jnp.bfloat16)
    return high, (value - high.astype(jnp.float32)).astype(jnp.bfloat16)


def dot3(left, right):
    def term(first, second):
        return jnp.dot(first, second, preferred_element_type=jnp.float32)

    return term(left[0], right[0]) + term(left[0], right[1]) + term(left[1], right[0])


def turn(first, second):
    return (
        first[0] * second[0] - first[1] * second[1],
        first[1] * second[0] + first[0] * second[1],
    )


def put(refs, place, value):
    high, low = halves_of(value)
    refs[0][place] = high
    refs[1][place] = low


def split_kernel(sign_ref, wave_ref, trans_ref, mine_ref, theirs_ref):
    wave_re, wave_im = wave_ref[0, 0], wave_ref[1, 0]
    trans_re, trans_im = trans_ref[0, 0], trans_ref[0, 1]
    sign = sign_ref[0]
    for part, value in enumerate(
        (wave_re * trans_re - wave_im * trans_im, wave_re * trans_im + wave_im * trans_re)
    ):
        low, high = value[:, :FOLD], sign * value[:, FOLD:]
        mine_ref[part] = low + high
        theirs_ref[part] = low - high


def split_columns(sign, plane_waves, transmission):
    rows = plane_waves.shape[2]
    step = 32
    out = jax.ShapeDtypeStruct((2, rows, FOLD), jnp.float32)
    out_spec = pl.BlockSpec((2, step, FOLD), lambda i, *_: (0, i, 0))
    return pl.pallas_call(
        split_kernel,
        out_shape=(out, out),
        grid_spec=pltpu.PrefetchScalarGridSpec(
            num_scalar_prefetch=1,
            grid=(rows // step,),
            in_specs=[
                pl.BlockSpec((2, 1, step, GRID), lambda i, *_: (0, 0, i, 0)),
                pl.BlockSpec((1, 2, step, GRID), lambda i, *_: (0, 0, i, 0)),
            ],
            out_specs=(out_spec, out_spec),
        ),
        cost_estimate=pl.CostEstimate(
            flops=20 * rows * GRID, bytes_accessed=24 * rows * GRID, transcendentals=0
        ),
        name="split_columns",
    )(sign, plane_waves, transmission)


def column_forward_kernel(parity_ref, field_ref, fine_ref, coarse_ref, out_ref, *scratch):
    field, table = scratch[:2], scratch[2:]
    rows = field_ref.shape[1]

    @pl.when(pl.program_id(0) == 0)
    def _():
        for part in (0, 1):
            put(field, slice(part * rows, (part + 1) * rows), field_ref[part])

    fine = fine_ref[0, 0], fine_ref[0, 1]
    for step in range(FOLD // FINE):
        place = slice(step, step + 1)
        value = turn((coarse_ref[0, 0, place], coarse_ref[0, 1, place]), fine)
        rows_here = slice(step * FINE, (step + 1) * FINE)
        put(table, (rows_here, slice(0, LANES)), value[0])
        put(table, (rows_here, slice(LANES, PAIR)), value[1])
    result = dot3((field[0][...], field[1][...]), (table[0][...], table[1][...]))
    for part in (0, 1):
        out_ref[part] = result[part * rows : (part + 1) * rows]


def column_forward(parity, field):
    rows = field.shape[1]
    fine = both(lambda freq: cos_sin(np.arange(FINE), freq))
    coarse = both(lambda freq: cos_sin(np.arange(0, FOLD, FINE), freq))
    half = functools.partial(pltpu.VMEM, dtype=jnp.bfloat16)
    return pl.pallas_call(
        column_forward_kernel,
        out_shape=jax.ShapeDtypeStruct((2, rows, DEPTH), jnp.float32),
        grid_spec=pltpu.PrefetchScalarGridSpec(
            num_scalar_prefetch=1,
            grid=(BLOCKS,),
            in_specs=[
                pl.BlockSpec((2, rows, FOLD), lambda j, *_: (0, 0, 0)),
                pl.BlockSpec((1, 2, FINE, LANES), lambda j, c: (c[0], 0, 0, j)),
                pl.BlockSpec((1, 2, FOLD // FINE, LANES), lambda j, c: (c[0], 0, 0, j)),
            ],
            out_specs=pl.BlockSpec((2, rows, PAIR), lambda j, *_: (0, 0, j)),
            scratch_shapes=[half((2 * rows, FOLD))] * 2 + [half((FOLD, PAIR))] * 2,
        ),
        cost_estimate=pl.CostEstimate(
            flops=12 * rows * FOLD * DEPTH,
            bytes_accessed=8 * rows * (FOLD + DEPTH),
            transcendentals=0,
        ),
        name="column_forward",
    )(parity, field, jnp.asarray(fine), jnp.asarray(coarse))


def row_forward_kernel(
    parity_ref, mine_ref, theirs_ref, fine_ref, coarse_ref, down_ref, along_ref,
    out_hi, out_lo, table_hi, table_lo,
):
    tables = (table_hi, table_lo)

    @pl.when(pl.program_id(0) == 0)
    def _():
        for block in range(2 * BLOCKS):
            freq = slice(block * LANES, (block + 1) * LANES)
            fine = fine_ref[0, freq], fine_ref[1, freq]
            for step in range(coarse_ref.shape[3]):
                place = slice(step, step + 1)
                value = turn((coarse_ref[0, 0, freq, place], coarse_ref[0, 1, freq, place]), fine)
                cols = slice(step * LANES, (step + 1) * LANES)
                for kind in (0, 1):
                    start = block * PAIR + kind * LANES
                    put(tables, (slice(start, start + LANES), cols), value[kind])

    parts = [
        halves_of(jnp.concatenate([mine_ref[part], theirs_ref[part]])) for part in (0, 1)
    ]
    cos_x, sin_x, square_x = (along_ref[0, i : i + 1] for i in range(3))

    def blocks(parity, count):
        rows = slice(parity * DEPTH, parity * DEPTH + count * PAIR)
        table = table_hi[rows], table_lo[rows]
        real_part, imag_part = dot3(table, parts[0]), dot3(table, parts[1])
        cos_y, sin_y, square_y = (down_ref[rows, i : i + 1] for i in range(3))
        inside = 9.0 * (square_y + square_x) <= GRID * GRID
        prop_re = jnp.where(inside, cos_y * cos_x - sin_y * sin_x, 0.0)
        prop_im = jnp.where(inside, -(sin_y * cos_x + cos_y * sin_x), 0.0)
        outs = (out_hi, out_lo)
        put(outs, (0, rows), prop_re * real_part - prop_im * imag_part)
        put(outs, (1, rows), prop_re * imag_part + prop_im * real_part)

    last = pl.program_id(0) == BLOCKS - 1
    for parity in (0, 1):
        pl.when(last)(functools.partial(blocks, parity, BLOCKS - 1))
        pl.when(jnp.logical_not(last))(functools.partial(blocks, parity, BLOCKS))


def axis_factors(freq):
    angle = freq.astype(np.float64) ** 2 * (math.pi * FRESNEL / GRID)
    weight = np.where(freq == 0, 1.0, 2.0) / GRID
    return [np.cos(angle) * weight, np.sin(angle) * weight, freq.astype(np.float64) ** 2]


def paired(values):
    blocks = values.reshape(values.shape[:-1] + (-1, 1, LANES))
    return np.concatenate([blocks, blocks], -2).reshape(values.shape[:-1] + (-1,))


def row_forward(parity, mine, theirs):
    rows = mine.shape[1]
    all_freqs = np.concatenate([freqs(0), freqs(1)])
    fine = cos_sin(all_freqs, np.arange(LANES))
    starts = np.arange(0, rows, LANES)
    coarse = np.stack(
        [
            cos_sin(all_freqs, np.concatenate([starts + rows * core, starts + rows * (1 - core)]))
            for core in (0, 1)
        ]
    )
    down = paired(np.stack(axis_factors(all_freqs))).T
    along = np.stack([paired(np.stack(axis_factors(freqs(core)))) for core in (0, 1)])
    down, along = down.astype(np.float32), along.astype(np.float32)
    tile = pl.BlockSpec((2, rows, PAIR), lambda j, *_: (0, 0, j))
    out = jax.ShapeDtypeStruct((2, 2 * DEPTH, DEPTH), jnp.bfloat16)
    out_spec = pl.BlockSpec((2, 2 * DEPTH, PAIR), lambda j, *_: (0, 0, j))
    return pl.pallas_call(
        row_forward_kernel,
        out_shape=(out, out),
        grid_spec=pltpu.PrefetchScalarGridSpec(
            num_scalar_prefetch=1,
            grid=(BLOCKS,),
            in_specs=[
                tile,
                tile,
                pl.BlockSpec(fine.shape, lambda j, *_: (0, 0, 0)),
                pl.BlockSpec((1,) + coarse.shape[1:], lambda j, c: (c[0], 0, 0, 0)),
                pl.BlockSpec(down.shape, lambda j, *_: (0, 0)),
                pl.BlockSpec((1, 3, PAIR), lambda j, c: (c[0], 0, j)),
            ],
            out_specs=(out_spec, out_spec),
            scratch_shapes=[pltpu.VMEM((2 * DEPTH, 2 * rows), jnp.bfloat16)] * 2,
        ),
        cost_estimate=pl.CostEstimate(
            flops=48 * rows * DEPTH * DEPTH,
            bytes_accessed=16 * rows * DEPTH + 16 * DEPTH * DEPTH,
            transcendentals=0,
        ),
        name="row_forward",
    )(
        parity, mine, theirs, jnp.asarray(fine), jnp.asarray(coarse), jnp.asarray(down),
        jnp.asarray(along),
    )


def row_inverse_kernel(steps, spec_hi, spec_lo, fine_ref, coarse_ref, out_hi, out_lo, *tables):
    count = len(steps) * FINE

    @pl.when(pl.program_id(0) == 0)
    def _():
        for block in range(2 * BLOCKS):
            freq = slice(block * LANES, (block + 1) * LANES)
            fine = fine_ref[0, :, freq], fine_ref[1, :, freq]
            for index, step in enumerate(steps):
                place = slice(step, step + 1)
                value = turn((coarse_ref[0, place, freq], coarse_ref[1, place, freq]), fine)
                rows = slice(index * FINE, (index + 1) * FINE)
                for kind in (0, 1):
                    start = block * PAIR + kind * LANES
                    put(tables, (rows, slice(start, start + LANES)), value[kind])

    def blocks(depth):
        sums = []
        for parity in (0, 1):
            part = slice(parity * DEPTH, parity * DEPTH + depth * PAIR)
            sums.append(
                dot3((tables[0][:, part], tables[1][:, part]), (spec_hi[0, part], spec_lo[0, part]))
            )
        outs = (out_hi, out_lo)
        put(outs, (0, slice(0, count)), sums[0] + sums[1])
        put(outs, (0, slice(count, 2 * count)), sums[0] - sums[1])

    last = pl.program_id(0) % BLOCKS == BLOCKS - 1
    pl.when(last)(functools.partial(blocks, BLOCKS - 1))
    pl.when(jnp.logical_not(last))(functools.partial(blocks, BLOCKS))


def row_inverse(spectrum, steps):
    count = len(steps) * FINE
    all_freqs = np.concatenate([freqs(0), freqs(1)])
    fine = cos_sin(np.arange(FINE), all_freqs)
    coarse = cos_sin(np.arange(-HALF, FOLD + HALF, FINE), all_freqs)
    out = jax.ShapeDtypeStruct((2, 2 * count, DEPTH), jnp.bfloat16)
    tile = pl.BlockSpec((1, 2 * count, PAIR), lambda j: (j // BLOCKS, 0, j % BLOCKS))
    spec = pl.BlockSpec((1, 2 * DEPTH, PAIR), lambda j: (j // BLOCKS, 0, j % BLOCKS))
    return pl.pallas_call(
        functools.partial(row_inverse_kernel, steps),
        out_shape=(out, out),
        grid=(2 * BLOCKS,),
        in_specs=[
            spec,
            spec,
            pl.BlockSpec(fine.shape, lambda j: (0, 0, 0)),
            pl.BlockSpec(coarse.shape, lambda j: (0, 0, 0)),
        ],
        out_specs=(tile, tile),
        scratch_shapes=[pltpu.VMEM((count, 2 * DEPTH), jnp.bfloat16)] * 2,
        cost_estimate=pl.CostEstimate(
            flops=24 * count * DEPTH * DEPTH,
            bytes_accessed=16 * DEPTH * DEPTH + 16 * count * DEPTH,
            transcendentals=0,
        ),
        name="row_inverse",
    )(*spectrum, jnp.asarray(fine), jnp.asarray(coarse))


def column_inverse_kernel(
    layout, info_ref, slot_ref, pos_ref, re_ref, im_ref, sign_ref,
    rows_hi, rows_lo, fine_ref, coarse_ref, keep_ref, send_ref, field, table_hi, table_lo,
):
    chip_rows, chips, waves, own = layout
    step = pl.program_id(0)
    tile = step % COL_TILES
    tables = (table_hi, table_lo)

    @pl.when(step < COL_TILES)
    def _():
        for block in range(BLOCKS):
            freq = slice(block * LANES, (block + 1) * LANES)
            fine = fine_ref[0, 0, freq], fine_ref[0, 1, freq]
            for side in (0, 1):
                place = slice(side, side + 1)
                value = turn(
                    (coarse_ref[0, 0, 0, freq, place], coarse_ref[0, 0, 1, freq, place]), fine
                )
                cols = slice(side * LANES, (side + 1) * LANES)
                for kind in (0, 1):
                    start = block * PAIR + kind * LANES
                    put(tables, (tile, slice(start, start + LANES), cols), value[kind])

    @pl.when(step < 2 * COL_TILES)
    def _():
        part = step // COL_TILES
        value = dot3((rows_hi[0], rows_lo[0]), (table_hi[tile], table_lo[tile]))
        field[part, 2 * tile] = value[:, :LANES]
        field[part, 2 * tile + 1] = value[:, LANES:]

        @pl.when(tile == 0)
        def _():
            field[part, 2 * COL_TILES] = value[:, :LANES] * sign_ref[0]

    @pl.when(step == 2 * COL_TILES)
    def _():
        lane = lax.broadcasted_iota(jnp.int32, (WINDOW, WINDOW), 1)
        row_rank, wave_rank = info_ref[0], info_ref[1]
        far = chips // 2
        segments = far // 2

        def one(index, out_ref, place):
            target = row_rank ^ slot_ref[0, index]
            probe = (target * waves + (wave_rank ^ slot_ref[1, index])) * own + slot_ref[2, index]
            away = lax.rem(target // 2 - row_rank // 2 + chips, chips)
            segment = away // far * segments + lax.rem(away, far) // 2
            row = segment * (chip_rows + WINDOW) + lax.rem(pos_ref[0, probe], chip_rows)
            start = lax.rem(pos_ref[1, probe] + (GRID - HALF), GRID)
            col = lax.rem(start, FOLD)
            turned = jnp.where(start >= FOLD, sign_ref[0], 1.0)
            shift = lax.rem(col, LANES)
            back = lax.rem(LANES - shift, LANES)

            def cut(part):
                sides = [
                    pltpu.roll(field[part, col // LANES + side, pl.ds(row, WINDOW)], back, 1)
                    for side in (0, 1)
                ]
                return jnp.where(lane < LANES - shift, sides[0], sides[1])

            real_part, imag_part = cut(0), cut(1)
            weight_re, weight_im = re_ref[probe] * turned, im_ref[probe] * turned
            out_ref[place, 0] = weight_re * real_part - weight_im * imag_part
            out_ref[place, 1] = weight_re * imag_part + weight_im * real_part

        count = keep_ref.shape[0]

        @pl.loop(0, count)
        def _(place):
            one(place, keep_ref, place)
            one(count + place, send_ref, place)


def column_inverse(layout, rows, slots, info, positions, weights, sign):
    count = slots.shape[1] // 2
    height = rows[0].shape[1]
    fine = both(lambda freq: cos_sin(freq, np.arange(LANES)))
    coarse = both(
        lambda freq: np.stack(
            [cos_sin(freq, PAIR * tile + np.array([0, LANES])) for tile in range(COL_TILES)]
        )
    )
    last = 2 * COL_TILES - 1
    rows_spec = pl.BlockSpec(
        (1, height, DEPTH), lambda i, *_: (jnp.minimum(i, last) // COL_TILES, 0, 0)
    )
    out = jax.ShapeDtypeStruct((count, 2, WINDOW, WINDOW), jnp.float32)
    out_spec = pl.BlockSpec(
        (count, 2, WINDOW, WINDOW), lambda i, *_: (0, 0, 0, 0), pipeline_mode=pl.Buffered(1)
    )
    return pl.pallas_call(
        functools.partial(column_inverse_kernel, layout),
        out_shape=(out, out),
        grid_spec=pltpu.PrefetchScalarGridSpec(
            num_scalar_prefetch=6,
            grid=(2 * COL_TILES + 1,),
            in_specs=[
                rows_spec,
                rows_spec,
                pl.BlockSpec((1,) + fine.shape[1:], lambda i, info, *_: (info[2], 0, 0, 0)),
                pl.BlockSpec(
                    (1, 1) + coarse.shape[2:],
                    lambda i, info, *_: (info[2], jnp.minimum(i, COL_TILES - 1), 0, 0, 0),
                ),
            ],
            out_specs=(out_spec, out_spec),
            scratch_shapes=[
                pltpu.VMEM((2, 2 * COL_TILES + 1, height, WINDOW), jnp.float32),
                pltpu.VMEM((COL_TILES, DEPTH, PAIR), jnp.bfloat16),
                pltpu.VMEM((COL_TILES, DEPTH, PAIR), jnp.bfloat16),
            ],
        ),
        cost_estimate=pl.CostEstimate(
            flops=12 * height * DEPTH * FOLD,
            bytes_accessed=8 * height * DEPTH + 16 * count * WINDOW * WINDOW,
            transcendentals=0,
        ),
        name="column_inverse",
    )(
        info, jnp.asarray(slots), positions, *weights, sign, *rows, jnp.asarray(fine),
        jnp.asarray(coarse),
    )


def coefficients(positions, wave_index, wave_weight, wave_phase):
    turns = (FACTOR * (positions[0] * wave_index[0, 0] + positions[1] * wave_index[0, 1])) % GRID
    angles = wave_phase[0] - turns.astype(jnp.float32) * (2.0 * math.pi / GRID)
    return wave_weight[0] * jnp.cos(angles), wave_weight[0] * jnp.sin(angles)


def flip(block, axis, bit):
    count = lax.axis_size(axis)
    return lax.ppermute(block, axis, [(i, i ^ bit) for i in range(count)])


def exchange(parts, axis, bit):
    return parts[0] + flip(parts[1], axis, bit)


def shards(plane_waves, transmission, wave_index, wave_weight, wave_phase, probe_pos):
    rows_here = plane_waves.shape[2]
    row_count = lax.axis_size("row")
    wave_count = lax.axis_size("wave")
    row_rank = lax.axis_index("row")
    wave_rank = lax.axis_index("wave")
    core = row_rank % 2
    sign = (1.0 - 2.0 * core.astype(jnp.float32))[None]
    parity = core[None]
    info = jnp.stack([row_rank, wave_rank, core])
    chip_rows = 2 * rows_here
    chips = row_count // 2
    far = chips // 2
    own = probe_pos.shape[0] // (row_count * wave_count)

    mine, theirs = split_columns(sign, plane_waves, transmission)
    theirs = flip(theirs, "row", 1)
    positions = probe_pos.T
    weights = coefficients(positions, wave_index, wave_weight, wave_phase)
    mine = column_forward(parity, mine)
    mine, theirs = lax.optimization_barrier((mine, theirs))
    spectrum = row_forward(parity, mine, column_forward(parity, theirs))

    wave_bits = wave_count.bit_length() - 1
    orders = (list(range(wave_bits - 1, -1, -1)), list(range(wave_bits)))
    order_of = [orders[0 if index < far // 2 else 1] for index in range(far)]
    layout = (chip_rows, chips, wave_count, own)

    def slots_of(odd):
        slots = []
        for core_bit in (0, 1):
            for index in range(far):
                for digits in range(wave_count):
                    wave = 0
                    for place, bit in enumerate(order_of[index]):
                        wave |= (digits >> (wave_bits - 1 - place) & 1) << bit
                    for probe in range(own):
                        slots.append(((index * 2 + odd) * 2 + core_bit, wave, probe))
        return np.array(slots, np.int32).T

    def steps_of(odd):
        steps = []
        for away in range(odd, far, 2):
            first = chip_rows * away // FINE
            steps += range(first, first + (chip_rows + WINDOW) // FINE)
        return tuple(steps)

    def by_half(parts):
        return [
            parts[half * (far // 2) : (half + 1) * (far // 2)].reshape(
                (far // 2, wave_count, own, 2, WINDOW, WINDOW)
            )
            for half in (0, 1)
        ]

    def column_part(odd, rows):
        keep, send = column_inverse(layout, rows, slots_of(odd), info, positions, weights, sign)
        return keep, flip(send, "row", 1)

    def add_core(keep, arrived):
        shape = (far, wave_count, own, 2, WINDOW, WINDOW)
        keep, arrived = by_half(keep.reshape(shape)), by_half(arrived.reshape(shape))
        middle = wave_count // 2
        return [
            (a[:, :middle] + b[:, :middle], a[:, middle:] + b[:, middle:])
            for a, b in zip(keep, arrived)
        ]

    def over_waves(halves):
        sums = []
        for (stay, send), order in zip(halves, orders):
            for place, bit in enumerate(order):
                arrived = flip(send, "wave", 1 << bit)
                middle = stay.shape[1] // 2
                if place + 1 < wave_bits:
                    stay, send = (
                        stay[:, :middle] + arrived[:, :middle],
                        stay[:, middle:] + arrived[:, middle:],
                    )
                else:
                    stay = stay + arrived
            sums.append(stay[:, 0])
        return sums

    rows_odd = row_inverse(spectrum, steps_of(1))
    keep_odd, arrived_odd = column_part(1, rows_odd)
    spectrum, keep_odd = lax.optimization_barrier((spectrum, keep_odd))
    rows_even = row_inverse(spectrum, steps_of(0))
    halves_odd = add_core(keep_odd, arrived_odd)
    rows_even, halves_odd = lax.optimization_barrier((rows_even, halves_odd))
    sums_odd = over_waves(halves_odd)
    sums_even = over_waves(add_core(*column_part(0, rows_even)))
    parts = [even + flip(odd, "row", 2) for even, odd in zip(sums_even, sums_odd)]
    bit = row_count // 2
    parts = exchange(parts, "row", bit)
    while bit > 4:
        bit //= 2
        parts = exchange(parts.reshape((2, -1) + parts.shape[1:]), "row", bit)
    window = parts[0]

    angle = angles_of(np.arange(WINDOW), FACTOR * np.arange(WINDOW))
    cos_t = jnp.asarray(np.cos(angle).astype(np.float32))
    sin_t = jnp.asarray(np.sin(angle).astype(np.float32))

    def one_dft(formula, halves):
        def term(table, value):
            return jnp.einsum(formula, table, value, precision=lax.Precision.HIGHEST)

        return (
            term(cos_t, halves[0]) + term(sin_t, halves[1]),
            term(cos_t, halves[1]) - term(sin_t, halves[0]),
        )

    halves = one_dft("ki,pij->pkj", (window[:, 0], window[:, 1]))
    halves = one_dft("kj,pij->pik", halves)
    total_waves = plane_waves.shape[1] * wave_count
    power = (halves[0] * halves[0] + halves[1] * halves[1]) / (WINDOW * WINDOW * total_waves)
    return lax.all_to_all(power, "wave", split_axis=1, concat_axis=0, tiled=True)


def solution(mesh):
    return jax.shard_map(
        shards,
        mesh=mesh,
        in_specs=(
            P(None, "wave", "row", None),
            P(None, None, "row", None),
            P("wave", None),
            P("wave"),
            P("wave"),
            P(),
        ),
        out_specs=P("row", "wave", None),
        check_vma=False,
    )
```

```python
import functools
import math

import jax
import jax.numpy as jnp
import numpy as np
from jax import lax
from jax.experimental import pallas as pl
from jax.experimental.pallas import tpu as pltpu
from jax.sharding import PartitionSpec as P

GRID = 2048
FACTOR = 16
WINDOW = 128
HALF = 64
FRESNEL = 0.1

BAND = math.isqrt(GRID * GRID // 9)
FOLD = GRID // 2
BLOCKS = 3
LANES = 128
PAIR = 2 * LANES
DEPTH = BLOCKS * PAIR
FREQS = BLOCKS * LANES
FINE = 64
COL_TILES = FOLD // PAIR


def angles_of(first, second):
    return (2.0 * math.pi / GRID) * (np.outer(first, second) % GRID)


def cos_sin(first, second):
    angle = angles_of(first, second)
    return np.stack([np.cos(angle), np.sin(angle)]).astype(np.float32)


def freqs(parity):
    return 2 * np.arange(FREQS) + parity


def both(function):
    return np.stack([function(freqs(0)), function(freqs(1))])


def halves_of(value):
    high = value.astype(jnp.bfloat16)
    return high, (value - high.astype(jnp.float32)).astype(jnp.bfloat16)


def dot3(left, right):
    def term(first, second):
        return jnp.dot(first, second, preferred_element_type=jnp.float32)

    return term(left[0], right[0]) + term(left[0], right[1]) + term(left[1], right[0])


def turn(first, second):
    return (
        first[0] * second[0] - first[1] * second[1],
        first[1] * second[0] + first[0] * second[1],
    )


def put(refs, place, value):
    high, low = halves_of(value)
    refs[0][place] = high
    refs[1][place] = low


def split_kernel(sign_ref, wave_ref, trans_ref, mine_ref, theirs_ref):
    wave_re, wave_im = wave_ref[0, 0], wave_ref[1, 0]
    trans_re, trans_im = trans_ref[0, 0], trans_ref[0, 1]
    sign = sign_ref[0]
    for part, value in enumerate(
        (wave_re * trans_re - wave_im * trans_im, wave_re * trans_im + wave_im * trans_re)
    ):
        low, high = value[:, :FOLD], sign * value[:, FOLD:]
        mine_ref[part] = low + high
        theirs_ref[part] = low - high


def split_columns(sign, plane_waves, transmission):
    rows = plane_waves.shape[2]
    step = 32
    out = jax.ShapeDtypeStruct((2, rows, FOLD), jnp.float32)
    out_spec = pl.BlockSpec((2, step, FOLD), lambda i, *_: (0, i, 0))
    return pl.pallas_call(
        split_kernel,
        out_shape=(out, out),
        grid_spec=pltpu.PrefetchScalarGridSpec(
            num_scalar_prefetch=1,
            grid=(rows // step,),
            in_specs=[
                pl.BlockSpec((2, 1, step, GRID), lambda i, *_: (0, 0, i, 0)),
                pl.BlockSpec((1, 2, step, GRID), lambda i, *_: (0, 0, i, 0)),
            ],
            out_specs=(out_spec, out_spec),
        ),
        cost_estimate=pl.CostEstimate(
            flops=20 * rows * GRID, bytes_accessed=24 * rows * GRID, transcendentals=0
        ),
        name="split_columns",
    )(sign, plane_waves, transmission)


def column_forward_kernel(parity_ref, field_ref, fine_ref, coarse_ref, out_ref, *scratch):
    field, table = scratch[:2], scratch[2:]
    rows = field_ref.shape[1]

    @pl.when(pl.program_id(0) == 0)
    def _():
        for part in (0, 1):
            put(field, slice(part * rows, (part + 1) * rows), field_ref[part])

    fine = fine_ref[0, 0], fine_ref[0, 1]
    for step in range(FOLD // FINE):
        place = slice(step, step + 1)
        value = turn((coarse_ref[0, 0, place], coarse_ref[0, 1, place]), fine)
        rows_here = slice(step * FINE, (step + 1) * FINE)
        put(table, (rows_here, slice(0, LANES)), value[0])
        put(table, (rows_here, slice(LANES, PAIR)), value[1])
    result = dot3((field[0][...], field[1][...]), (table[0][...], table[1][...]))
    for part in (0, 1):
        out_ref[part] = result[part * rows : (part + 1) * rows]


def column_forward(parity, field):
    rows = field.shape[1]
    fine = both(lambda freq: cos_sin(np.arange(FINE), freq))
    coarse = both(lambda freq: cos_sin(np.arange(0, FOLD, FINE), freq))
    half = functools.partial(pltpu.VMEM, dtype=jnp.bfloat16)
    return pl.pallas_call(
        column_forward_kernel,
        out_shape=jax.ShapeDtypeStruct((2, rows, DEPTH), jnp.float32),
        grid_spec=pltpu.PrefetchScalarGridSpec(
            num_scalar_prefetch=1,
            grid=(BLOCKS,),
            in_specs=[
                pl.BlockSpec((2, rows, FOLD), lambda j, *_: (0, 0, 0)),
                pl.BlockSpec((1, 2, FINE, LANES), lambda j, c: (c[0], 0, 0, j)),
                pl.BlockSpec((1, 2, FOLD // FINE, LANES), lambda j, c: (c[0], 0, 0, j)),
            ],
            out_specs=pl.BlockSpec((2, rows, PAIR), lambda j, *_: (0, 0, j)),
            scratch_shapes=[half((2 * rows, FOLD))] * 2 + [half((FOLD, PAIR))] * 2,
        ),
        cost_estimate=pl.CostEstimate(
            flops=12 * rows * FOLD * DEPTH,
            bytes_accessed=8 * rows * (FOLD + DEPTH),
            transcendentals=0,
        ),
        name="column_forward",
    )(parity, field, jnp.asarray(fine), jnp.asarray(coarse))


def row_forward_kernel(
    parity_ref, mine_ref, theirs_ref, fine_ref, coarse_ref, down_ref, along_ref,
    out_hi, out_lo, table_hi, table_lo,
):
    tables = (table_hi, table_lo)

    @pl.when(pl.program_id(0) == 0)
    def _():
        for block in range(2 * BLOCKS):
            freq = slice(block * LANES, (block + 1) * LANES)
            fine = fine_ref[0, freq], fine_ref[1, freq]
            for step in range(coarse_ref.shape[3]):
                place = slice(step, step + 1)
                value = turn((coarse_ref[0, 0, freq, place], coarse_ref[0, 1, freq, place]), fine)
                cols = slice(step * LANES, (step + 1) * LANES)
                for kind in (0, 1):
                    start = block * PAIR + kind * LANES
                    put(tables, (slice(start, start + LANES), cols), value[kind])

    parts = [
        halves_of(jnp.concatenate([mine_ref[part], theirs_ref[part]])) for part in (0, 1)
    ]
    cos_x, sin_x, square_x = (along_ref[0, i : i + 1] for i in range(3))

    def blocks(parity, count):
        rows = slice(parity * DEPTH, parity * DEPTH + count * PAIR)
        table = table_hi[rows], table_lo[rows]
        real_part, imag_part = dot3(table, parts[0]), dot3(table, parts[1])
        cos_y, sin_y, square_y = (down_ref[rows, i : i + 1] for i in range(3))
        inside = 9.0 * (square_y + square_x) <= GRID * GRID
        prop_re = jnp.where(inside, cos_y * cos_x - sin_y * sin_x, 0.0)
        prop_im = jnp.where(inside, -(sin_y * cos_x + cos_y * sin_x), 0.0)
        outs = (out_hi, out_lo)
        put(outs, (0, rows), prop_re * real_part - prop_im * imag_part)
        put(outs, (1, rows), prop_re * imag_part + prop_im * real_part)

    last = pl.program_id(0) == BLOCKS - 1
    for parity in (0, 1):
        pl.when(last)(functools.partial(blocks, parity, BLOCKS - 1))
        pl.when(jnp.logical_not(last))(functools.partial(blocks, parity, BLOCKS))


def axis_factors(freq):
    angle = freq.astype(np.float64) ** 2 * (math.pi * FRESNEL / GRID)
    weight = np.where(freq == 0, 1.0, 2.0) / GRID
    return [np.cos(angle) * weight, np.sin(angle) * weight, freq.astype(np.float64) ** 2]


def paired(values):
    blocks = values.reshape(values.shape[:-1] + (-1, 1, LANES))
    return np.concatenate([blocks, blocks], -2).reshape(values.shape[:-1] + (-1,))


def row_forward(parity, mine, theirs):
    rows = mine.shape[1]
    all_freqs = np.concatenate([freqs(0), freqs(1)])
    fine = cos_sin(all_freqs, np.arange(LANES))
    starts = np.arange(0, rows, LANES)
    coarse = np.stack(
        [
            cos_sin(all_freqs, np.concatenate([starts + rows * core, starts + rows * (1 - core)]))
            for core in (0, 1)
        ]
    )
    down = paired(np.stack(axis_factors(all_freqs))).T
    along = np.stack([paired(np.stack(axis_factors(freqs(core)))) for core in (0, 1)])
    down, along = down.astype(np.float32), along.astype(np.float32)
    tile = pl.BlockSpec((2, rows, PAIR), lambda j, *_: (0, 0, j))
    out = jax.ShapeDtypeStruct((2, 2 * DEPTH, DEPTH), jnp.bfloat16)
    out_spec = pl.BlockSpec((2, 2 * DEPTH, PAIR), lambda j, *_: (0, 0, j))
    return pl.pallas_call(
        row_forward_kernel,
        out_shape=(out, out),
        grid_spec=pltpu.PrefetchScalarGridSpec(
            num_scalar_prefetch=1,
            grid=(BLOCKS,),
            in_specs=[
                tile,
                tile,
                pl.BlockSpec(fine.shape, lambda j, *_: (0, 0, 0)),
                pl.BlockSpec((1,) + coarse.shape[1:], lambda j, c: (c[0], 0, 0, 0)),
                pl.BlockSpec(down.shape, lambda j, *_: (0, 0)),
                pl.BlockSpec((1, 3, PAIR), lambda j, c: (c[0], 0, j)),
            ],
            out_specs=(out_spec, out_spec),
            scratch_shapes=[pltpu.VMEM((2 * DEPTH, 2 * rows), jnp.bfloat16)] * 2,
        ),
        cost_estimate=pl.CostEstimate(
            flops=48 * rows * DEPTH * DEPTH,
            bytes_accessed=16 * rows * DEPTH + 16 * DEPTH * DEPTH,
            transcendentals=0,
        ),
        name="row_forward",
    )(
        parity, mine, theirs, jnp.asarray(fine), jnp.asarray(coarse), jnp.asarray(down),
        jnp.asarray(along),
    )


def row_inverse_kernel(steps, spec_hi, spec_lo, fine_ref, coarse_ref, out_hi, out_lo, *tables):
    count = len(steps) * FINE

    @pl.when(pl.program_id(0) == 0)
    def _():
        for block in range(2 * BLOCKS):
            freq = slice(block * LANES, (block + 1) * LANES)
            fine = fine_ref[0, :, freq], fine_ref[1, :, freq]
            for index, step in enumerate(steps):
                place = slice(step, step + 1)
                value = turn((coarse_ref[0, place, freq], coarse_ref[1, place, freq]), fine)
                rows = slice(index * FINE, (index + 1) * FINE)
                for kind in (0, 1):
                    start = block * PAIR + kind * LANES
                    put(tables, (rows, slice(start, start + LANES)), value[kind])

    def blocks(depth):
        sums = []
        for parity in (0, 1):
            part = slice(parity * DEPTH, parity * DEPTH + depth * PAIR)
            sums.append(
                dot3((tables[0][:, part], tables[1][:, part]), (spec_hi[0, part], spec_lo[0, part]))
            )
        outs = (out_hi, out_lo)
        put(outs, (0, slice(0, count)), sums[0] + sums[1])
        put(outs, (0, slice(count, 2 * count)), sums[0] - sums[1])

    last = pl.program_id(0) % BLOCKS == BLOCKS - 1
    pl.when(last)(functools.partial(blocks, BLOCKS - 1))
    pl.when(jnp.logical_not(last))(functools.partial(blocks, BLOCKS))


def row_inverse(spectrum, steps):
    count = len(steps) * FINE
    all_freqs = np.concatenate([freqs(0), freqs(1)])
    fine = cos_sin(np.arange(FINE), all_freqs)
    coarse = cos_sin(np.arange(-HALF, FOLD + HALF, FINE), all_freqs)
    out = jax.ShapeDtypeStruct((2, 2 * count, DEPTH), jnp.bfloat16)
    tile = pl.BlockSpec((1, 2 * count, PAIR), lambda j: (j // BLOCKS, 0, j % BLOCKS))
    spec = pl.BlockSpec((1, 2 * DEPTH, PAIR), lambda j: (j // BLOCKS, 0, j % BLOCKS))
    return pl.pallas_call(
        functools.partial(row_inverse_kernel, steps),
        out_shape=(out, out),
        grid=(2 * BLOCKS,),
        in_specs=[
            spec,
            spec,
            pl.BlockSpec(fine.shape, lambda j: (0, 0, 0)),
            pl.BlockSpec(coarse.shape, lambda j: (0, 0, 0)),
        ],
        out_specs=(tile, tile),
        scratch_shapes=[pltpu.VMEM((count, 2 * DEPTH), jnp.bfloat16)] * 2,
        cost_estimate=pl.CostEstimate(
            flops=24 * count * DEPTH * DEPTH,
            bytes_accessed=16 * DEPTH * DEPTH + 16 * count * DEPTH,
            transcendentals=0,
        ),
        name="row_inverse",
    )(*spectrum, jnp.asarray(fine), jnp.asarray(coarse))


def column_inverse_kernel(
    layout, info_ref, slot_ref, pos_ref, re_ref, im_ref, sign_ref,
    rows_hi, rows_lo, fine_ref, coarse_ref, keep_ref, send_ref, field, table_hi, table_lo,
):
    chip_rows, waves, own, segments = layout
    height = chip_rows + WINDOW
    step = pl.program_id(0)
    tile = step % COL_TILES
    tables = (table_hi, table_lo)

    @pl.when(step < COL_TILES)
    def _():
        for block in range(BLOCKS):
            freq = slice(block * LANES, (block + 1) * LANES)
            fine = fine_ref[0, 0, freq], fine_ref[0, 1, freq]
            for side in (0, 1):
                place = slice(side, side + 1)
                value = turn(
                    (coarse_ref[0, 0, 0, freq, place], coarse_ref[0, 0, 1, freq, place]), fine
                )
                cols = slice(side * LANES, (side + 1) * LANES)
                for kind in (0, 1):
                    start = block * PAIR + kind * LANES
                    put(tables, (tile, slice(start, start + LANES), cols), value[kind])

    @pl.when(step < 2 * segments * COL_TILES)
    def _():
        part = step // COL_TILES % 2
        start = pl.multiple_of(step // (2 * COL_TILES) * height, LANES)
        rows = pl.ds(start, height)
        value = dot3((rows_hi[0], rows_lo[0]), (table_hi[tile], table_lo[tile]))
        field[part, 2 * tile, rows] = value[:, :LANES]
        field[part, 2 * tile + 1, rows] = value[:, LANES:]

        @pl.when(tile == 0)
        def _():
            field[part, 2 * COL_TILES, rows] = value[:, :LANES] * sign_ref[0]

    @pl.when(step == 2 * segments * COL_TILES)
    def _():
        lane = lax.broadcasted_iota(jnp.int32, (WINDOW, WINDOW), 1)
        row_rank, wave_rank = info_ref[0], info_ref[1]

        def one(index, out_ref, place):
            target = row_rank ^ slot_ref[0, index]
            probe = (target * waves + (wave_rank ^ slot_ref[1, index])) * own + slot_ref[2, index]
            row = slot_ref[3, index] * height + lax.rem(pos_ref[0, probe], chip_rows)
            start = lax.rem(pos_ref[1, probe] + (GRID - HALF), GRID)
            col = lax.rem(start, FOLD)
            turned = jnp.where(start >= FOLD, sign_ref[0], 1.0)
            shift = lax.rem(col, LANES)
            back = lax.rem(LANES - shift, LANES)

            def cut(part):
                sides = [
                    pltpu.roll(field[part, col // LANES + side, pl.ds(row, WINDOW)], back, 1)
                    for side in (0, 1)
                ]
                return jnp.where(lane < LANES - shift, sides[0], sides[1])

            real_part, imag_part = cut(0), cut(1)
            weight_re, weight_im = re_ref[probe] * turned, im_ref[probe] * turned
            out_ref[place, 0] = weight_re * real_part - weight_im * imag_part
            out_ref[place, 1] = weight_re * imag_part + weight_im * real_part

        count = keep_ref.shape[0]

        @pl.loop(0, count)
        def _(place):
            one(count + place, send_ref, place)
            one(place, keep_ref, place)


def column_inverse(layout, rows, slots, info, positions, weights, sign):
    chip_rows, _, _, segments = layout
    count = slots.shape[1] // 2
    height = chip_rows + WINDOW
    fine = both(lambda freq: cos_sin(freq, np.arange(LANES)))
    coarse = both(
        lambda freq: np.stack(
            [cos_sin(freq, PAIR * tile + np.array([0, LANES])) for tile in range(COL_TILES)]
        )
    )
    last = 2 * segments * COL_TILES - 1

    def rows_map(i, info, *_):
        i = jnp.minimum(i, last)
        return i // COL_TILES % 2, info[3 + i // (2 * COL_TILES)], 0

    rows_spec = pl.BlockSpec((1, height, DEPTH), rows_map)
    out = jax.ShapeDtypeStruct((count, 2, WINDOW, WINDOW), jnp.float32)
    out_spec = pl.BlockSpec(
        (count, 2, WINDOW, WINDOW), lambda i, *_: (0, 0, 0, 0), pipeline_mode=pl.Buffered(1)
    )
    return pl.pallas_call(
        functools.partial(column_inverse_kernel, layout),
        out_shape=(out, out),
        grid_spec=pltpu.PrefetchScalarGridSpec(
            num_scalar_prefetch=6,
            grid=(last + 2,),
            in_specs=[
                rows_spec,
                rows_spec,
                pl.BlockSpec((1,) + fine.shape[1:], lambda i, info, *_: (info[2], 0, 0, 0)),
                pl.BlockSpec(
                    (1, 1) + coarse.shape[2:],
                    lambda i, info, *_: (info[2], jnp.minimum(i, COL_TILES - 1), 0, 0, 0),
                ),
            ],
            out_specs=(out_spec, out_spec),
            scratch_shapes=[
                pltpu.VMEM((2, 2 * COL_TILES + 1, segments * height, WINDOW), jnp.float32),
                pltpu.VMEM((COL_TILES, DEPTH, PAIR), jnp.bfloat16),
                pltpu.VMEM((COL_TILES, DEPTH, PAIR), jnp.bfloat16),
            ],
        ),
        cost_estimate=pl.CostEstimate(
            flops=12 * segments * height * DEPTH * FOLD,
            bytes_accessed=8 * segments * height * DEPTH + 16 * count * WINDOW * WINDOW,
            transcendentals=0,
        ),
        name="column_inverse",
    )(
        info, jnp.asarray(slots), positions, *weights, sign, *rows, jnp.asarray(fine),
        jnp.asarray(coarse),
    )


def sum_kernel(count, *refs):
    total = refs[0][...]
    for ref in refs[1:count]:
        total += ref[...]
    if len(refs) == count + 1:
        refs[count][...] = total
    else:
        refs[count][...] = total[0]
        refs[count + 1][...] = total[1]


def sum_of(terms, halve):
    count, tail = terms[0].shape[0], terms[0].shape[1:]
    zeros = (0,) * len(tail)
    if halve:
        count //= 2
        terms = [term.reshape((2, count) + tail) for term in terms]
        step = max(1, count // 2)
        in_spec = pl.BlockSpec((2, step) + tail, lambda i: (0, i) + zeros)
    else:
        step = max(1, count // 2)
        in_spec = pl.BlockSpec((step,) + tail, lambda i: (i,) + zeros)
    out = jax.ShapeDtypeStruct((count,) + tail, jnp.float32)
    out_spec = pl.BlockSpec((step,) + tail, lambda i: (i,) + zeros)
    size = count * 4 * math.prod(tail) * (2 if halve else 1)
    result = pl.pallas_call(
        functools.partial(sum_kernel, len(terms)),
        out_shape=(out, out) if halve else out,
        grid=(count // step,),
        in_specs=[in_spec] * len(terms),
        out_specs=(out_spec, out_spec) if halve else out_spec,
        cost_estimate=pl.CostEstimate(
            flops=size, bytes_accessed=(len(terms) + 1) * size, transcendentals=0
        ),
        name="sum_of",
    )(*terms)
    return result


def power_kernel(count, scale, *refs):
    terms, (down_ref, along_ref, out_ref) = refs[:count], refs[count:]
    down, along = halves_of(down_ref[...]), halves_of(along_ref[...])
    for probe in range(out_ref.shape[0]):
        total = terms[0][probe]
        for term in terms[1:]:
            total += term[probe]
        value = dot3(down, halves_of(jnp.concatenate([total[0], total[1]], axis=1)))
        cos_part, sin_part = value[:WINDOW], value[WINDOW:]
        real_part = cos_part[:, :WINDOW] + sin_part[:, WINDOW:]
        imag_part = cos_part[:, WINDOW:] - sin_part[:, :WINDOW]
        value = dot3(halves_of(jnp.concatenate([real_part, imag_part])), along)
        real_part = value[:WINDOW, :WINDOW] + value[WINDOW:, WINDOW:]
        imag_part = value[WINDOW:, :WINDOW] - value[:WINDOW, WINDOW:]
        out_ref[probe] = (real_part * real_part + imag_part * imag_part) * scale


def power_of(terms, scale):
    count = terms[0].shape[0]
    table = cos_sin(np.arange(WINDOW), FACTOR * np.arange(WINDOW))
    return pl.pallas_call(
        functools.partial(power_kernel, len(terms), scale),
        out_shape=jax.ShapeDtypeStruct((count, WINDOW, WINDOW), jnp.float32),
        name="power_of",
    )(
        *terms, jnp.asarray(np.concatenate(list(table))),
        jnp.asarray(np.concatenate(list(table), axis=1)),
    )


def coefficients(positions, wave_index, wave_weight, wave_phase):
    turns = (FACTOR * (positions[0] * wave_index[0, 0] + positions[1] * wave_index[0, 1])) % GRID
    angles = wave_phase[0] - turns.astype(jnp.float32) * (2.0 * math.pi / GRID)
    return wave_weight[0] * jnp.cos(angles), wave_weight[0] * jnp.sin(angles)


def flip(block, axis, bit):
    count = lax.axis_size(axis)
    return lax.ppermute(block, axis, [(i, i ^ bit) for i in range(count)])


def shards(plane_waves, transmission, wave_index, wave_weight, wave_phase, probe_pos):
    rows_here = plane_waves.shape[2]
    row_count = lax.axis_size("row")
    wave_count = lax.axis_size("wave")
    row_rank = lax.axis_index("row")
    wave_rank = lax.axis_index("wave")
    core = row_rank % 2
    sign = (1.0 - 2.0 * core.astype(jnp.float32))[None]
    parity = core[None]
    chip_rows = 2 * rows_here
    chips = row_count // 2
    far = chips // 2
    own = probe_pos.shape[0] // (row_count * wave_count)

    mine, theirs = split_columns(sign, plane_waves, transmission)
    theirs = flip(theirs, "row", 1)
    positions = probe_pos.T
    weights = coefficients(positions, wave_index, wave_weight, wave_phase)
    mine = column_forward(parity, mine)
    mine, theirs = lax.optimization_barrier((mine, theirs))
    spectrum = row_forward(parity, mine, column_forward(parity, theirs))

    wave_bits = wave_count.bit_length() - 1
    orders = (list(range(wave_bits - 1, -1, -1)), list(range(wave_bits)))
    segments = far // 2
    layout = (chip_rows, wave_count, own, segments)

    def slots_of(odd, half):
        slots = []
        for core_bit in (0, 1):
            for digits in range(wave_count):
                wave = 0
                for place, bit in enumerate(orders[half]):
                    wave |= (digits >> (wave_bits - 1 - place) & 1) << bit
                for index in range(segments):
                    row = ((half * segments + index) * 2 + odd) * 2 + core_bit
                    slots += [(row, wave, probe, index) for probe in range(own)]
        return np.array(slots, np.int32).T

    def info_of(odd, half):
        chip = row_rank // 2
        info = [row_rank, wave_rank, core]
        for index in range(segments):
            target = chip ^ ((half * segments + index) * 2 + odd)
            away = (target - chip) % chips
            info.append(away // far * segments + away % far // 2)
        return jnp.stack(info)

    def steps_of(odd):
        steps = []
        for away in range(odd, far, 2):
            first = chip_rows * away // FINE
            steps += range(first, first + (chip_rows + WINDOW) // FINE)
        return tuple(steps)

    def cut(odd, half, rows):
        keep, send = column_inverse(
            layout, rows, slots_of(odd, half), info_of(odd, half), positions, weights, sign
        )
        return keep, flip(send, "row", 1)

    def wave_stage(half, place, terms):
        stay, send = sum_of(terms, True)
        return stay, flip(send, "wave", 1 << orders[half][place])

    def later(value, *before):
        return lax.optimization_barrier((value,) + before)

    upper, lower = 1, 0
    rows_odd = row_inverse(spectrum, steps_of(1))
    odd_upper = cut(1, upper, rows_odd)
    rows_odd, keep = later(rows_odd, odd_upper[0])
    odd_upper = (keep, odd_upper[1])
    odd_lower = cut(1, lower, rows_odd)

    stages = {(1, upper): [odd_upper, 0], (1, lower): [odd_lower, 0]}

    def advance(value, *keys):
        for key in keys:
            terms, place = stages[key]
            if place == wave_bits:
                continue
            stay, send = sum_of(terms, True)
            value, stay, send = later(value, stay, send)
            stages[key] = [
                (stay, flip(send, "wave", 1 << orders[key[1]][place])), place + 1
            ]
        return value

    spectrum = later(spectrum, odd_lower[0])
    spectrum, keep = spectrum
    stages[1, lower] = [(keep, odd_lower[1]), 0]
    spectrum = advance(spectrum, (1, upper))
    rows_even = row_inverse(spectrum, steps_of(0))
    rows_even = advance(rows_even, (1, upper), (1, lower))
    even_upper = cut(0, upper, rows_even)
    rows_even, keep = later(rows_even, even_upper[0])
    stages[0, upper] = [(keep, even_upper[1]), 0]
    rows_even = advance(rows_even, (1, lower))
    near_upper = None
    if stages[1, upper][1] == wave_bits:
        total = sum_of(stages[1, upper][0], False)
        rows_even, total = later(rows_even, total)
        near_upper = flip(total, "row", 2)
    stages[0, lower] = [cut(0, lower, rows_even), 0]

    def finish(key):
        while stages[key][1] < wave_bits:
            terms, place = stages[key]
            stages[key] = [wave_stage(key[1], place, terms), place + 1]
        return list(stages[key][0])

    if near_upper is None:
        near_upper = flip(sum_of(finish((1, upper)), False), "row", 2)
    near_lower = flip(sum_of(finish((1, lower)), False), "row", 2)
    bit = row_count // 2
    send = sum_of(finish((0, upper)) + [near_upper], False)
    terms = finish((0, lower)) + [near_lower, flip(send, "row", bit)]
    while bit > 4:
        bit //= 2
        stay, send = sum_of(terms, True)
        terms = [stay, flip(send, "row", bit)]
    total_waves = plane_waves.shape[1] * wave_count
    power = power_of(terms, 1.0 / (WINDOW * WINDOW * total_waves))
    return lax.all_to_all(power, "wave", split_axis=1, concat_axis=0, tiled=True)


def solution(mesh):
    return jax.shard_map(
        shards,
        mesh=mesh,
        in_specs=(
            P(None, "wave", "row", None),
            P(None, None, "row", None),
            P("wave", None),
            P("wave"),
            P("wave"),
            P(),
        ),
        out_specs=P("row", "wave", None),
        check_vma=False,
    )
```

```python
import functools
import math

import jax
import jax.numpy as jnp
import numpy as np
from jax import lax
from jax.experimental import pallas as pl
from jax.experimental.pallas import tpu as pltpu
from jax.sharding import PartitionSpec as P

GRID = 2048
FACTOR = 16
WINDOW = 128
HALF = 64
FRESNEL = 0.1

BAND = math.isqrt(GRID * GRID // 9)
FOLD = GRID // 2
BLOCKS = 3
LANES = 128
PAIR = 2 * LANES
DEPTH = BLOCKS * PAIR
FREQS = BLOCKS * LANES
COL_TILES = FOLD // PAIR


def angles_of(first, second):
    return (2.0 * math.pi / GRID) * (np.outer(first, second) % GRID)


def cos_sin(first, second):
    angle = angles_of(first, second)
    return np.stack([np.cos(angle), np.sin(angle)])


def freqs(parity):
    return 2 * np.arange(FREQS) + parity


def both(function):
    return np.stack([function(freqs(0)), function(freqs(1))])


def halves_of(value):
    high = value.astype(jnp.bfloat16)
    return high, (value - high.astype(jnp.float32)).astype(jnp.bfloat16)


def dot3(left, right):
    def term(first, second):
        return jnp.dot(first, second, preferred_element_type=jnp.float32)

    return term(left[0], right[0]) + term(left[0], right[1]) + term(left[1], right[0])


def paired(values):
    blocks = values.reshape(values.shape[:-1] + (-1, LANES))
    return np.moveaxis(blocks, 0, -2).reshape(values.shape[1:-1] + (-1,))


def table_halves(table):
    high = table.astype(jnp.bfloat16)
    low = (table - high.astype(np.float64)).astype(jnp.bfloat16)
    return jnp.asarray(high), jnp.asarray(low)


def put(refs, place, value):
    high, low = halves_of(value)
    refs[0][place] = high
    refs[1][place] = low


def split_kernel(sign_ref, wave_ref, trans_ref, mine_ref, theirs_ref):
    wave_re, wave_im = wave_ref[0, 0], wave_ref[1, 0]
    trans_re, trans_im = trans_ref[0, 0], trans_ref[0, 1]
    sign = sign_ref[0]
    for part, value in enumerate(
        (wave_re * trans_re - wave_im * trans_im, wave_re * trans_im + wave_im * trans_re)
    ):
        low, high = value[:, :FOLD], sign * value[:, FOLD:]
        mine_ref[part] = low + high
        theirs_ref[part] = low - high


def split_columns(sign, plane_waves, transmission):
    rows = plane_waves.shape[2]
    step = 32
    out = jax.ShapeDtypeStruct((2, rows, FOLD), jnp.float32)
    out_spec = pl.BlockSpec((2, step, FOLD), lambda i, *_: (0, i, 0))
    return pl.pallas_call(
        split_kernel,
        out_shape=(out, out),
        grid_spec=pltpu.PrefetchScalarGridSpec(
            num_scalar_prefetch=1,
            grid=(rows // step,),
            in_specs=[
                pl.BlockSpec((2, 1, step, GRID), lambda i, *_: (0, 0, i, 0)),
                pl.BlockSpec((1, 2, step, GRID), lambda i, *_: (0, 0, i, 0)),
            ],
            out_specs=(out_spec, out_spec),
        ),
        cost_estimate=pl.CostEstimate(
            flops=20 * rows * GRID, bytes_accessed=24 * rows * GRID, transcendentals=0
        ),
        name="split_columns",
    )(sign, plane_waves, transmission)


def column_forward_kernel(parity_ref, field_ref, table_hi, table_lo, out_ref, *field):
    rows = field_ref.shape[1]

    @pl.when(pl.program_id(0) == 0)
    def _():
        for part in (0, 1):
            put(field, slice(part * rows, (part + 1) * rows), field_ref[part])

    result = dot3((field[0][...], field[1][...]), (table_hi[0], table_lo[0]))
    for part in (0, 1):
        out_ref[part] = result[part * rows : (part + 1) * rows]


def column_forward(parity, field):
    rows = field.shape[1]
    table = table_halves(both(lambda freq: paired(cos_sin(np.arange(FOLD), freq))))
    table_spec = pl.BlockSpec((1, FOLD, PAIR), lambda j, c: (c[0], 0, j))
    return pl.pallas_call(
        column_forward_kernel,
        out_shape=jax.ShapeDtypeStruct((2, rows, DEPTH), jnp.float32),
        grid_spec=pltpu.PrefetchScalarGridSpec(
            num_scalar_prefetch=1,
            grid=(BLOCKS,),
            in_specs=[
                pl.BlockSpec((2, rows, FOLD), lambda j, *_: (0, 0, 0)),
                table_spec,
                table_spec,
            ],
            out_specs=pl.BlockSpec((2, rows, PAIR), lambda j, *_: (0, 0, j)),
            scratch_shapes=[pltpu.VMEM((2 * rows, FOLD), jnp.bfloat16)] * 2,
        ),
        cost_estimate=pl.CostEstimate(
            flops=12 * rows * FOLD * DEPTH,
            bytes_accessed=8 * rows * (FOLD + DEPTH),
            transcendentals=0,
        ),
        name="column_forward",
    )(parity, field, *table)


def row_forward_kernel(
    parity_ref, mine_ref, theirs_ref, table_hi, table_lo, down_ref, along_ref,
    out_hi, out_lo, field_hi, field_lo,
):
    rows = mine_ref.shape[1]
    field = (field_hi, field_lo)
    core = parity_ref[0]
    for place, ref in ((core, mine_ref), (1 - core, theirs_ref)):
        start = pl.ds(pl.multiple_of(place * rows, LANES), rows)
        for part in (0, 1):
            put(field, (start, slice(part * PAIR, (part + 1) * PAIR)), ref[part])
    cos_x, sin_x, square_x = (along_ref[0, i : i + 1] for i in range(3))
    outs = (out_hi, out_lo)

    def blocks(parity, count):
        first = parity * DEPTH
        part = slice(first, first + count * PAIR)
        result = dot3((table_hi[part], table_lo[part]), (field_hi[...], field_lo[...]))
        for block in range(count):
            freq = slice((parity * BLOCKS + block) * LANES, (parity * BLOCKS + block + 1) * LANES)
            cos_y, sin_y, square_y = (down_ref[freq, i : i + 1] for i in range(3))
            inside = 9.0 * (square_y + square_x) <= GRID * GRID
            prop_re = jnp.where(inside, cos_y * cos_x - sin_y * sin_x, 0.0)
            prop_im = jnp.where(inside, -(sin_y * cos_x + cos_y * sin_x), 0.0)
            for kind in (0, 1):
                start = block * PAIR + kind * LANES
                place = slice(first + start, first + start + LANES)
                for side in (0, 1):
                    cols = slice(side * LANES, (side + 1) * LANES)
                    real_part = result[start : start + LANES, cols]
                    imag_part = result[start : start + LANES, slice(PAIR + side * LANES, PAIR + (side + 1) * LANES)]
                    put(outs, (0, place, cols), prop_re * real_part - prop_im * imag_part)
                    put(outs, (1, place, cols), prop_re * imag_part + prop_im * real_part)

    last = pl.program_id(0) == BLOCKS - 1
    for parity in (0, 1):
        pl.when(last)(functools.partial(blocks, parity, BLOCKS - 1))
        pl.when(jnp.logical_not(last))(functools.partial(blocks, parity, BLOCKS))


def axis_factors(freq):
    angle = freq.astype(np.float64) ** 2 * (math.pi * FRESNEL / GRID)
    weight = np.where(freq == 0, 1.0, 2.0) / GRID
    return [np.cos(angle) * weight, np.sin(angle) * weight, freq.astype(np.float64) ** 2]


def row_forward(parity, mine, theirs):
    rows = mine.shape[1]
    all_freqs = np.concatenate([freqs(0), freqs(1)])
    table = table_halves(paired(cos_sin(np.arange(2 * rows), all_freqs)).T)
    down = np.stack(axis_factors(all_freqs)).T.astype(np.float32)
    along = both(lambda freq: np.stack(axis_factors(freq))).astype(np.float32)
    tile = pl.BlockSpec((2, rows, PAIR), lambda j, *_: (0, 0, j))
    out = jax.ShapeDtypeStruct((2, 2 * DEPTH, DEPTH), jnp.bfloat16)
    out_spec = pl.BlockSpec((2, 2 * DEPTH, PAIR), lambda j, *_: (0, 0, j))
    table_spec = pl.BlockSpec((2 * DEPTH, 2 * rows), lambda j, *_: (0, 0))
    return pl.pallas_call(
        row_forward_kernel,
        out_shape=(out, out),
        grid_spec=pltpu.PrefetchScalarGridSpec(
            num_scalar_prefetch=1,
            grid=(BLOCKS,),
            in_specs=[
                tile,
                tile,
                table_spec,
                table_spec,
                pl.BlockSpec(down.shape, lambda j, *_: (0, 0)),
                pl.BlockSpec((1, 3, LANES), lambda j, c: (c[0], 0, j)),
            ],
            out_specs=(out_spec, out_spec),
            scratch_shapes=[pltpu.VMEM((2 * rows, 2 * PAIR), jnp.bfloat16)] * 2,
        ),
        cost_estimate=pl.CostEstimate(
            flops=48 * rows * DEPTH * DEPTH,
            bytes_accessed=16 * rows * DEPTH + 16 * DEPTH * DEPTH,
            transcendentals=0,
        ),
        name="row_forward",
    )(parity, mine, theirs, *table, jnp.asarray(down), jnp.asarray(along))


def row_inverse_kernel(spec_hi, spec_lo, table_hi, table_lo, out_hi, out_lo):
    count = table_hi.shape[0]

    def blocks(depth):
        sums = []
        for parity in (0, 1):
            part = slice(parity * DEPTH, parity * DEPTH + depth * PAIR)
            sums.append(
                dot3((table_hi[:, part], table_lo[:, part]), (spec_hi[0, part], spec_lo[0, part]))
            )
        outs = (out_hi, out_lo)
        put(outs, (0, slice(0, count)), sums[0] + sums[1])
        put(outs, (0, slice(count, 2 * count)), sums[0] - sums[1])

    last = pl.program_id(0) % BLOCKS == BLOCKS - 1
    pl.when(last)(functools.partial(blocks, BLOCKS - 1))
    pl.when(jnp.logical_not(last))(functools.partial(blocks, BLOCKS))


def row_inverse(spectrum, rows):
    count = len(rows)
    table = table_halves(paired(cos_sin(rows, np.concatenate([freqs(0), freqs(1)]))))
    out = jax.ShapeDtypeStruct((2, 2 * count, DEPTH), jnp.bfloat16)
    tile = pl.BlockSpec((1, 2 * count, PAIR), lambda j: (j // BLOCKS, 0, j % BLOCKS))
    spec = pl.BlockSpec((1, 2 * DEPTH, PAIR), lambda j: (j // BLOCKS, 0, j % BLOCKS))
    table_spec = pl.BlockSpec((count, 2 * DEPTH), lambda j: (0, 0))
    return pl.pallas_call(
        row_inverse_kernel,
        out_shape=(out, out),
        grid=(2 * BLOCKS,),
        in_specs=[spec, spec, table_spec, table_spec],
        out_specs=(tile, tile),
        cost_estimate=pl.CostEstimate(
            flops=24 * count * DEPTH * DEPTH,
            bytes_accessed=16 * DEPTH * DEPTH + 16 * count * DEPTH,
            transcendentals=0,
        ),
        name="row_inverse",
    )(*spectrum, *table)


def column_inverse_kernel(
    layout, info_ref, slot_ref, pos_ref, re_ref, im_ref, sign_ref,
    rows_hi, rows_lo, table_hi, table_lo, keep_ref, send_ref, field,
):
    chip_rows, waves, own, segments = layout
    height = chip_rows + WINDOW
    step = pl.program_id(0)
    tile = step % COL_TILES

    @pl.when(step < 2 * segments * COL_TILES)
    def _():
        part = step // COL_TILES % 2
        start = pl.multiple_of(step // (2 * COL_TILES) * height, LANES)
        rows = pl.ds(start, height)
        value = dot3((rows_hi[0], rows_lo[0]), (table_hi[0], table_lo[0]))
        field[part, 2 * tile, rows] = value[:, :LANES]
        field[part, 2 * tile + 1, rows] = value[:, LANES:]

        @pl.when(tile == 0)
        def _():
            field[part, 2 * COL_TILES, rows] = value[:, :LANES] * sign_ref[0]

    @pl.when(step == 2 * segments * COL_TILES)
    def _():
        lane = lax.broadcasted_iota(jnp.int32, (WINDOW, WINDOW), 1)
        row_rank, wave_rank = info_ref[0], info_ref[1]

        def one(index, out_ref, place):
            target = row_rank ^ slot_ref[0, index]
            probe = (target * waves + (wave_rank ^ slot_ref[1, index])) * own + slot_ref[2, index]
            row = slot_ref[3, index] * height + lax.rem(pos_ref[0, probe], chip_rows)
            start = lax.rem(pos_ref[1, probe] + (GRID - HALF), GRID)
            col = lax.rem(start, FOLD)
            turned = jnp.where(start >= FOLD, sign_ref[0], 1.0)
            shift = lax.rem(col, LANES)
            back = lax.rem(LANES - shift, LANES)

            def cut(part):
                sides = [
                    pltpu.roll(field[part, col // LANES + side, pl.ds(row, WINDOW)], back, 1)
                    for side in (0, 1)
                ]
                return jnp.where(lane < LANES - shift, sides[0], sides[1])

            real_part, imag_part = cut(0), cut(1)
            weight_re, weight_im = re_ref[probe] * turned, im_ref[probe] * turned
            out_ref[place, 0] = weight_re * real_part - weight_im * imag_part
            out_ref[place, 1] = weight_re * imag_part + weight_im * real_part

        count = keep_ref.shape[0]

        @pl.loop(0, count)
        def _(place):
            one(count + place, send_ref, place)
            one(place, keep_ref, place)


def column_inverse(layout, rows, slots, info, positions, weights, sign):
    chip_rows, _, _, segments = layout
    count = slots.shape[1] // 2
    height = chip_rows + WINDOW
    table = table_halves(
        both(lambda freq: paired(cos_sin(np.arange(FOLD), freq)).T)
    )
    last = 2 * segments * COL_TILES - 1

    def rows_map(i, info, *_):
        i = jnp.minimum(i, last)
        return i // COL_TILES % 2, info[3 + i // (2 * COL_TILES)], 0

    rows_spec = pl.BlockSpec((1, height, DEPTH), rows_map)
    table_spec = pl.BlockSpec(
        (1, DEPTH, PAIR), lambda i, info, *_: (info[2], 0, jnp.minimum(i, last) % COL_TILES)
    )
    out = jax.ShapeDtypeStruct((count, 2, WINDOW, WINDOW), jnp.float32)
    out_spec = pl.BlockSpec(
        (count, 2, WINDOW, WINDOW), lambda i, *_: (0, 0, 0, 0), pipeline_mode=pl.Buffered(1)
    )
    return pl.pallas_call(
        functools.partial(column_inverse_kernel, layout),
        out_shape=(out, out),
        grid_spec=pltpu.PrefetchScalarGridSpec(
            num_scalar_prefetch=6,
            grid=(last + 2,),
            in_specs=[
                rows_spec,
                rows_spec,
                table_spec,
                table_spec,
            ],
            out_specs=(out_spec, out_spec),
            scratch_shapes=[
                pltpu.VMEM((2, 2 * COL_TILES + 1, segments * height, WINDOW), jnp.float32)
            ],
        ),
        cost_estimate=pl.CostEstimate(
            flops=12 * segments * height * DEPTH * FOLD,
            bytes_accessed=8 * segments * height * DEPTH + 16 * count * WINDOW * WINDOW,
            transcendentals=0,
        ),
        name="column_inverse",
    )(
        info, jnp.asarray(slots), positions, *weights, sign, *rows, *table,
    )


def sum_kernel(count, *refs):
    total = refs[0][...]
    for ref in refs[1:count]:
        total += ref[...]
    if len(refs) == count + 1:
        refs[count][...] = total
    else:
        refs[count][...] = total[0]
        refs[count + 1][...] = total[1]


def sum_of(terms, halve):
    count, tail = terms[0].shape[0], terms[0].shape[1:]
    zeros = (0,) * len(tail)
    if halve:
        count //= 2
        terms = [term.reshape((2, count) + tail) for term in terms]
        step = max(1, count // 2)
        in_spec = pl.BlockSpec((2, step) + tail, lambda i: (0, i) + zeros)
    else:
        step = max(1, count // 2)
        in_spec = pl.BlockSpec((step,) + tail, lambda i: (i,) + zeros)
    out = jax.ShapeDtypeStruct((count,) + tail, jnp.float32)
    out_spec = pl.BlockSpec((step,) + tail, lambda i: (i,) + zeros)
    size = count * 4 * math.prod(tail) * (2 if halve else 1)
    result = pl.pallas_call(
        functools.partial(sum_kernel, len(terms)),
        out_shape=(out, out) if halve else out,
        grid=(count // step,),
        in_specs=[in_spec] * len(terms),
        out_specs=(out_spec, out_spec) if halve else out_spec,
        cost_estimate=pl.CostEstimate(
            flops=size, bytes_accessed=(len(terms) + 1) * size, transcendentals=0
        ),
        name="sum_of",
    )(*terms)
    return result


def power_kernel(count, scale, *refs):
    terms, (down_ref, along_ref, out_ref) = refs[:count], refs[count:]
    down, along = halves_of(down_ref[...]), halves_of(along_ref[...])
    for probe in range(out_ref.shape[0]):
        total = terms[0][probe]
        for term in terms[1:]:
            total += term[probe]
        value = dot3(down, halves_of(jnp.concatenate([total[0], total[1]], axis=1)))
        cos_part, sin_part = value[:WINDOW], value[WINDOW:]
        real_part = cos_part[:, :WINDOW] + sin_part[:, WINDOW:]
        imag_part = cos_part[:, WINDOW:] - sin_part[:, :WINDOW]
        value = dot3(halves_of(jnp.concatenate([real_part, imag_part])), along)
        real_part = value[:WINDOW, :WINDOW] + value[WINDOW:, WINDOW:]
        imag_part = value[WINDOW:, :WINDOW] - value[:WINDOW, WINDOW:]
        out_ref[probe] = (real_part * real_part + imag_part * imag_part) * scale


def power_of(terms, scale):
    count = terms[0].shape[0]
    table = cos_sin(np.arange(WINDOW), FACTOR * np.arange(WINDOW))
    return pl.pallas_call(
        functools.partial(power_kernel, len(terms), scale),
        out_shape=jax.ShapeDtypeStruct((count, WINDOW, WINDOW), jnp.float32),
        name="power_of",
    )(
        *terms, jnp.asarray(np.concatenate(list(table)).astype(np.float32)),
        jnp.asarray(np.concatenate(list(table), axis=1).astype(np.float32)),
    )


def coefficients(positions, wave_index, wave_weight, wave_phase):
    turns = (FACTOR * (positions[0] * wave_index[0, 0] + positions[1] * wave_index[0, 1])) % GRID
    angles = wave_phase[0] - turns.astype(jnp.float32) * (2.0 * math.pi / GRID)
    return wave_weight[0] * jnp.cos(angles), wave_weight[0] * jnp.sin(angles)


def flip(block, axis, bit):
    count = lax.axis_size(axis)
    return lax.ppermute(block, axis, [(i, i ^ bit) for i in range(count)])


def shards(plane_waves, transmission, wave_index, wave_weight, wave_phase, probe_pos):
    rows_here = plane_waves.shape[2]
    row_count = lax.axis_size("row")
    wave_count = lax.axis_size("wave")
    row_rank = lax.axis_index("row")
    wave_rank = lax.axis_index("wave")
    core = row_rank % 2
    sign = (1.0 - 2.0 * core.astype(jnp.float32))[None]
    parity = core[None]
    chip_rows = 2 * rows_here
    chips = row_count // 2
    far = chips // 2
    own = probe_pos.shape[0] // (row_count * wave_count)

    mine, theirs = split_columns(sign, plane_waves, transmission)
    theirs = flip(theirs, "row", 1)
    positions = probe_pos.T
    weights = coefficients(positions, wave_index, wave_weight, wave_phase)
    mine = column_forward(parity, mine)
    mine, theirs = lax.optimization_barrier((mine, theirs))
    spectrum = row_forward(parity, mine, column_forward(parity, theirs))

    wave_bits = wave_count.bit_length() - 1
    orders = (list(range(wave_bits - 1, -1, -1)), list(range(wave_bits)))
    segments = far // 2
    layout = (chip_rows, wave_count, own, segments)

    def slots_of(odd, half):
        slots = []
        for core_bit in (0, 1):
            for digits in range(wave_count):
                wave = 0
                for place, bit in enumerate(orders[half]):
                    wave |= (digits >> (wave_bits - 1 - place) & 1) << bit
                for index in range(segments):
                    row = ((half * segments + index) * 2 + odd) * 2 + core_bit
                    slots += [(row, wave, probe, index) for probe in range(own)]
        return np.array(slots, np.int32).T

    def info_of(odd, half):
        chip = row_rank // 2
        info = [row_rank, wave_rank, core]
        for index in range(segments):
            target = chip ^ ((half * segments + index) * 2 + odd)
            away = (target - chip) % chips
            info.append(away // far * segments + away % far // 2)
        return jnp.stack(info)

    def rows_of(odd):
        return np.concatenate(
            [
                chip_rows * away - HALF + np.arange(chip_rows + WINDOW)
                for away in range(odd, far, 2)
            ]
        )

    def cut(odd, half, rows):
        keep, send = column_inverse(
            layout, rows, slots_of(odd, half), info_of(odd, half), positions, weights, sign
        )
        return keep, flip(send, "row", 1)

    def wave_stage(half, place, terms):
        stay, send = sum_of(terms, True)
        return stay, flip(send, "wave", 1 << orders[half][place])

    def later(value, *before):
        return lax.optimization_barrier((value,) + before)

    upper, lower = 1, 0
    rows_odd = row_inverse(spectrum, rows_of(1))
    odd_upper = cut(1, upper, rows_odd)
    rows_odd, keep = later(rows_odd, odd_upper[0])
    odd_upper = (keep, odd_upper[1])
    odd_lower = cut(1, lower, rows_odd)

    stages = {(1, upper): [odd_upper, 0], (1, lower): [odd_lower, 0]}

    def advance(value, *keys):
        for key in keys:
            terms, place = stages[key]
            if place == wave_bits:
                continue
            stay, send = sum_of(terms, True)
            value, stay, send = later(value, stay, send)
            stages[key] = [
                (stay, flip(send, "wave", 1 << orders[key[1]][place])), place + 1
            ]
        return value

    spectrum = later(spectrum, odd_lower[0])
    spectrum, keep = spectrum
    stages[1, lower] = [(keep, odd_lower[1]), 0]
    spectrum = advance(spectrum, (1, upper))
    rows_even = row_inverse(spectrum, rows_of(0))
    rows_even = advance(rows_even, (1, upper), (1, lower))
    even_upper = cut(0, upper, rows_even)
    rows_even, keep = later(rows_even, even_upper[0])
    stages[0, upper] = [(keep, even_upper[1]), 0]
    rows_even = advance(rows_even, (1, lower))
    near_upper = None
    if stages[1, upper][1] == wave_bits:
        total = sum_of(stages[1, upper][0], False)
        rows_even, total = later(rows_even, total)
        near_upper = flip(total, "row", 2)
    stages[0, lower] = [cut(0, lower, rows_even), 0]

    def finish(key):
        while stages[key][1] < wave_bits:
            terms, place = stages[key]
            stages[key] = [wave_stage(key[1], place, terms), place + 1]
        return list(stages[key][0])

    if near_upper is None:
        near_upper = flip(sum_of(finish((1, upper)), False), "row", 2)
    near_lower = flip(sum_of(finish((1, lower)), False), "row", 2)
    bit = row_count // 2
    send = sum_of(finish((0, upper)) + [near_upper], False)
    terms = finish((0, lower)) + [near_lower, flip(send, "row", bit)]
    while bit > 4:
        bit //= 2
        stay, send = sum_of(terms, True)
        terms = [stay, flip(send, "row", bit)]
    total_waves = plane_waves.shape[1] * wave_count
    power = power_of(terms, 1.0 / (WINDOW * WINDOW * total_waves))
    return lax.all_to_all(power, "wave", split_axis=1, concat_axis=0, tiled=True)


def solution(mesh):
    return jax.shard_map(
        shards,
        mesh=mesh,
        in_specs=(
            P(None, "wave", "row", None),
            P(None, None, "row", None),
            P("wave", None),
            P("wave"),
            P("wave"),
            P(),
        ),
        out_specs=P("row", "wave", None),
        check_vma=False,
    )
```

```python
import functools
import math

import jax
import jax.numpy as jnp
import numpy as np
from jax import lax
from jax.experimental import pallas as pl
from jax.experimental.pallas import tpu as pltpu
from jax.sharding import PartitionSpec as P

GRID = 2048
FACTOR = 16
WINDOW = 128
HALF = 64
FRESNEL = 0.1

BAND = math.isqrt(GRID * GRID // 9)
FOLD = GRID // 2
BLOCKS = 3
LANES = 128
PAIR = 2 * LANES
DEPTH = BLOCKS * PAIR
FREQS = BLOCKS * LANES
COL_TILES = FOLD // PAIR


def angles_of(first, second):
    return (2.0 * math.pi / GRID) * (np.outer(first, second) % GRID)


def cos_sin(first, second):
    angle = angles_of(first, second)
    return np.stack([np.cos(angle), np.sin(angle)])


def freqs(parity):
    return 2 * np.arange(FREQS) + parity


def both(function):
    return np.stack([function(freqs(0)), function(freqs(1))])


def halves_of(value):
    high = value.astype(jnp.bfloat16)
    return high, (value - high.astype(jnp.float32)).astype(jnp.bfloat16)


def dot3(left, right):
    def term(first, second):
        return jnp.dot(first, second, preferred_element_type=jnp.float32)

    return term(left[0], right[0]) + term(left[0], right[1]) + term(left[1], right[0])


def paired(values):
    blocks = values.reshape(values.shape[:-1] + (-1, LANES))
    return np.moveaxis(blocks, 0, -2).reshape(values.shape[1:-1] + (-1,))


def table_halves(table):
    high = table.astype(jnp.bfloat16)
    low = (table - high.astype(np.float64)).astype(jnp.bfloat16)
    return jnp.asarray(high), jnp.asarray(low)


def put(refs, place, value):
    high, low = halves_of(value)
    refs[0][place] = high
    refs[1][place] = low


def split_kernel(sign_ref, wave_ref, trans_ref, mine_ref, theirs_ref):
    wave_re, wave_im = wave_ref[0, 0], wave_ref[1, 0]
    trans_re, trans_im = trans_ref[0, 0], trans_ref[0, 1]
    sign = sign_ref[0]
    for part, value in enumerate(
        (wave_re * trans_re - wave_im * trans_im, wave_re * trans_im + wave_im * trans_re)
    ):
        low, high = value[:, :FOLD], sign * value[:, FOLD:]
        mine_ref[part] = low + high
        theirs_ref[part] = low - high


def split_columns(sign, plane_waves, transmission):
    rows = plane_waves.shape[2]
    step = 32
    out = jax.ShapeDtypeStruct((2, rows, FOLD), jnp.float32)
    out_spec = pl.BlockSpec((2, step, FOLD), lambda i, *_: (0, i, 0))
    return pl.pallas_call(
        split_kernel,
        out_shape=(out, out),
        grid_spec=pltpu.PrefetchScalarGridSpec(
            num_scalar_prefetch=1,
            grid=(rows // step,),
            in_specs=[
                pl.BlockSpec((2, 1, step, GRID), lambda i, *_: (0, 0, i, 0)),
                pl.BlockSpec((1, 2, step, GRID), lambda i, *_: (0, 0, i, 0)),
            ],
            out_specs=(out_spec, out_spec),
        ),
        cost_estimate=pl.CostEstimate(
            flops=20 * rows * GRID, bytes_accessed=24 * rows * GRID, transcendentals=0
        ),
        name="split_columns",
    )(sign, plane_waves, transmission)


def column_forward_kernel(parity_ref, field_ref, table_hi, table_lo, out_ref, *field):
    rows = field_ref.shape[1]

    @pl.when(pl.program_id(0) == 0)
    def _():
        for part in (0, 1):
            put(field, slice(part * rows, (part + 1) * rows), field_ref[part])

    result = dot3((field[0][...], field[1][...]), (table_hi[0], table_lo[0]))
    for part in (0, 1):
        out_ref[part] = result[part * rows : (part + 1) * rows]


def column_forward(parity, field):
    rows = field.shape[1]
    table = table_halves(both(lambda freq: paired(cos_sin(np.arange(FOLD), freq))))
    table_spec = pl.BlockSpec((1, FOLD, PAIR), lambda j, c: (c[0], 0, j))
    return pl.pallas_call(
        column_forward_kernel,
        out_shape=jax.ShapeDtypeStruct((2, rows, DEPTH), jnp.float32),
        grid_spec=pltpu.PrefetchScalarGridSpec(
            num_scalar_prefetch=1,
            grid=(BLOCKS,),
            in_specs=[
                pl.BlockSpec((2, rows, FOLD), lambda j, *_: (0, 0, 0)),
                table_spec,
                table_spec,
            ],
            out_specs=pl.BlockSpec((2, rows, PAIR), lambda j, *_: (0, 0, j)),
            scratch_shapes=[pltpu.VMEM((2 * rows, FOLD), jnp.bfloat16)] * 2,
        ),
        cost_estimate=pl.CostEstimate(
            flops=12 * rows * FOLD * DEPTH,
            bytes_accessed=8 * rows * (FOLD + DEPTH),
            transcendentals=0,
        ),
        name="column_forward",
    )(parity, field, *table)


def row_forward_kernel(
    parity_ref, mine_ref, theirs_ref, table_hi, table_lo, down_ref, along_ref,
    out_hi, out_lo, field_hi, field_lo,
):
    rows = mine_ref.shape[1]
    field = (field_hi, field_lo)
    core = parity_ref[0]
    for place, ref in ((core, mine_ref), (1 - core, theirs_ref)):
        start = pl.ds(pl.multiple_of(place * rows, LANES), rows)
        for part in (0, 1):
            put(field, (start, slice(part * PAIR, (part + 1) * PAIR)), ref[part])
    cos_x, sin_x, square_x = (along_ref[0, i : i + 1] for i in range(3))
    outs = (out_hi, out_lo)

    def blocks(parity, count):
        first = parity * DEPTH
        part = slice(first, first + count * PAIR)
        result = dot3((table_hi[part], table_lo[part]), (field_hi[...], field_lo[...]))
        for block in range(count):
            freq = slice((parity * BLOCKS + block) * LANES, (parity * BLOCKS + block + 1) * LANES)
            cos_y, sin_y, square_y = (down_ref[freq, i : i + 1] for i in range(3))
            inside = 9.0 * (square_y + square_x) <= GRID * GRID
            prop_re = jnp.where(inside, cos_y * cos_x - sin_y * sin_x, 0.0)
            prop_im = jnp.where(inside, -(sin_y * cos_x + cos_y * sin_x), 0.0)
            for kind in (0, 1):
                start = block * PAIR + kind * LANES
                place = slice(first + start, first + start + LANES)
                for side in (0, 1):
                    cols = slice(side * LANES, (side + 1) * LANES)
                    real_part = result[start : start + LANES, cols]
                    imag_part = result[start : start + LANES, slice(PAIR + side * LANES, PAIR + (side + 1) * LANES)]
                    put(outs, (0, place, cols), prop_re * real_part - prop_im * imag_part)
                    put(outs, (1, place, cols), prop_re * imag_part + prop_im * real_part)

    last = pl.program_id(0) == BLOCKS - 1
    for parity in (0, 1):
        pl.when(last)(functools.partial(blocks, parity, BLOCKS - 1))
        pl.when(jnp.logical_not(last))(functools.partial(blocks, parity, BLOCKS))


def axis_factors(freq):
    angle = freq.astype(np.float64) ** 2 * (math.pi * FRESNEL / GRID)
    weight = np.where(freq == 0, 1.0, 2.0) / GRID
    return [np.cos(angle) * weight, np.sin(angle) * weight, freq.astype(np.float64) ** 2]


def row_forward(parity, mine, theirs):
    rows = mine.shape[1]
    all_freqs = np.concatenate([freqs(0), freqs(1)])
    table = table_halves(paired(cos_sin(np.arange(2 * rows), all_freqs)).T)
    down = np.stack(axis_factors(all_freqs)).T.astype(np.float32)
    along = both(lambda freq: np.stack(axis_factors(freq))).astype(np.float32)
    tile = pl.BlockSpec((2, rows, PAIR), lambda j, *_: (0, 0, j))
    out = jax.ShapeDtypeStruct((2, 2 * DEPTH, DEPTH), jnp.bfloat16)
    out_spec = pl.BlockSpec((2, 2 * DEPTH, PAIR), lambda j, *_: (0, 0, j))
    table_spec = pl.BlockSpec((2 * DEPTH, 2 * rows), lambda j, *_: (0, 0))
    return pl.pallas_call(
        row_forward_kernel,
        out_shape=(out, out),
        grid_spec=pltpu.PrefetchScalarGridSpec(
            num_scalar_prefetch=1,
            grid=(BLOCKS,),
            in_specs=[
                tile,
                tile,
                table_spec,
                table_spec,
                pl.BlockSpec(down.shape, lambda j, *_: (0, 0)),
                pl.BlockSpec((1, 3, LANES), lambda j, c: (c[0], 0, j)),
            ],
            out_specs=(out_spec, out_spec),
            scratch_shapes=[pltpu.VMEM((2 * rows, 2 * PAIR), jnp.bfloat16)] * 2,
        ),
        cost_estimate=pl.CostEstimate(
            flops=48 * rows * DEPTH * DEPTH,
            bytes_accessed=16 * rows * DEPTH + 16 * DEPTH * DEPTH,
            transcendentals=0,
        ),
        name="row_forward",
    )(parity, mine, theirs, *table, jnp.asarray(down), jnp.asarray(along))


def cut_slots(layout, info_ref, slot_ref, pos_ref, re_ref, im_ref, sign_ref, field, outs):
    chip_rows, waves, own, _ = layout
    height = chip_rows + WINDOW
    lane = lax.broadcasted_iota(jnp.int32, (WINDOW, WINDOW), 1)
    row_rank, wave_rank = info_ref[0], info_ref[1]

    def one(index, out_ref, place):
        target = row_rank ^ slot_ref[0, index]
        probe = (target * waves + (wave_rank ^ slot_ref[1, index])) * own + slot_ref[2, index]
        row = slot_ref[3, index] * height + lax.rem(pos_ref[0, probe], chip_rows)
        start = lax.rem(pos_ref[1, probe] + (GRID - HALF), GRID)
        col = lax.rem(start, FOLD)
        turned = jnp.where(start >= FOLD, sign_ref[0], 1.0)
        shift = lax.rem(col, LANES)
        back = lax.rem(LANES - shift, LANES)

        def cut(part):
            sides = [
                pltpu.roll(field[part, col // LANES + side, pl.ds(row, WINDOW)], back, 1)
                for side in (0, 1)
            ]
            return jnp.where(lane < LANES - shift, sides[0], sides[1])

        real_part, imag_part = cut(0), cut(1)
        weight_re, weight_im = re_ref[probe] * turned, im_ref[probe] * turned
        out_ref[place, 0] = weight_re * real_part - weight_im * imag_part
        out_ref[place, 1] = weight_re * imag_part + weight_im * real_part

    keep_ref, send_ref = outs
    count = keep_ref.shape[0]

    @pl.loop(0, count)
    def _(place):
        one(count + place, send_ref, place)
        one(place, keep_ref, place)


def inverse_kernel(
    layout, cuts, info_ref, slot_ref, pos_ref, re_ref, im_ref, sign_ref,
    spec_hi, spec_lo, row_hi, row_lo, col_hi, col_lo, *refs,
):
    chip_rows, _, _, segments = layout
    height = chip_rows + WINDOW
    refs = list(refs)
    outs = refs[:2]
    exports = refs[2:4] if len(refs) > 5 else None
    rows, field = refs[-3:-1], refs[-1]
    step = pl.program_id(0)
    first = 2 * BLOCKS
    last = first + 2 * cuts * COL_TILES

    def row_part(depth):
        part = step // BLOCKS
        place = pl.multiple_of(step % BLOCKS * PAIR, PAIR)
        cols = pl.ds(place, PAIR)
        count = row_hi.shape[0]
        sums = []
        for parity in (0, 1):
            freq = slice(parity * DEPTH, parity * DEPTH + depth * PAIR)
            sums.append(
                dot3((row_hi[:, freq], row_lo[:, freq]), (spec_hi[0, freq], spec_lo[0, freq]))
            )
        put(rows, (part, slice(0, count), cols), sums[0] + sums[1])
        put(rows, (part, slice(count, 2 * count), cols), sums[0] - sums[1])
        if exports is not None:
            for index in range(segments):
                start = pl.multiple_of(info_ref[3 + cuts + index] * height, LANES)
                for export, source in zip(exports, rows):
                    export[0, index * height : (index + 1) * height] = source[
                        part, pl.ds(start, height), cols
                    ]

    zero_blocks = step % BLOCKS == BLOCKS - 1
    pl.when((step < first) & zero_blocks)(functools.partial(row_part, BLOCKS - 1))
    pl.when((step < first) & jnp.logical_not(zero_blocks))(functools.partial(row_part, BLOCKS))

    @pl.when((step >= first) & (step < last))
    def _():
        now = step - first
        tile = now % COL_TILES
        part = now // COL_TILES % 2
        segment = now // (2 * COL_TILES)
        source = pl.ds(pl.multiple_of(info_ref[3 + segment] * height, LANES), height)
        place = pl.ds(pl.multiple_of(segment * height, LANES), height)
        value = dot3((rows[0][part, source], rows[1][part, source]), (col_hi[0], col_lo[0]))
        field[part, 2 * tile, place] = value[:, :LANES]
        field[part, 2 * tile + 1, place] = value[:, LANES:]

        @pl.when(tile == 0)
        def _():
            field[part, 2 * COL_TILES, place] = value[:, :LANES] * sign_ref[0]

    @pl.when(step == last)
    def _():
        cut_slots(
            layout, info_ref, slot_ref, pos_ref, re_ref, im_ref, sign_ref, field, outs
        )


def column_table():
    return table_halves(both(lambda freq: paired(cos_sin(np.arange(FOLD), freq)).T))


def inverse(layout, cuts, export, spectrum, row_list, slots, info, positions, weights, sign):
    chip_rows, _, _, segments = layout
    height = chip_rows + WINDOW
    count = slots.shape[1] // 2
    tall = len(row_list)
    row_table = table_halves(paired(cos_sin(row_list, np.concatenate([freqs(0), freqs(1)]))))
    first = 2 * BLOCKS
    last = first + 2 * cuts * COL_TILES

    def spec_map(i, *_):
        i = jnp.minimum(i, first - 1)
        return i // BLOCKS, 0, i % BLOCKS

    def col_map(i, info, *_):
        return info[2], 0, (jnp.clip(i, first, last - 1) - first) % COL_TILES

    spec = pl.BlockSpec((1, 2 * DEPTH, PAIR), spec_map)
    row_spec = pl.BlockSpec(
        (tall, 2 * DEPTH), lambda i, *_: (0, 0), pipeline_mode=pl.Buffered(1)
    )
    col_spec = pl.BlockSpec((1, DEPTH, PAIR), col_map)
    shapes = [jax.ShapeDtypeStruct((count, 2, WINDOW, WINDOW), jnp.float32)] * 2
    specs = [
        pl.BlockSpec(
            (count, 2, WINDOW, WINDOW), lambda i, *_: (0, 0, 0, 0), pipeline_mode=pl.Buffered(1)
        )
    ] * 2
    if export:
        shapes += [jax.ShapeDtypeStruct((2, segments * height, DEPTH), jnp.bfloat16)] * 2
        specs += [pl.BlockSpec((1, segments * height, PAIR), spec_map)] * 2
    return pl.pallas_call(
        functools.partial(inverse_kernel, layout, cuts),
        out_shape=shapes,
        grid_spec=pltpu.PrefetchScalarGridSpec(
            num_scalar_prefetch=6,
            grid=(last + 1,),
            in_specs=[spec, spec, row_spec, row_spec, col_spec, col_spec],
            out_specs=specs,
            scratch_shapes=[
                pltpu.VMEM((2, 2 * tall, DEPTH), jnp.bfloat16),
                pltpu.VMEM((2, 2 * tall, DEPTH), jnp.bfloat16),
                pltpu.VMEM((2, 2 * COL_TILES + 1, cuts * height, WINDOW), jnp.float32),
            ],
        ),
        cost_estimate=pl.CostEstimate(
            flops=24 * tall * DEPTH * DEPTH + 12 * cuts * height * DEPTH * FOLD,
            bytes_accessed=16 * DEPTH * DEPTH + 16 * tall * DEPTH,
            transcendentals=0,
        ),
        name="inverse",
    )(
        info, jnp.asarray(slots), positions, *weights, sign, *spectrum, *row_table,
        *column_table(),
    )


def column_inverse_kernel(
    layout, info_ref, slot_ref, pos_ref, re_ref, im_ref, sign_ref,
    rows_hi, rows_lo, table_hi, table_lo, keep_ref, send_ref, field,
):
    chip_rows, _, _, segments = layout
    height = chip_rows + WINDOW
    step = pl.program_id(0)
    tile = step % COL_TILES

    @pl.when(step < 2 * segments * COL_TILES)
    def _():
        part = step // COL_TILES % 2
        start = pl.multiple_of(step // (2 * COL_TILES) * height, LANES)
        rows = pl.ds(start, height)
        value = dot3((rows_hi[0], rows_lo[0]), (table_hi[0], table_lo[0]))
        field[part, 2 * tile, rows] = value[:, :LANES]
        field[part, 2 * tile + 1, rows] = value[:, LANES:]

        @pl.when(tile == 0)
        def _():
            field[part, 2 * COL_TILES, rows] = value[:, :LANES] * sign_ref[0]

    @pl.when(step == 2 * segments * COL_TILES)
    def _():
        cut_slots(
            layout, info_ref, slot_ref, pos_ref, re_ref, im_ref, sign_ref, field,
            (keep_ref, send_ref),
        )


def column_inverse(layout, rows, slots, info, positions, weights, sign):
    chip_rows, _, _, segments = layout
    count = slots.shape[1] // 2
    height = chip_rows + WINDOW
    table = column_table()
    last = 2 * segments * COL_TILES - 1

    def rows_map(i, info, *_):
        i = jnp.minimum(i, last)
        return i // COL_TILES % 2, i // (2 * COL_TILES), 0

    rows_spec = pl.BlockSpec((1, height, DEPTH), rows_map)
    table_spec = pl.BlockSpec(
        (1, DEPTH, PAIR), lambda i, info, *_: (info[2], 0, jnp.minimum(i, last) % COL_TILES)
    )
    out = jax.ShapeDtypeStruct((count, 2, WINDOW, WINDOW), jnp.float32)
    out_spec = pl.BlockSpec(
        (count, 2, WINDOW, WINDOW), lambda i, *_: (0, 0, 0, 0), pipeline_mode=pl.Buffered(1)
    )
    return pl.pallas_call(
        functools.partial(column_inverse_kernel, layout),
        out_shape=(out, out),
        grid_spec=pltpu.PrefetchScalarGridSpec(
            num_scalar_prefetch=6,
            grid=(last + 2,),
            in_specs=[
                rows_spec,
                rows_spec,
                table_spec,
                table_spec,
            ],
            out_specs=(out_spec, out_spec),
            scratch_shapes=[
                pltpu.VMEM((2, 2 * COL_TILES + 1, segments * height, WINDOW), jnp.float32)
            ],
        ),
        cost_estimate=pl.CostEstimate(
            flops=12 * segments * height * DEPTH * FOLD,
            bytes_accessed=8 * segments * height * DEPTH + 16 * count * WINDOW * WINDOW,
            transcendentals=0,
        ),
        name="column_inverse",
    )(
        info, jnp.asarray(slots), positions, *weights, sign, *rows, *table,
    )


def sum_kernel(count, halve, *refs):
    total = refs[0][0]
    for ref in refs[1:count]:
        total += ref[0]
    if halve:
        refs[count][...] = total[0]
        refs[count + 1][...] = total[1]
    else:
        refs[count][...] = total


def sum_of(terms, halve):
    tail = terms[0][0].shape[1:]
    zeros = (0,) * len(tail)
    count = terms[0][0].shape[0] // terms[0][2] // (2 if halve else 1)
    step = max(1, count // 2)
    specs, arrays = [], []
    for array, part, parts in terms:
        if halve:
            arrays.append(array.reshape((parts, 2, count) + tail))
            specs.append(
                pl.BlockSpec((1, 2, step) + tail, lambda i, part=part: (part, 0, i) + zeros)
            )
        else:
            arrays.append(array.reshape((parts, count) + tail))
            specs.append(
                pl.BlockSpec((1, step) + tail, lambda i, part=part: (part, i) + zeros)
            )
    out = jax.ShapeDtypeStruct((count,) + tail, jnp.float32)
    out_spec = pl.BlockSpec((step,) + tail, lambda i: (i,) + zeros)
    size = count * 4 * math.prod(tail) * (2 if halve else 1)
    return pl.pallas_call(
        functools.partial(sum_kernel, len(terms), halve),
        out_shape=(out, out) if halve else out,
        grid=(count // step,),
        in_specs=specs,
        out_specs=(out_spec, out_spec) if halve else out_spec,
        cost_estimate=pl.CostEstimate(
            flops=size, bytes_accessed=(len(terms) + 1) * size, transcendentals=0
        ),
        name="sum_of",
    )(*arrays)


def power_kernel(count, scale, *refs):
    terms, (down_ref, along_ref, out_ref) = refs[:count], refs[count:]
    down, along = halves_of(down_ref[...]), halves_of(along_ref[...])
    for probe in range(out_ref.shape[0]):
        total = terms[0][probe]
        for term in terms[1:]:
            total += term[probe]
        value = dot3(down, halves_of(jnp.concatenate([total[0], total[1]], axis=1)))
        cos_part, sin_part = value[:WINDOW], value[WINDOW:]
        real_part = cos_part[:, :WINDOW] + sin_part[:, WINDOW:]
        imag_part = cos_part[:, WINDOW:] - sin_part[:, :WINDOW]
        value = dot3(halves_of(jnp.concatenate([real_part, imag_part])), along)
        real_part = value[:WINDOW, :WINDOW] + value[WINDOW:, WINDOW:]
        imag_part = value[WINDOW:, :WINDOW] - value[:WINDOW, WINDOW:]
        out_ref[probe] = (real_part * real_part + imag_part * imag_part) * scale


def power_of(terms, scale):
    count = terms[0].shape[0]
    table = cos_sin(np.arange(WINDOW), FACTOR * np.arange(WINDOW))
    return pl.pallas_call(
        functools.partial(power_kernel, len(terms), scale),
        out_shape=jax.ShapeDtypeStruct((count, WINDOW, WINDOW), jnp.float32),
        name="power_of",
    )(
        *terms, jnp.asarray(np.concatenate(list(table)).astype(np.float32)),
        jnp.asarray(np.concatenate(list(table), axis=1).astype(np.float32)),
    )


def coefficients(positions, wave_index, wave_weight, wave_phase):
    turns = (FACTOR * (positions[0] * wave_index[0, 0] + positions[1] * wave_index[0, 1])) % GRID
    angles = wave_phase[0] - turns.astype(jnp.float32) * (2.0 * math.pi / GRID)
    return wave_weight[0] * jnp.cos(angles), wave_weight[0] * jnp.sin(angles)


def flip(block, axis, bit):
    count = lax.axis_size(axis)
    return lax.ppermute(block, axis, [(i, i ^ bit) for i in range(count)])


def shards(plane_waves, transmission, wave_index, wave_weight, wave_phase, probe_pos):
    rows_here = plane_waves.shape[2]
    row_count = lax.axis_size("row")
    wave_count = lax.axis_size("wave")
    row_rank = lax.axis_index("row")
    wave_rank = lax.axis_index("wave")
    core = row_rank % 2
    sign = (1.0 - 2.0 * core.astype(jnp.float32))[None]
    parity = core[None]
    chip_rows = 2 * rows_here
    chips = row_count // 2
    far = chips // 2
    own = probe_pos.shape[0] // (row_count * wave_count)

    mine, theirs = split_columns(sign, plane_waves, transmission)
    theirs = flip(theirs, "row", 1)
    positions = probe_pos.T
    weights = coefficients(positions, wave_index, wave_weight, wave_phase)
    mine = column_forward(parity, mine)
    mine, theirs = lax.optimization_barrier((mine, theirs))
    spectrum = row_forward(parity, mine, column_forward(parity, theirs))

    wave_bits = wave_count.bit_length() - 1
    orders = (list(range(wave_bits - 1, -1, -1)), list(range(wave_bits)))
    segments = far // 2
    layout = (chip_rows, wave_count, own, segments)

    def slots_of(odd, halves):
        slots = []
        for core_bit in (0, 1):
            for at, half in enumerate(halves):
                for digits in range(wave_count):
                    wave = 0
                    for place, bit in enumerate(orders[half]):
                        wave |= (digits >> (wave_bits - 1 - place) & 1) << bit
                    for index in range(segments):
                        row = ((half * segments + index) * 2 + odd) * 2 + core_bit
                        where = at * segments + index
                        slots += [(row, wave, probe, where) for probe in range(own)]
        return np.array(slots, np.int32).T

    def info_of(odd, halves):
        chip = row_rank // 2
        info = [row_rank, wave_rank, core]
        for half in halves:
            for index in range(segments):
                target = chip ^ ((half * segments + index) * 2 + odd)
                away = (target - chip) % chips
                info.append(away // far * segments + away % far // 2)
        return jnp.stack(info)

    def rows_of(odd):
        return np.concatenate(
            [
                chip_rows * away - HALF + np.arange(chip_rows + WINDOW)
                for away in range(odd, far, 2)
            ]
        )

    def later(value, *before):
        return lax.optimization_barrier((value,) + before)

    upper, lower = 1, 0
    common = (positions, weights, sign)
    stages = {}

    def advance(value, *keys):
        for key in keys:
            terms, place = stages[key]
            stay, send = sum_of(terms, True)
            if value is not None:
                value, stay, send = later(value, stay, send)
            arrived = flip(send, "wave", 1 << orders[key[1]][place])
            stages[key] = [[(stay, 0, 1), (arrived, 0, 1)], place + 1]
        return value

    def finish(key):
        while stages[key][1] < wave_bits:
            advance(None, key)
        return stages[key][0]

    keep, send = inverse(
        layout, 2 * segments, False, spectrum, rows_of(1), slots_of(1, (upper, lower)),
        info_of(1, (upper, lower)), *common,
    )
    arrived = flip(send, "row", 1)
    for at, half in enumerate((upper, lower)):
        stages[1, half] = [[(keep, at, 2), (arrived, at, 2)], 0]
    spectrum = later(spectrum, send)[0]
    keep, send, rows_hi, rows_lo = inverse(
        layout, segments, True, spectrum, rows_of(0), slots_of(0, (upper,)),
        info_of(0, (upper, lower)), *common,
    )
    stages[0, upper] = [[(keep, 0, 1), (flip(send, "row", 1), 0, 1)], 0]
    rows = (rows_hi, rows_lo)
    rows = advance(rows, (1, upper), (1, lower))
    keep, send = column_inverse(
        layout, rows, slots_of(0, (lower,)), info_of(0, (lower,)), *common
    )
    stages[0, lower] = [[(keep, 0, 1), (flip(send, "row", 1), 0, 1)], 0]

    near_upper = flip(sum_of(finish((1, upper)), False), "row", 2)
    near_lower = flip(sum_of(finish((1, lower)), False), "row", 2)
    bit = row_count // 2
    send = sum_of(finish((0, upper)) + [(near_upper, 0, 1)], False)
    terms = [term[0] for term in finish((0, lower))] + [near_lower, flip(send, "row", bit)]
    while bit > 4:
        bit //= 2
        stay, send = sum_of([(term, 0, 1) for term in terms], True)
        terms = [stay, flip(send, "row", bit)]
    total_waves = plane_waves.shape[1] * wave_count
    power = power_of(terms, 1.0 / (WINDOW * WINDOW * total_waves))
    return lax.all_to_all(power, "wave", split_axis=1, concat_axis=0, tiled=True)


def solution(mesh):
    return jax.shard_map(
        shards,
        mesh=mesh,
        in_specs=(
            P(None, "wave", "row", None),
            P(None, None, "row", None),
            P("wave", None),
            P("wave"),
            P("wave"),
            P(),
        ),
        out_specs=P("row", "wave", None),
        check_vma=False,
    )
```

```python
import functools
import math

import jax
import jax.numpy as jnp
import numpy as np
from jax import lax
from jax.experimental import pallas as pl
from jax.experimental.pallas import tpu as pltpu
from jax.sharding import PartitionSpec as P

GRID = 2048
FACTOR = 16
WINDOW = 128
HALF = 64
FRESNEL = 0.1

BAND = math.isqrt(GRID * GRID // 9)
FOLD = GRID // 2
BLOCKS = 3
LANES = 128
PAIR = 2 * LANES
DEPTH = BLOCKS * PAIR
FREQS = BLOCKS * LANES
COL_TILES = FOLD // PAIR
CUT_STEPS = 4


def angles_of(first, second):
    return (2.0 * math.pi / GRID) * (np.outer(first, second) % GRID)


def cos_sin(first, second):
    angle = angles_of(first, second)
    return np.stack([np.cos(angle), np.sin(angle)])


def freqs(parity):
    return 2 * np.arange(FREQS) + parity


def both(function):
    return np.stack([function(freqs(0)), function(freqs(1))])


def halves_of(value):
    high = value.astype(jnp.bfloat16)
    return high, (value - high.astype(jnp.float32)).astype(jnp.bfloat16)


def dot3(left, right):
    def term(first, second):
        return jnp.dot(first, second, preferred_element_type=jnp.float32)

    return term(left[0], right[0]) + term(left[0], right[1]) + term(left[1], right[0])


def paired(values):
    blocks = values.reshape(values.shape[:-1] + (-1, LANES))
    return np.moveaxis(blocks, 0, -2).reshape(values.shape[1:-1] + (-1,))


def table_halves(table):
    high = table.astype(jnp.bfloat16)
    low = (table - high.astype(np.float64)).astype(jnp.bfloat16)
    return jnp.asarray(high), jnp.asarray(low)


def put(refs, place, value):
    high, low = halves_of(value)
    refs[0][place] = high
    refs[1][place] = low


def sign_of(info_ref):
    return 1.0 - 2.0 * info_ref[2].astype(jnp.float32)


def split_kernel(info_ref, wave_ref, trans_ref, mine_ref, theirs_ref):
    wave_re, wave_im = wave_ref[0, 0], wave_ref[1, 0]
    trans_re, trans_im = trans_ref[0, 0], trans_ref[0, 1]
    sign = sign_of(info_ref)
    for part, value in enumerate(
        (wave_re * trans_re - wave_im * trans_im, wave_re * trans_im + wave_im * trans_re)
    ):
        low, high = value[:, :FOLD], sign * value[:, FOLD:]
        mine_ref[part] = low + high
        theirs_ref[part] = low - high


def split_columns(info, plane_waves, transmission):
    rows = plane_waves.shape[2]
    step = 32
    out = jax.ShapeDtypeStruct((2, rows, FOLD), jnp.float32)
    out_spec = pl.BlockSpec((2, step, FOLD), lambda i, *_: (0, i, 0))
    return pl.pallas_call(
        split_kernel,
        out_shape=(out, out),
        grid_spec=pltpu.PrefetchScalarGridSpec(
            num_scalar_prefetch=1,
            grid=(rows // step,),
            in_specs=[
                pl.BlockSpec((2, 1, step, GRID), lambda i, *_: (0, 0, i, 0)),
                pl.BlockSpec((1, 2, step, GRID), lambda i, *_: (0, 0, i, 0)),
            ],
            out_specs=(out_spec, out_spec),
        ),
        cost_estimate=pl.CostEstimate(
            flops=20 * rows * GRID, bytes_accessed=24 * rows * GRID, transcendentals=0
        ),
        name="split_columns",
    )(info, plane_waves, transmission)


def column_forward_table():
    return table_halves(both(lambda freq: paired(cos_sin(np.arange(FOLD), freq))))


def column_forward_kernel(info_ref, field_ref, table_hi, table_lo, out_ref, *field):
    rows = field_ref.shape[1]

    @pl.when(pl.program_id(0) == 0)
    def _():
        for part in (0, 1):
            put(field, slice(part * rows, (part + 1) * rows), field_ref[part])

    result = dot3((field[0][...], field[1][...]), (table_hi[0], table_lo[0]))
    for part in (0, 1):
        out_ref[part] = result[part * rows : (part + 1) * rows]


def column_forward(info, field):
    rows = field.shape[1]
    table = column_forward_table()
    table_spec = pl.BlockSpec((1, FOLD, PAIR), lambda j, info: (info[2], 0, j))
    return pl.pallas_call(
        column_forward_kernel,
        out_shape=jax.ShapeDtypeStruct((2, rows, DEPTH), jnp.float32),
        grid_spec=pltpu.PrefetchScalarGridSpec(
            num_scalar_prefetch=1,
            grid=(BLOCKS,),
            in_specs=[
                pl.BlockSpec((2, rows, FOLD), lambda j, *_: (0, 0, 0)),
                table_spec,
                table_spec,
            ],
            out_specs=pl.BlockSpec((2, rows, PAIR), lambda j, *_: (0, 0, j)),
            scratch_shapes=[pltpu.VMEM((2 * rows, FOLD), jnp.bfloat16)] * 2,
        ),
        cost_estimate=pl.CostEstimate(
            flops=12 * rows * FOLD * DEPTH,
            bytes_accessed=8 * rows * (FOLD + DEPTH),
            transcendentals=0,
        ),
        name="column_forward",
    )(info, field, *table)


def row_forward_kernel(
    info_ref, mine_ref, theirs_ref, col_hi, col_lo, table_hi, table_lo, down_ref, along_ref,
    out_hi, out_lo, field_hi, field_lo, theirs_hi, theirs_lo,
):
    rows = mine_ref.shape[1]
    field = (field_hi, field_lo)
    core = info_ref[2]

    @pl.when(pl.program_id(0) == 0)
    def _():
        for part in (0, 1):
            put((theirs_hi, theirs_lo), slice(part * rows, (part + 1) * rows), theirs_ref[part])

    theirs = dot3((theirs_hi[...], theirs_lo[...]), (col_hi[0], col_lo[0]))
    here = pl.ds(pl.multiple_of(core * rows, LANES), rows)
    there = pl.ds(pl.multiple_of((1 - core) * rows, LANES), rows)
    for part in (0, 1):
        cols = slice(part * PAIR, (part + 1) * PAIR)
        put(field, (here, cols), mine_ref[part])
        put(field, (there, cols), theirs[part * rows : (part + 1) * rows])
    cos_x, sin_x, square_x = (along_ref[0, i : i + 1] for i in range(3))
    outs = (out_hi, out_lo)

    def blocks(parity, count):
        first = parity * DEPTH
        part = slice(first, first + count * PAIR)
        result = dot3((table_hi[part], table_lo[part]), (field_hi[...], field_lo[...]))
        for block in range(count):
            freq = slice((parity * BLOCKS + block) * LANES, (parity * BLOCKS + block + 1) * LANES)
            cos_y, sin_y, square_y = (down_ref[freq, i : i + 1] for i in range(3))
            inside = 9.0 * (square_y + square_x) <= GRID * GRID
            prop_re = jnp.where(inside, cos_y * cos_x - sin_y * sin_x, 0.0)
            prop_im = jnp.where(inside, -(sin_y * cos_x + cos_y * sin_x), 0.0)
            for kind in (0, 1):
                start = block * PAIR + kind * LANES
                place = slice(first + start, first + start + LANES)
                for side in (0, 1):
                    cols = slice(side * LANES, (side + 1) * LANES)
                    real_part = result[start : start + LANES, cols]
                    imag_part = result[start : start + LANES, slice(PAIR + side * LANES, PAIR + (side + 1) * LANES)]
                    put(outs, (0, place, cols), prop_re * real_part - prop_im * imag_part)
                    put(outs, (1, place, cols), prop_re * imag_part + prop_im * real_part)

    last = pl.program_id(0) == BLOCKS - 1
    for parity in (0, 1):
        pl.when(last)(functools.partial(blocks, parity, BLOCKS - 1))
        pl.when(jnp.logical_not(last))(functools.partial(blocks, parity, BLOCKS))


def axis_factors(freq):
    angle = freq.astype(np.float64) ** 2 * (math.pi * FRESNEL / GRID)
    weight = np.where(freq == 0, 1.0, 2.0) / GRID
    return [np.cos(angle) * weight, np.sin(angle) * weight, freq.astype(np.float64) ** 2]


def row_forward(info, mine, theirs):
    rows = mine.shape[1]
    all_freqs = np.concatenate([freqs(0), freqs(1)])
    table = table_halves(paired(cos_sin(np.arange(2 * rows), all_freqs)).T)
    down = np.stack(axis_factors(all_freqs)).T.astype(np.float32)
    along = both(lambda freq: np.stack(axis_factors(freq))).astype(np.float32)
    tile = pl.BlockSpec((2, rows, PAIR), lambda j, *_: (0, 0, j))
    out = jax.ShapeDtypeStruct((2, 2 * DEPTH, DEPTH), jnp.bfloat16)
    out_spec = pl.BlockSpec((2, 2 * DEPTH, PAIR), lambda j, *_: (0, 0, j))
    table_spec = pl.BlockSpec(
        (2 * DEPTH, 2 * rows), lambda j, *_: (0, 0), pipeline_mode=pl.Buffered(1)
    )
    col_spec = pl.BlockSpec((1, FOLD, PAIR), lambda j, info: (info[2], 0, j))
    return pl.pallas_call(
        row_forward_kernel,
        out_shape=(out, out),
        grid_spec=pltpu.PrefetchScalarGridSpec(
            num_scalar_prefetch=1,
            grid=(BLOCKS,),
            in_specs=[
                tile,
                pl.BlockSpec(
                    (2, rows, FOLD), lambda j, *_: (0, 0, 0), pipeline_mode=pl.Buffered(1)
                ),
                col_spec,
                col_spec,
                table_spec,
                table_spec,
                pl.BlockSpec(down.shape, lambda j, *_: (0, 0)),
                pl.BlockSpec((1, 3, LANES), lambda j, info: (info[2], 0, j)),
            ],
            out_specs=(out_spec, out_spec),
            scratch_shapes=[pltpu.VMEM((2 * rows, 2 * PAIR), jnp.bfloat16)] * 2
            + [pltpu.VMEM((2 * rows, FOLD), jnp.bfloat16)] * 2,
        ),
        cost_estimate=pl.CostEstimate(
            flops=48 * rows * DEPTH * DEPTH,
            bytes_accessed=16 * rows * DEPTH + 16 * DEPTH * DEPTH,
            transcendentals=0,
        ),
        name="row_forward",
    )(
        info, mine, theirs, *column_forward_table(), *table, jnp.asarray(down),
        jnp.asarray(along),
    )


def cut_slots(layout, first, info_ref, slot_ref, pos_ref, weight_ref, field, outs):
    chip_rows, waves, own, _ = layout
    height = chip_rows + WINDOW
    lane = lax.broadcasted_iota(jnp.int32, (WINDOW, WINDOW), 1)
    row_rank, wave_rank = info_ref[0], info_ref[1]

    def one(index, out_ref, place):
        target = row_rank ^ slot_ref[0, index]
        probe = (target * waves + (wave_rank ^ slot_ref[1, index])) * own + slot_ref[2, index]
        row = slot_ref[3, index] * height + lax.rem(pos_ref[probe, 0], chip_rows)
        start = lax.rem(pos_ref[probe, 1] + (GRID - HALF), GRID)
        col = lax.rem(start, FOLD)
        turned = jnp.where(start >= FOLD, sign_of(info_ref), 1.0)
        shift = lax.rem(col, LANES)
        back = lax.rem(LANES - shift, LANES)

        def cut(part):
            sides = [
                pltpu.roll(field[part, col // LANES + side, pl.ds(row, WINDOW)], back, 1)
                for side in (0, 1)
            ]
            return jnp.where(lane < LANES - shift, sides[0], sides[1])

        real_part, imag_part = cut(0), cut(1)
        weight_re, weight_im = weight_ref[0, probe] * turned, weight_ref[1, probe] * turned
        out_ref[place, 0] = weight_re * real_part - weight_im * imag_part
        out_ref[place, 1] = weight_re * imag_part + weight_im * real_part

    keep_ref, send_ref = outs
    total = slot_ref.shape[1] // 2

    @pl.loop(0, keep_ref.shape[0])
    def _(place):
        one(total + first + place, send_ref, place)
        one(first + place, keep_ref, place)


def inverse_kernel(
    layout, cuts, base, info_ref, slot_ref, pos_ref, weight_ref,
    spec_hi, spec_lo, row_hi, row_lo, col_hi, col_lo, *refs,
):
    chip_rows, _, _, segments = layout
    height = chip_rows + WINDOW
    refs = list(refs)
    outs = refs[:2]
    exports = refs[2:4] if len(refs) > 5 else None
    rows, field = refs[-3:-1], refs[-1]
    step = pl.program_id(0)
    first = 2 * BLOCKS
    last = first + 2 * cuts * COL_TILES

    def row_part(depth):
        part = step // BLOCKS
        place = pl.multiple_of(step % BLOCKS * PAIR, PAIR)
        cols = pl.ds(place, PAIR)
        count = row_hi.shape[0]
        sums = []
        for parity in (0, 1):
            freq = slice(parity * DEPTH, parity * DEPTH + depth * PAIR)
            sums.append(
                dot3((row_hi[:, freq], row_lo[:, freq]), (spec_hi[0, freq], spec_lo[0, freq]))
            )
        put(rows, (part, slice(0, count), cols), sums[0] + sums[1])
        put(rows, (part, slice(count, 2 * count), cols), sums[0] - sums[1])
        if exports is not None:
            for index in range(segments):
                start = pl.multiple_of(info_ref[base + cuts + index] * height, LANES)
                for export, source in zip(exports, rows):
                    export[0, index * height : (index + 1) * height] = source[
                        part, pl.ds(start, height), cols
                    ]

    zero_blocks = step % BLOCKS == BLOCKS - 1
    pl.when((step < first) & zero_blocks)(functools.partial(row_part, BLOCKS - 1))
    pl.when((step < first) & jnp.logical_not(zero_blocks))(functools.partial(row_part, BLOCKS))

    @pl.when((step >= first) & (step < last))
    def _():
        now = step - first
        tile = now % COL_TILES
        part = now // COL_TILES % 2
        segment = now // (2 * COL_TILES)
        source = pl.ds(pl.multiple_of(info_ref[base + segment] * height, LANES), height)
        place = pl.ds(pl.multiple_of(segment * height, LANES), height)
        value = dot3((rows[0][part, source], rows[1][part, source]), (col_hi[0], col_lo[0]))
        field[part, 2 * tile, place] = value[:, :LANES]
        field[part, 2 * tile + 1, place] = value[:, LANES:]

        @pl.when(tile == 0)
        def _():
            field[part, 2 * COL_TILES, place] = value[:, :LANES] * sign_of(info_ref)

    @pl.when(step >= last)
    def _():
        begin = (step - last) * outs[0].shape[0]
        cut_slots(layout, begin, info_ref, slot_ref, pos_ref, weight_ref, field, outs)


def window_spec(count, last):
    return pl.BlockSpec(
        (count // CUT_STEPS, 2, WINDOW, WINDOW),
        lambda i, *_: (jnp.maximum(i - last, 0), 0, 0, 0),
    )


def column_table():
    return table_halves(both(lambda freq: paired(cos_sin(np.arange(FOLD), freq)).T))


def inverse(layout, cuts, export, base, spectrum, row_list, slots, info, positions, weights):
    chip_rows, _, _, segments = layout
    height = chip_rows + WINDOW
    count = slots.shape[1] // 2
    tall = len(row_list)
    row_table = table_halves(paired(cos_sin(row_list, np.concatenate([freqs(0), freqs(1)]))))
    first = 2 * BLOCKS
    last = first + 2 * cuts * COL_TILES

    def spec_map(i, *_):
        i = jnp.minimum(i, first - 1)
        return i // BLOCKS, 0, i % BLOCKS

    def col_map(i, info, *_):
        return info[2], 0, (jnp.clip(i, first, last - 1) - first) % COL_TILES

    spec = pl.BlockSpec((1, 2 * DEPTH, PAIR), spec_map)
    row_spec = pl.BlockSpec(
        (tall, 2 * DEPTH), lambda i, *_: (0, 0), pipeline_mode=pl.Buffered(1)
    )
    col_spec = pl.BlockSpec((1, DEPTH, PAIR), col_map)
    shapes = [jax.ShapeDtypeStruct((count, 2, WINDOW, WINDOW), jnp.float32)] * 2
    specs = [window_spec(count, last)] * 2
    if export:
        shapes += [jax.ShapeDtypeStruct((2, segments * height, DEPTH), jnp.bfloat16)] * 2
        specs += [pl.BlockSpec((1, segments * height, PAIR), spec_map)] * 2
    return pl.pallas_call(
        functools.partial(inverse_kernel, layout, cuts, base),
        out_shape=shapes,
        grid_spec=pltpu.PrefetchScalarGridSpec(
            num_scalar_prefetch=4,
            grid=(last + CUT_STEPS,),
            in_specs=[spec, spec, row_spec, row_spec, col_spec, col_spec],
            out_specs=specs,
            scratch_shapes=[
                pltpu.VMEM((2, 2 * tall, DEPTH), jnp.bfloat16),
                pltpu.VMEM((2, 2 * tall, DEPTH), jnp.bfloat16),
                pltpu.VMEM((2, 2 * COL_TILES + 1, cuts * height, WINDOW), jnp.float32),
            ],
        ),
        cost_estimate=pl.CostEstimate(
            flops=24 * tall * DEPTH * DEPTH + 12 * cuts * height * DEPTH * FOLD,
            bytes_accessed=16 * DEPTH * DEPTH + 16 * tall * DEPTH,
            transcendentals=0,
        ),
        name="inverse",
    )(
        info, jnp.asarray(slots), positions, weights, *spectrum, *row_table, *column_table(),
    )


def column_inverse_kernel(
    layout, info_ref, slot_ref, pos_ref, weight_ref,
    rows_hi, rows_lo, table_hi, table_lo, keep_ref, send_ref, field,
):
    chip_rows, _, _, segments = layout
    height = chip_rows + WINDOW
    step = pl.program_id(0)
    tile = step % COL_TILES

    @pl.when(step < 2 * segments * COL_TILES)
    def _():
        part = step // COL_TILES % 2
        start = pl.multiple_of(step // (2 * COL_TILES) * height, LANES)
        rows = pl.ds(start, height)
        value = dot3((rows_hi[0], rows_lo[0]), (table_hi[0], table_lo[0]))
        field[part, 2 * tile, rows] = value[:, :LANES]
        field[part, 2 * tile + 1, rows] = value[:, LANES:]

        @pl.when(tile == 0)
        def _():
            field[part, 2 * COL_TILES, rows] = value[:, :LANES] * sign_of(info_ref)

    @pl.when(step >= 2 * segments * COL_TILES)
    def _():
        begin = (step - 2 * segments * COL_TILES) * keep_ref.shape[0]
        outs = (keep_ref, send_ref)
        cut_slots(layout, begin, info_ref, slot_ref, pos_ref, weight_ref, field, outs)


def column_inverse(layout, rows, slots, info, positions, weights):
    chip_rows, _, _, segments = layout
    count = slots.shape[1] // 2
    height = chip_rows + WINDOW
    table = column_table()
    last = 2 * segments * COL_TILES - 1

    def rows_map(i, info, *_):
        i = jnp.minimum(i, last)
        return i // COL_TILES % 2, i // (2 * COL_TILES), 0

    rows_spec = pl.BlockSpec((1, height, DEPTH), rows_map)
    table_spec = pl.BlockSpec(
        (1, DEPTH, PAIR), lambda i, info, *_: (info[2], 0, jnp.minimum(i, last) % COL_TILES)
    )
    out = jax.ShapeDtypeStruct((count, 2, WINDOW, WINDOW), jnp.float32)
    out_spec = window_spec(count, last + 1)
    return pl.pallas_call(
        functools.partial(column_inverse_kernel, layout),
        out_shape=(out, out),
        grid_spec=pltpu.PrefetchScalarGridSpec(
            num_scalar_prefetch=4,
            grid=(last + 1 + CUT_STEPS,),
            in_specs=[
                rows_spec,
                rows_spec,
                table_spec,
                table_spec,
            ],
            out_specs=(out_spec, out_spec),
            scratch_shapes=[
                pltpu.VMEM((2, 2 * COL_TILES + 1, segments * height, WINDOW), jnp.float32)
            ],
        ),
        cost_estimate=pl.CostEstimate(
            flops=12 * segments * height * DEPTH * FOLD,
            bytes_accessed=8 * segments * height * DEPTH + 16 * count * WINDOW * WINDOW,
            transcendentals=0,
        ),
        name="column_inverse",
    )(
        info, jnp.asarray(slots), positions, weights, *rows, *table,
    )


def sum_kernel(count, halve, *refs):
    total = refs[0][0]
    for ref in refs[1:count]:
        total += ref[0]
    if halve:
        refs[count][...] = total[0]
        refs[count + 1][...] = total[1]
    else:
        refs[count][...] = total


def sum_of(terms, halve):
    tail = terms[0][0].shape[1:]
    zeros = (0,) * len(tail)
    count = terms[0][0].shape[0] // terms[0][2] // (2 if halve else 1)
    step = max(1, count // 2)
    specs, arrays = [], []
    for array, part, parts in terms:
        if halve:
            arrays.append(array.reshape((parts, 2, count) + tail))
            specs.append(
                pl.BlockSpec((1, 2, step) + tail, lambda i, part=part: (part, 0, i) + zeros)
            )
        else:
            arrays.append(array.reshape((parts, count) + tail))
            specs.append(
                pl.BlockSpec((1, step) + tail, lambda i, part=part: (part, i) + zeros)
            )
    out = jax.ShapeDtypeStruct((count,) + tail, jnp.float32)
    out_spec = pl.BlockSpec((step,) + tail, lambda i: (i,) + zeros)
    size = count * 4 * math.prod(tail) * (2 if halve else 1)
    return pl.pallas_call(
        functools.partial(sum_kernel, len(terms), halve),
        out_shape=(out, out) if halve else out,
        grid=(count // step,),
        in_specs=specs,
        out_specs=(out_spec, out_spec) if halve else out_spec,
        cost_estimate=pl.CostEstimate(
            flops=size, bytes_accessed=(len(terms) + 1) * size, transcendentals=0
        ),
        name="sum_of",
    )(*arrays)


def spread_kernel(first_ref, second_ref, *outs):
    for index, out_ref in enumerate(outs):
        out_ref[...] = first_ref[index] + second_ref[index]


def spread_sum(first, second, count):
    tail = first.shape[1:]
    zeros = (0,) * len(tail)
    size = first.shape[0] // count
    step = max(1, size // 2)
    out = jax.ShapeDtypeStruct((size,) + tail, jnp.float32)
    spec = pl.BlockSpec((count, step) + tail, lambda i: (0, i) + zeros)
    return pl.pallas_call(
        spread_kernel,
        out_shape=[out] * count,
        grid=(size // step,),
        in_specs=[spec, spec],
        out_specs=[pl.BlockSpec((step,) + tail, lambda i: (i,) + zeros)] * count,
        cost_estimate=pl.CostEstimate(
            flops=first.size, bytes_accessed=12 * first.size, transcendentals=0
        ),
        name="spread_sum",
    )(*(value.reshape((count, size) + tail) for value in (first, second)))


def power_kernel(count, scale, *refs):
    terms, (down_ref, along_ref, out_ref) = refs[:count], refs[count:]
    down, along = halves_of(down_ref[...]), halves_of(along_ref[...])
    total = terms[0][0, 0]
    for term in terms[1:]:
        total += term[0, 0]
    value = dot3(down, halves_of(jnp.concatenate([total[0], total[1]], axis=1)))
    cos_part, sin_part = value[:WINDOW], value[WINDOW:]
    real_part = cos_part[:, :WINDOW] + sin_part[:, WINDOW:]
    imag_part = cos_part[:, WINDOW:] - sin_part[:, :WINDOW]
    value = dot3(halves_of(jnp.concatenate([real_part, imag_part])), along)
    real_part = value[:WINDOW, :WINDOW] + value[WINDOW:, WINDOW:]
    imag_part = value[WINDOW:, :WINDOW] - value[:WINDOW, WINDOW:]
    out_ref[0] = (real_part * real_part + imag_part * imag_part) * scale


def power_of(terms, scale):
    tail = terms[0][0].shape[1:]
    count = terms[0][0].shape[0] // terms[0][2]
    table = cos_sin(np.arange(WINDOW), FACTOR * np.arange(WINDOW)).astype(np.float32)
    down, along = np.concatenate(list(table)), np.concatenate(list(table), axis=1)
    return pl.pallas_call(
        functools.partial(power_kernel, len(terms), scale),
        out_shape=jax.ShapeDtypeStruct((count, WINDOW, WINDOW), jnp.float32),
        grid=(count,),
        in_specs=[
            pl.BlockSpec((1, 1) + tail, lambda i, part=part: (part, i, 0, 0, 0))
            for _, part, _ in terms
        ]
        + [
            pl.BlockSpec(down.shape, lambda i: (0, 0)),
            pl.BlockSpec(along.shape, lambda i: (0, 0)),
        ],
        out_specs=pl.BlockSpec((1, WINDOW, WINDOW), lambda i: (i, 0, 0)),
        name="power_of",
    )(
        *(array.reshape((parts, count) + tail) for array, _, parts in terms),
        jnp.asarray(down), jnp.asarray(along),
    )


def coefficients(positions, wave_index, wave_weight, wave_phase):
    turns = (
        FACTOR * (positions[:, 0] * wave_index[0, 0] + positions[:, 1] * wave_index[0, 1])
    ) % GRID
    angles = wave_phase[0] - turns.astype(jnp.float32) * (2.0 * math.pi / GRID)
    return wave_weight[0] * jnp.stack([jnp.cos(angles), jnp.sin(angles)])


def flip(block, axis, bit):
    count = lax.axis_size(axis)
    return lax.ppermute(block, axis, [(i, i ^ bit) for i in range(count)])


def shards(plane_waves, transmission, wave_index, wave_weight, wave_phase, probe_pos):
    rows_here = plane_waves.shape[2]
    row_count = lax.axis_size("row")
    wave_count = lax.axis_size("wave")
    row_rank = lax.axis_index("row")
    wave_rank = lax.axis_index("wave")
    core = row_rank % 2
    chip_rows = 2 * rows_here
    chips = row_count // 2
    far = chips // 2
    own = probe_pos.shape[0] // (row_count * wave_count)

    segments = far // 2
    layout = (chip_rows, wave_count, own, segments)

    def slots_of(odd, halves):
        slots = []
        for core_bit in (0, 1):
            for wave in range(wave_count):
                for at, half in enumerate(halves):
                    for index in range(segments):
                        row = ((half * segments + index) * 2 + odd) * 2 + core_bit
                        where = at * segments + index
                        slots += [(row, wave, probe, where) for probe in range(own)]
        return np.array(slots, np.int32).T

    upper, lower = 1, 0
    chip = row_rank // 2
    info = [row_rank, wave_rank, core]
    for odd in (1, 0):
        for half in (upper, lower):
            for index in range(segments):
                target = chip ^ ((half * segments + index) * 2 + odd)
                away = (target - chip) % chips
                info.append(away // far * segments + away % far // 2)
    info = jnp.stack(info)

    mine, theirs = split_columns(info, plane_waves, transmission)
    theirs = flip(theirs, "row", 1)
    weights = coefficients(probe_pos, wave_index, wave_weight, wave_phase)
    mine = column_forward(info, mine)
    mine, theirs = lax.optimization_barrier((mine, theirs))
    spectrum = row_forward(info, mine, theirs)

    def rows_of(odd):
        return np.concatenate(
            [
                chip_rows * away - HALF + np.arange(chip_rows + WINDOW)
                for away in range(odd, far, 2)
            ]
        )

    def later(value, *before):
        return lax.optimization_barrier((value,) + before)

    def over_waves(pieces):
        return [(pieces[0], 0, 1)] + [
            (flip(piece, "wave", bits), 0, 1) for bits, piece in enumerate(pieces) if bits
        ]

    common = (info, probe_pos, weights)
    keep, send = inverse(
        layout, 2 * segments, False, 3, spectrum, rows_of(1), slots_of(1, (upper, lower)), *common
    )
    arrived = flip(send, "row", 1)
    spectrum, keep = later(spectrum, keep)
    keep_upper, send, rows_hi, rows_lo = inverse(
        layout, segments, True, 3 + far, spectrum, rows_of(0), slots_of(0, (upper,)), *common
    )
    arrived_upper = flip(send, "row", 1)
    pieces = spread_sum(keep, arrived, wave_count)
    (rows_hi, rows_lo), pieces = later((rows_hi, rows_lo), pieces)
    odd_terms = over_waves(pieces)
    keep_lower, send = column_inverse(
        layout, (rows_hi, rows_lo), slots_of(0, (lower,)), *common
    )
    arrived_lower = flip(send, "row", 1)
    pieces = spread_sum(keep_upper, arrived_upper, wave_count)
    odd_arrays, pieces = later([term[0] for term in odd_terms], pieces)
    odd_terms = [(array, 0, 1) for array in odd_arrays]
    upper_terms = over_waves(pieces)
    near = flip(sum_of(odd_terms, False), "row", 2)
    lower_terms = over_waves(spread_sum(keep_lower, arrived_lower, wave_count))

    bit = row_count // 2
    send = sum_of(upper_terms + [(near, 0, 2)], False)
    terms = lower_terms + [(near, 1, 2), (flip(send, "row", bit), 0, 1)]
    while bit > 4:
        bit //= 2
        stay, send = sum_of(terms, True)
        terms = [(stay, 0, 1), (flip(send, "row", bit), 0, 1)]
    total_waves = plane_waves.shape[1] * wave_count
    power = power_of(terms, 1.0 / (WINDOW * WINDOW * total_waves))
    return lax.all_to_all(power, "wave", split_axis=1, concat_axis=0, tiled=True)


def solution(mesh):
    return jax.shard_map(
        shards,
        mesh=mesh,
        in_specs=(
            P(None, "wave", "row", None),
            P(None, None, "row", None),
            P("wave", None),
            P("wave"),
            P("wave"),
            P(),
        ),
        out_specs=P("row", "wave", None),
        check_vma=False,
    )
```

```python
import functools
import math

import jax
import jax.numpy as jnp
import numpy as np
from jax import lax
from jax.experimental import pallas as pl
from jax.experimental.pallas import tpu as pltpu
from jax.sharding import PartitionSpec as P

GRID = 2048
FACTOR = 16
WINDOW = 128
HALF = 64
FRESNEL = 0.1

BAND = math.isqrt(GRID * GRID // 9)
FOLD = GRID // 2
BLOCKS = 3
LANES = 128
PAIR = 2 * LANES
DEPTH = BLOCKS * PAIR
FREQS = BLOCKS * LANES
COL_TILES = FOLD // PAIR
CUT_STEPS = 4


def angles_of(first, second):
    return (2.0 * math.pi / GRID) * (np.outer(first, second) % GRID)


def cos_sin(first, second):
    angle = angles_of(first, second)
    return np.stack([np.cos(angle), np.sin(angle)])


def freqs(parity):
    return 2 * np.arange(FREQS) + parity


def both(function):
    return np.stack([function(freqs(0)), function(freqs(1))])


def halves_of(value):
    high = value.astype(jnp.bfloat16)
    return high, (value - high.astype(jnp.float32)).astype(jnp.bfloat16)


def dot3(left, right):
    def term(first, second):
        return jnp.dot(first, second, preferred_element_type=jnp.float32)

    return term(left[0], right[0]) + term(left[0], right[1]) + term(left[1], right[0])


def paired(values):
    blocks = values.reshape(values.shape[:-1] + (-1, LANES))
    return np.moveaxis(blocks, 0, -2).reshape(values.shape[1:-1] + (-1,))


def table_halves(table):
    high = table.astype(jnp.bfloat16)
    low = (table - high.astype(np.float64)).astype(jnp.bfloat16)
    return jnp.asarray(high), jnp.asarray(low)


def put(refs, place, value):
    high, low = halves_of(value)
    refs[0][place] = high
    refs[1][place] = low


def sign_of(info_ref):
    return 1.0 - 2.0 * info_ref[2].astype(jnp.float32)


def split_kernel(info_ref, wave_ref, trans_ref, mine_ref, theirs_ref):
    wave_re, wave_im = wave_ref[0, 0], wave_ref[1, 0]
    trans_re, trans_im = trans_ref[0, 0], trans_ref[0, 1]
    sign = sign_of(info_ref)
    for part, value in enumerate(
        (wave_re * trans_re - wave_im * trans_im, wave_re * trans_im + wave_im * trans_re)
    ):
        low, high = value[:, :FOLD], sign * value[:, FOLD:]
        mine_ref[part] = low + high
        theirs_ref[part] = low - high


def split_columns(info, plane_waves, transmission):
    rows = plane_waves.shape[2]
    step = 32
    out = jax.ShapeDtypeStruct((2, rows, FOLD), jnp.float32)
    out_spec = pl.BlockSpec((2, step, FOLD), lambda i, *_: (0, i, 0))
    return pl.pallas_call(
        split_kernel,
        out_shape=(out, out),
        grid_spec=pltpu.PrefetchScalarGridSpec(
            num_scalar_prefetch=1,
            grid=(rows // step,),
            in_specs=[
                pl.BlockSpec((2, 1, step, GRID), lambda i, *_: (0, 0, i, 0)),
                pl.BlockSpec((1, 2, step, GRID), lambda i, *_: (0, 0, i, 0)),
            ],
            out_specs=(out_spec, out_spec),
        ),
        cost_estimate=pl.CostEstimate(
            flops=20 * rows * GRID, bytes_accessed=24 * rows * GRID, transcendentals=0
        ),
        name="split_columns",
    )(info, plane_waves, transmission)


def column_forward_table():
    return table_halves(both(lambda freq: paired(cos_sin(np.arange(FOLD), freq))))


def column_forward_kernel(info_ref, field_ref, table_hi, table_lo, out_ref, *field):
    rows = field_ref.shape[1]

    @pl.when(pl.program_id(0) == 0)
    def _():
        for part in (0, 1):
            put(field, slice(part * rows, (part + 1) * rows), field_ref[part])

    result = dot3((field[0][...], field[1][...]), (table_hi[0], table_lo[0]))
    for part in (0, 1):
        out_ref[part] = result[part * rows : (part + 1) * rows]


def column_forward(info, field):
    rows = field.shape[1]
    table = column_forward_table()
    table_spec = pl.BlockSpec((1, FOLD, PAIR), lambda j, info: (info[2], 0, j))
    return pl.pallas_call(
        column_forward_kernel,
        out_shape=jax.ShapeDtypeStruct((2, rows, DEPTH), jnp.float32),
        grid_spec=pltpu.PrefetchScalarGridSpec(
            num_scalar_prefetch=1,
            grid=(BLOCKS,),
            in_specs=[
                pl.BlockSpec((2, rows, FOLD), lambda j, *_: (0, 0, 0)),
                table_spec,
                table_spec,
            ],
            out_specs=pl.BlockSpec((2, rows, PAIR), lambda j, *_: (0, 0, j)),
            scratch_shapes=[pltpu.VMEM((2 * rows, FOLD), jnp.bfloat16)] * 2,
        ),
        cost_estimate=pl.CostEstimate(
            flops=12 * rows * FOLD * DEPTH,
            bytes_accessed=8 * rows * (FOLD + DEPTH),
            transcendentals=0,
        ),
        name="column_forward",
    )(info, field, *table)


def row_forward_kernel(
    info_ref, mine_ref, theirs_ref, col_hi, col_lo, table_hi, table_lo, down_ref, along_ref,
    out_hi, out_lo, field_hi, field_lo, theirs_hi, theirs_lo,
):
    rows = mine_ref.shape[1]
    field = (field_hi, field_lo)
    core = info_ref[2]

    @pl.when(pl.program_id(0) == 0)
    def _():
        for part in (0, 1):
            put((theirs_hi, theirs_lo), slice(part * rows, (part + 1) * rows), theirs_ref[part])

    theirs = dot3((theirs_hi[...], theirs_lo[...]), (col_hi[0], col_lo[0]))
    here = pl.ds(pl.multiple_of(core * rows, LANES), rows)
    there = pl.ds(pl.multiple_of((1 - core) * rows, LANES), rows)
    for part in (0, 1):
        cols = slice(part * PAIR, (part + 1) * PAIR)
        put(field, (here, cols), mine_ref[part])
        put(field, (there, cols), theirs[part * rows : (part + 1) * rows])
    cos_x, sin_x, square_x = (along_ref[0, i : i + 1] for i in range(3))
    outs = (out_hi, out_lo)

    def blocks(parity, count):
        first = parity * DEPTH
        part = slice(first, first + count * PAIR)
        result = dot3((table_hi[part], table_lo[part]), (field_hi[...], field_lo[...]))
        for block in range(count):
            freq = slice((parity * BLOCKS + block) * LANES, (parity * BLOCKS + block + 1) * LANES)
            cos_y, sin_y, square_y = (down_ref[freq, i : i + 1] for i in range(3))
            inside = 9.0 * (square_y + square_x) <= GRID * GRID
            prop_re = jnp.where(inside, cos_y * cos_x - sin_y * sin_x, 0.0)
            prop_im = jnp.where(inside, -(sin_y * cos_x + cos_y * sin_x), 0.0)
            for kind in (0, 1):
                start = block * PAIR + kind * LANES
                place = slice(first + start, first + start + LANES)
                for side in (0, 1):
                    cols = slice(side * LANES, (side + 1) * LANES)
                    real_part = result[start : start + LANES, cols]
                    imag_part = result[start : start + LANES, slice(PAIR + side * LANES, PAIR + (side + 1) * LANES)]
                    put(outs, (0, place, cols), prop_re * real_part - prop_im * imag_part)
                    put(outs, (1, place, cols), prop_re * imag_part + prop_im * real_part)

    last = pl.program_id(0) == BLOCKS - 1
    for parity in (0, 1):
        pl.when(last)(functools.partial(blocks, parity, BLOCKS - 1))
        pl.when(jnp.logical_not(last))(functools.partial(blocks, parity, BLOCKS))


def axis_factors(freq):
    angle = freq.astype(np.float64) ** 2 * (math.pi * FRESNEL / GRID)
    weight = np.where(freq == 0, 1.0, 2.0) / GRID
    return [np.cos(angle) * weight, np.sin(angle) * weight, freq.astype(np.float64) ** 2]


def row_forward(info, mine, theirs):
    rows = mine.shape[1]
    all_freqs = np.concatenate([freqs(0), freqs(1)])
    table = table_halves(paired(cos_sin(np.arange(2 * rows), all_freqs)).T)
    down = np.stack(axis_factors(all_freqs)).T.astype(np.float32)
    along = both(lambda freq: np.stack(axis_factors(freq))).astype(np.float32)
    tile = pl.BlockSpec((2, rows, PAIR), lambda j, *_: (0, 0, j))
    out = jax.ShapeDtypeStruct((2, 2 * DEPTH, DEPTH), jnp.bfloat16)
    out_spec = pl.BlockSpec((2, 2 * DEPTH, PAIR), lambda j, *_: (0, 0, j))
    table_spec = pl.BlockSpec(
        (2 * DEPTH, 2 * rows), lambda j, *_: (0, 0), pipeline_mode=pl.Buffered(1)
    )
    col_spec = pl.BlockSpec((1, FOLD, PAIR), lambda j, info: (info[2], 0, j))
    return pl.pallas_call(
        row_forward_kernel,
        out_shape=(out, out),
        grid_spec=pltpu.PrefetchScalarGridSpec(
            num_scalar_prefetch=1,
            grid=(BLOCKS,),
            in_specs=[
                tile,
                pl.BlockSpec(
                    (2, rows, FOLD), lambda j, *_: (0, 0, 0), pipeline_mode=pl.Buffered(1)
                ),
                col_spec,
                col_spec,
                table_spec,
                table_spec,
                pl.BlockSpec(down.shape, lambda j, *_: (0, 0)),
                pl.BlockSpec((1, 3, LANES), lambda j, info: (info[2], 0, j)),
            ],
            out_specs=(out_spec, out_spec),
            scratch_shapes=[pltpu.VMEM((2 * rows, 2 * PAIR), jnp.bfloat16)] * 2
            + [pltpu.VMEM((2 * rows, FOLD), jnp.bfloat16)] * 2,
        ),
        cost_estimate=pl.CostEstimate(
            flops=48 * rows * DEPTH * DEPTH,
            bytes_accessed=16 * rows * DEPTH + 16 * DEPTH * DEPTH,
            transcendentals=0,
        ),
        name="row_forward",
    )(
        info, mine, theirs, *column_forward_table(), *table, jnp.asarray(down),
        jnp.asarray(along),
    )


def cut_slots(layout, first, info_ref, slot_ref, pos_ref, weight_ref, field, outs):
    chip_rows, waves, own, _ = layout
    height = chip_rows + WINDOW
    lane = lax.broadcasted_iota(jnp.int32, (WINDOW, WINDOW), 1)
    row_rank, wave_rank = info_ref[0], info_ref[1]

    def one(index, out_ref, place):
        target = row_rank ^ slot_ref[0, index]
        probe = (target * waves + (wave_rank ^ slot_ref[1, index])) * own + slot_ref[2, index]
        row = slot_ref[3, index] * height + lax.rem(pos_ref[probe, 0], chip_rows)
        start = lax.rem(pos_ref[probe, 1] + (GRID - HALF), GRID)
        col = lax.rem(start, FOLD)
        turned = jnp.where(start >= FOLD, sign_of(info_ref), 1.0)
        shift = lax.rem(col, LANES)
        back = lax.rem(LANES - shift, LANES)

        def cut(part):
            sides = [
                pltpu.roll(field[part, col // LANES + side, pl.ds(row, WINDOW)], back, 1)
                for side in (0, 1)
            ]
            return jnp.where(lane < LANES - shift, sides[0], sides[1])

        real_part, imag_part = cut(0), cut(1)
        weight_re, weight_im = weight_ref[0, probe] * turned, weight_ref[1, probe] * turned
        out_ref[place, 0] = weight_re * real_part - weight_im * imag_part
        out_ref[place, 1] = weight_re * imag_part + weight_im * real_part

    keep_ref, send_ref = outs
    total = slot_ref.shape[1] // 2

    @pl.loop(0, keep_ref.shape[0])
    def _(place):
        one(total + first + place, send_ref, place)
        one(first + place, keep_ref, place)


def inverse_kernel(
    layout, cuts, base, info_ref, slot_ref, pos_ref, weight_ref,
    spec_hi, spec_lo, row_hi, row_lo, col_hi, col_lo, *refs,
):
    chip_rows, _, _, segments = layout
    height = chip_rows + WINDOW
    refs = list(refs)
    outs = refs[:2]
    exports = refs[2:4] if len(refs) > 5 else None
    rows, field = refs[-3:-1], refs[-1]
    step = pl.program_id(0)
    first = 2 * BLOCKS
    last = first + 2 * cuts * COL_TILES

    def row_part(depth):
        part = step // BLOCKS
        place = pl.multiple_of(step % BLOCKS * PAIR, PAIR)
        cols = pl.ds(place, PAIR)
        count = row_hi.shape[0]
        sums = []
        for parity in (0, 1):
            freq = slice(parity * DEPTH, parity * DEPTH + depth * PAIR)
            sums.append(
                dot3((row_hi[:, freq], row_lo[:, freq]), (spec_hi[0, freq], spec_lo[0, freq]))
            )
        put(rows, (part, slice(0, count), cols), sums[0] + sums[1])
        put(rows, (part, slice(count, 2 * count), cols), sums[0] - sums[1])
        if exports is not None:
            for index in range(segments):
                start = pl.multiple_of(info_ref[base + cuts + index] * height, LANES)
                for export, source in zip(exports, rows):
                    export[0, index * height : (index + 1) * height] = source[
                        part, pl.ds(start, height), cols
                    ]

    zero_blocks = step % BLOCKS == BLOCKS - 1
    pl.when((step < first) & zero_blocks)(functools.partial(row_part, BLOCKS - 1))
    pl.when((step < first) & jnp.logical_not(zero_blocks))(functools.partial(row_part, BLOCKS))

    @pl.when((step >= first) & (step < last))
    def _():
        now = step - first
        tile = now % COL_TILES
        part = now // COL_TILES % 2
        segment = now // (2 * COL_TILES)
        source = pl.ds(pl.multiple_of(info_ref[base + segment] * height, LANES), height)
        place = pl.ds(pl.multiple_of(segment * height, LANES), height)
        value = dot3((rows[0][part, source], rows[1][part, source]), (col_hi[0], col_lo[0]))
        field[part, 2 * tile, place] = value[:, :LANES]
        field[part, 2 * tile + 1, place] = value[:, LANES:]

        @pl.when(tile == 0)
        def _():
            field[part, 2 * COL_TILES, place] = value[:, :LANES] * sign_of(info_ref)

    @pl.when(step >= last)
    def _():
        begin = (step - last) * outs[0].shape[0]
        cut_slots(layout, begin, info_ref, slot_ref, pos_ref, weight_ref, field, outs)


def window_spec(count, last):
    return pl.BlockSpec(
        (count // CUT_STEPS, 2, WINDOW, WINDOW),
        lambda i, *_: (jnp.maximum(i - last, 0), 0, 0, 0),
    )


def column_table():
    return table_halves(both(lambda freq: paired(cos_sin(np.arange(FOLD), freq)).T))


def inverse(layout, cuts, export, base, spectrum, row_list, slots, info, positions, weights):
    chip_rows, _, _, segments = layout
    height = chip_rows + WINDOW
    count = slots.shape[1] // 2
    tall = len(row_list)
    row_table = table_halves(paired(cos_sin(row_list, np.concatenate([freqs(0), freqs(1)]))))
    first = 2 * BLOCKS
    last = first + 2 * cuts * COL_TILES

    def spec_map(i, *_):
        i = jnp.minimum(i, first - 1)
        return i // BLOCKS, 0, i % BLOCKS

    def col_map(i, info, *_):
        return info[2], 0, (jnp.clip(i, first, last - 1) - first) % COL_TILES

    spec = pl.BlockSpec((1, 2 * DEPTH, PAIR), spec_map)
    row_spec = pl.BlockSpec(
        (tall, 2 * DEPTH), lambda i, *_: (0, 0), pipeline_mode=pl.Buffered(1)
    )
    col_spec = pl.BlockSpec((1, DEPTH, PAIR), col_map)
    shapes = [jax.ShapeDtypeStruct((count, 2, WINDOW, WINDOW), jnp.float32)] * 2
    specs = [window_spec(count, last)] * 2
    if export:
        shapes += [jax.ShapeDtypeStruct((2, segments * height, DEPTH), jnp.bfloat16)] * 2
        specs += [pl.BlockSpec((1, segments * height, PAIR), spec_map)] * 2
    return pl.pallas_call(
        functools.partial(inverse_kernel, layout, cuts, base),
        out_shape=shapes,
        grid_spec=pltpu.PrefetchScalarGridSpec(
            num_scalar_prefetch=4,
            grid=(last + CUT_STEPS,),
            in_specs=[spec, spec, row_spec, row_spec, col_spec, col_spec],
            out_specs=specs,
            scratch_shapes=[
                pltpu.VMEM((2, 2 * tall, DEPTH), jnp.bfloat16),
                pltpu.VMEM((2, 2 * tall, DEPTH), jnp.bfloat16),
                pltpu.VMEM((2, 2 * COL_TILES + 1, cuts * height, WINDOW), jnp.float32),
            ],
        ),
        cost_estimate=pl.CostEstimate(
            flops=24 * tall * DEPTH * DEPTH + 12 * cuts * height * DEPTH * FOLD,
            bytes_accessed=16 * DEPTH * DEPTH + 16 * tall * DEPTH,
            transcendentals=0,
        ),
        name="inverse",
    )(
        info, jnp.asarray(slots), positions, weights, *spectrum, *row_table, *column_table(),
    )


def column_inverse_kernel(
    layout, info_ref, slot_ref, pos_ref, weight_ref,
    rows_hi, rows_lo, table_hi, table_lo, keep_ref, send_ref, field,
):
    chip_rows, _, _, segments = layout
    height = chip_rows + WINDOW
    step = pl.program_id(0)
    tile = step % COL_TILES

    @pl.when(step < 2 * segments * COL_TILES)
    def _():
        part = step // COL_TILES % 2
        start = pl.multiple_of(step // (2 * COL_TILES) * height, LANES)
        rows = pl.ds(start, height)
        value = dot3((rows_hi[0], rows_lo[0]), (table_hi[0], table_lo[0]))
        field[part, 2 * tile, rows] = value[:, :LANES]
        field[part, 2 * tile + 1, rows] = value[:, LANES:]

        @pl.when(tile == 0)
        def _():
            field[part, 2 * COL_TILES, rows] = value[:, :LANES] * sign_of(info_ref)

    @pl.when(step >= 2 * segments * COL_TILES)
    def _():
        begin = (step - 2 * segments * COL_TILES) * keep_ref.shape[0]
        outs = (keep_ref, send_ref)
        cut_slots(layout, begin, info_ref, slot_ref, pos_ref, weight_ref, field, outs)


def column_inverse(layout, rows, slots, info, positions, weights):
    chip_rows, _, _, segments = layout
    count = slots.shape[1] // 2
    height = chip_rows + WINDOW
    table = column_table()
    last = 2 * segments * COL_TILES - 1

    def rows_map(i, info, *_):
        i = jnp.minimum(i, last)
        return i // COL_TILES % 2, i // (2 * COL_TILES), 0

    rows_spec = pl.BlockSpec((1, height, DEPTH), rows_map)
    table_spec = pl.BlockSpec(
        (1, DEPTH, PAIR), lambda i, info, *_: (info[2], 0, jnp.minimum(i, last) % COL_TILES)
    )
    out = jax.ShapeDtypeStruct((count, 2, WINDOW, WINDOW), jnp.float32)
    out_spec = window_spec(count, last + 1)
    return pl.pallas_call(
        functools.partial(column_inverse_kernel, layout),
        out_shape=(out, out),
        grid_spec=pltpu.PrefetchScalarGridSpec(
            num_scalar_prefetch=4,
            grid=(last + 1 + CUT_STEPS,),
            in_specs=[
                rows_spec,
                rows_spec,
                table_spec,
                table_spec,
            ],
            out_specs=(out_spec, out_spec),
            scratch_shapes=[
                pltpu.VMEM((2, 2 * COL_TILES + 1, segments * height, WINDOW), jnp.float32)
            ],
        ),
        cost_estimate=pl.CostEstimate(
            flops=12 * segments * height * DEPTH * FOLD,
            bytes_accessed=8 * segments * height * DEPTH + 16 * count * WINDOW * WINDOW,
            transcendentals=0,
        ),
        name="column_inverse",
    )(
        info, jnp.asarray(slots), positions, weights, *rows, *table,
    )


def sum_kernel(count, halve, *refs):
    total = refs[0][0]
    for ref in refs[1:count]:
        total += ref[0]
    if halve:
        refs[count][...] = total[0]
        refs[count + 1][...] = total[1]
    else:
        refs[count][...] = total


def sum_of(terms, halve):
    tail = terms[0][0].shape[1:]
    zeros = (0,) * len(tail)
    count = terms[0][0].shape[0] // terms[0][2] // (2 if halve else 1)
    step = max(1, count // 2)
    specs, arrays = [], []
    for array, part, parts in terms:
        if halve:
            arrays.append(array.reshape((parts, 2, count) + tail))
            specs.append(
                pl.BlockSpec((1, 2, step) + tail, lambda i, part=part: (part, 0, i) + zeros)
            )
        else:
            arrays.append(array.reshape((parts, count) + tail))
            specs.append(
                pl.BlockSpec((1, step) + tail, lambda i, part=part: (part, i) + zeros)
            )
    out = jax.ShapeDtypeStruct((count,) + tail, jnp.float32)
    out_spec = pl.BlockSpec((step,) + tail, lambda i: (i,) + zeros)
    size = count * 4 * math.prod(tail) * (2 if halve else 1)
    return pl.pallas_call(
        functools.partial(sum_kernel, len(terms), halve),
        out_shape=(out, out) if halve else out,
        grid=(count // step,),
        in_specs=specs,
        out_specs=(out_spec, out_spec) if halve else out_spec,
        cost_estimate=pl.CostEstimate(
            flops=size, bytes_accessed=(len(terms) + 1) * size, transcendentals=0
        ),
        name="sum_of",
    )(*arrays)


def spread_kernel(first_ref, second_ref, *outs):
    for index, out_ref in enumerate(outs):
        out_ref[...] = first_ref[index] + second_ref[index]


def spread_sum(first, second, count):
    tail = first.shape[1:]
    zeros = (0,) * len(tail)
    size = first.shape[0] // count
    step = max(1, size // 2)
    out = jax.ShapeDtypeStruct((size,) + tail, jnp.float32)
    spec = pl.BlockSpec((count, step) + tail, lambda i: (0, i) + zeros)
    return pl.pallas_call(
        spread_kernel,
        out_shape=[out] * count,
        grid=(size // step,),
        in_specs=[spec, spec],
        out_specs=[pl.BlockSpec((step,) + tail, lambda i: (i,) + zeros)] * count,
        cost_estimate=pl.CostEstimate(
            flops=first.size, bytes_accessed=12 * first.size, transcendentals=0
        ),
        name="spread_sum",
    )(*(value.reshape((count, size) + tail) for value in (first, second)))


def power_kernel(count, scale, *refs):
    terms, (down_ref, along_ref, out_ref) = refs[:count], refs[count:]
    down, along = halves_of(down_ref[...]), halves_of(along_ref[...])
    total = terms[0][0, 0]
    for term in terms[1:]:
        total += term[0, 0]
    value = dot3(down, halves_of(jnp.concatenate([total[0], total[1]], axis=1)))
    cos_part, sin_part = value[:WINDOW], value[WINDOW:]
    real_part = cos_part[:, :WINDOW] + sin_part[:, WINDOW:]
    imag_part = cos_part[:, WINDOW:] - sin_part[:, :WINDOW]
    value = dot3(halves_of(jnp.concatenate([real_part, imag_part])), along)
    real_part = value[:WINDOW, :WINDOW] + value[WINDOW:, WINDOW:]
    imag_part = value[WINDOW:, :WINDOW] - value[:WINDOW, WINDOW:]
    out_ref[0] = (real_part * real_part + imag_part * imag_part) * scale


def power_of(terms, scale):
    tail = terms[0][0].shape[1:]
    count = terms[0][0].shape[0] // terms[0][2]
    table = cos_sin(np.arange(WINDOW), FACTOR * np.arange(WINDOW)).astype(np.float32)
    down, along = np.concatenate(list(table)), np.concatenate(list(table), axis=1)
    return pl.pallas_call(
        functools.partial(power_kernel, len(terms), scale),
        out_shape=jax.ShapeDtypeStruct((count, WINDOW, WINDOW), jnp.float32),
        grid=(count,),
        in_specs=[
            pl.BlockSpec((1, 1) + tail, lambda i, part=part: (part, i, 0, 0, 0))
            for _, part, _ in terms
        ]
        + [
            pl.BlockSpec(down.shape, lambda i: (0, 0)),
            pl.BlockSpec(along.shape, lambda i: (0, 0)),
        ],
        out_specs=pl.BlockSpec((1, WINDOW, WINDOW), lambda i: (i, 0, 0)),
        name="power_of",
    )(
        *(array.reshape((parts, count) + tail) for array, _, parts in terms),
        jnp.asarray(down), jnp.asarray(along),
    )


def coefficients(positions, wave_index, wave_weight, wave_phase):
    turns = (
        FACTOR * (positions[:, 0] * wave_index[0, 0] + positions[:, 1] * wave_index[0, 1])
    ) % GRID
    angles = wave_phase[0] - turns.astype(jnp.float32) * (2.0 * math.pi / GRID)
    return wave_weight[0] * jnp.stack([jnp.cos(angles), jnp.sin(angles)])


def flip(block, axis, bit):
    count = lax.axis_size(axis)
    return lax.ppermute(block, axis, [(i, i ^ bit) for i in range(count)])


def shards(plane_waves, transmission, wave_index, wave_weight, wave_phase, probe_pos):
    rows_here = plane_waves.shape[2]
    row_count = lax.axis_size("row")
    wave_count = lax.axis_size("wave")
    row_rank = lax.axis_index("row")
    wave_rank = lax.axis_index("wave")
    core = row_rank % 2
    chip_rows = 2 * rows_here
    chips = row_count // 2
    far = chips // 2
    own = probe_pos.shape[0] // (row_count * wave_count)

    segments = far // 2
    layout = (chip_rows, wave_count, own, segments)

    def slots_of(odd, halves):
        slots = []
        for core_bit in (0, 1):
            for wave in range(wave_count):
                for at, half in enumerate(halves):
                    for index in range(segments):
                        row = ((half * segments + index) * 2 + odd) * 2 + core_bit
                        where = at * segments + index
                        slots += [(row, wave, probe, where) for probe in range(own)]
        return np.array(slots, np.int32).T

    upper, lower = 1, 0
    chip = row_rank // 2
    info = [row_rank, wave_rank, core]
    for odd in (1, 0):
        for half in (upper, lower):
            for index in range(segments):
                target = chip ^ ((half * segments + index) * 2 + odd)
                away = (target - chip) % chips
                info.append(away // far * segments + away % far // 2)
    info = jnp.stack(info)

    mine, theirs = split_columns(info, plane_waves, transmission)
    theirs = flip(theirs, "row", 1)
    weights = coefficients(probe_pos, wave_index, wave_weight, wave_phase)
    mine = column_forward(info, mine)
    mine, theirs = lax.optimization_barrier((mine, theirs))
    spectrum = row_forward(info, mine, theirs)

    def rows_of(odd):
        return np.concatenate(
            [
                chip_rows * away - HALF + np.arange(chip_rows + WINDOW)
                for away in range(odd, far, 2)
            ]
        )

    def later(value, *before):
        return lax.optimization_barrier((value,) + before)

    def over_waves(pieces):
        return [(pieces[0], 0, 1)] + [
            (flip(piece, "wave", bits), 0, 1) for bits, piece in enumerate(pieces) if bits
        ]

    common = (info, probe_pos, weights)
    keep, send = inverse(
        layout, 2 * segments, False, 3, spectrum, rows_of(1), slots_of(1, (upper, lower)), *common
    )
    arrived = flip(send, "row", 1)
    spectrum, keep = later(spectrum, keep)
    keep_upper, send, rows_hi, rows_lo = inverse(
        layout, segments, True, 3 + far, spectrum, rows_of(0), slots_of(0, (upper,)), *common
    )
    arrived_upper = flip(send, "row", 1)
    pieces = spread_sum(keep, arrived, wave_count)
    (rows_hi, rows_lo), pieces = later((rows_hi, rows_lo), pieces)
    odd_terms = over_waves(pieces)
    keep_lower, send = column_inverse(
        layout, (rows_hi, rows_lo), slots_of(0, (lower,)), *common
    )
    arrived_lower = flip(send, "row", 1)
    pieces = spread_sum(keep_upper, arrived_upper, wave_count)
    odd_arrays, pieces = later([term[0] for term in odd_terms], pieces)
    odd_terms = [(array, 0, 1) for array in odd_arrays]
    upper_terms = over_waves(pieces)
    near = flip(sum_of(odd_terms, False), "row", 2)
    pieces = spread_sum(keep_lower, arrived_lower, wave_count)
    arrays, pieces = later([term[0] for term in upper_terms], pieces)
    upper_terms = [(array, 0, 1) for array in arrays]
    lower_terms = over_waves(pieces)

    bit = row_count // 2
    send = sum_of(upper_terms + [(near, 0, 2)], False)
    terms = lower_terms + [(near, 1, 2), (flip(send, "row", bit), 0, 1)]
    while bit > 4:
        bit //= 2
        stay, send = sum_of(terms, True)
        terms = [(stay, 0, 1), (flip(send, "row", bit), 0, 1)]
    total_waves = plane_waves.shape[1] * wave_count
    power = power_of(terms, 1.0 / (WINDOW * WINDOW * total_waves))
    return lax.all_to_all(power, "wave", split_axis=1, concat_axis=0, tiled=True)


def solution(mesh):
    return jax.shard_map(
        shards,
        mesh=mesh,
        in_specs=(
            P(None, "wave", "row", None),
            P(None, None, "row", None),
            P("wave", None),
            P("wave"),
            P("wave"),
            P(),
        ),
        out_specs=P("row", "wave", None),
        check_vma=False,
    )
```

```python
import functools
import math

import jax
import jax.numpy as jnp
import numpy as np
from jax import lax
from jax.experimental import pallas as pl
from jax.experimental.pallas import tpu as pltpu
from jax.sharding import PartitionSpec as P

GRID = 2048
FACTOR = 16
WINDOW = 128
HALF = 64
FRESNEL = 0.1

BAND = math.isqrt(GRID * GRID // 9)
FOLD = GRID // 2
BLOCKS = 3
LANES = 128
PAIR = 2 * LANES
DEPTH = BLOCKS * PAIR
FREQS = BLOCKS * LANES
COL_TILES = FOLD // PAIR
CUT_STEPS = 4
VMEM_BYTES = 67043328


def angles_of(first, second):
    return (2.0 * math.pi / GRID) * (np.outer(first, second) % GRID)


def cos_sin(first, second):
    angle = angles_of(first, second)
    return np.stack([np.cos(angle), np.sin(angle)])


def freqs(parity):
    return 2 * np.arange(FREQS) + parity


def both(function):
    return np.stack([function(freqs(0)), function(freqs(1))])


def halves_of(value):
    high = value.astype(jnp.bfloat16)
    return high, (value - high.astype(jnp.float32)).astype(jnp.bfloat16)


def dot3(left, right):
    def term(first, second):
        return jnp.dot(first, second, preferred_element_type=jnp.float32)

    return term(left[0], right[0]) + term(left[0], right[1]) + term(left[1], right[0])


def paired(values):
    blocks = values.reshape(values.shape[:-1] + (-1, LANES))
    return np.moveaxis(blocks, 0, -2).reshape(values.shape[1:-1] + (-1,))


def table_halves(table):
    high = table.astype(jnp.bfloat16)
    low = (table - high.astype(np.float64)).astype(jnp.bfloat16)
    return jnp.asarray(high), jnp.asarray(low)


def put(refs, place, value):
    high, low = halves_of(value)
    refs[0][place] = high
    refs[1][place] = low


def sign_of(info_ref):
    return 1.0 - 2.0 * info_ref[2].astype(jnp.float32)


def split_kernel(info_ref, wave_ref, trans_ref, mine_ref, theirs_ref):
    wave_re, wave_im = wave_ref[0, 0], wave_ref[1, 0]
    trans_re, trans_im = trans_ref[0, 0], trans_ref[0, 1]
    sign = sign_of(info_ref)
    for part, value in enumerate(
        (wave_re * trans_re - wave_im * trans_im, wave_re * trans_im + wave_im * trans_re)
    ):
        low, high = value[:, :FOLD], sign * value[:, FOLD:]
        mine_ref[part] = low + high
        theirs_ref[part] = low - high


def split_columns(info, plane_waves, transmission):
    rows = plane_waves.shape[2]
    step = 32
    out = jax.ShapeDtypeStruct((2, rows, FOLD), jnp.float32)
    out_spec = pl.BlockSpec((2, step, FOLD), lambda i, *_: (0, i, 0))
    return pl.pallas_call(
        split_kernel,
        out_shape=(out, out),
        grid_spec=pltpu.PrefetchScalarGridSpec(
            num_scalar_prefetch=1,
            grid=(rows // step,),
            in_specs=[
                pl.BlockSpec((2, 1, step, GRID), lambda i, *_: (0, 0, i, 0)),
                pl.BlockSpec((1, 2, step, GRID), lambda i, *_: (0, 0, i, 0)),
            ],
            out_specs=(out_spec, out_spec),
        ),
        cost_estimate=pl.CostEstimate(
            flops=20 * rows * GRID, bytes_accessed=24 * rows * GRID, transcendentals=0
        ),
        name="split_columns",
    )(info, plane_waves, transmission)


def column_forward_table():
    return table_halves(both(lambda freq: paired(cos_sin(np.arange(FOLD), freq))))


def column_forward_kernel(info_ref, field_ref, table_hi, table_lo, out_ref, *field):
    rows = field_ref.shape[1]

    @pl.when(pl.program_id(0) == 0)
    def _():
        for part in (0, 1):
            put(field, slice(part * rows, (part + 1) * rows), field_ref[part])

    result = dot3((field[0][...], field[1][...]), (table_hi[0], table_lo[0]))
    for part in (0, 1):
        out_ref[part] = result[part * rows : (part + 1) * rows]


def column_forward(info, field):
    rows = field.shape[1]
    table = column_forward_table()
    table_spec = pl.BlockSpec((1, FOLD, PAIR), lambda j, info: (info[2], 0, j))
    return pl.pallas_call(
        column_forward_kernel,
        out_shape=jax.ShapeDtypeStruct((2, rows, DEPTH), jnp.float32),
        grid_spec=pltpu.PrefetchScalarGridSpec(
            num_scalar_prefetch=1,
            grid=(BLOCKS,),
            in_specs=[
                pl.BlockSpec((2, rows, FOLD), lambda j, *_: (0, 0, 0)),
                table_spec,
                table_spec,
            ],
            out_specs=pl.BlockSpec((2, rows, PAIR), lambda j, *_: (0, 0, j)),
            scratch_shapes=[pltpu.VMEM((2 * rows, FOLD), jnp.bfloat16)] * 2,
        ),
        cost_estimate=pl.CostEstimate(
            flops=12 * rows * FOLD * DEPTH,
            bytes_accessed=8 * rows * (FOLD + DEPTH),
            transcendentals=0,
        ),
        compiler_params=pltpu.CompilerParams(vmem_limit_bytes=VMEM_BYTES),
        name="column_forward",
    )(info, field, *table)


def row_forward_kernel(
    info_ref, mine_ref, theirs_ref, col_hi, col_lo, table_hi, table_lo, down_ref, along_ref,
    out_hi, out_lo, field_hi, field_lo, theirs_hi, theirs_lo,
):
    rows = mine_ref.shape[1]
    field = (field_hi, field_lo)
    core = info_ref[2]

    @pl.when(pl.program_id(0) == 0)
    def _():
        for part in (0, 1):
            put((theirs_hi, theirs_lo), slice(part * rows, (part + 1) * rows), theirs_ref[part])

    theirs = dot3((theirs_hi[...], theirs_lo[...]), (col_hi[0], col_lo[0]))
    here = pl.ds(pl.multiple_of(core * rows, LANES), rows)
    there = pl.ds(pl.multiple_of((1 - core) * rows, LANES), rows)
    for part in (0, 1):
        cols = slice(part * PAIR, (part + 1) * PAIR)
        put(field, (here, cols), mine_ref[part])
        put(field, (there, cols), theirs[part * rows : (part + 1) * rows])
    cos_x, sin_x, square_x = (along_ref[0, i : i + 1] for i in range(3))
    outs = (out_hi, out_lo)

    def blocks(parity, count):
        first = parity * DEPTH
        part = slice(first, first + count * PAIR)
        result = dot3((table_hi[part], table_lo[part]), (field_hi[...], field_lo[...]))
        for block in range(count):
            freq = slice((parity * BLOCKS + block) * LANES, (parity * BLOCKS + block + 1) * LANES)
            cos_y, sin_y, square_y = (down_ref[freq, i : i + 1] for i in range(3))
            inside = 9.0 * (square_y + square_x) <= GRID * GRID
            prop_re = jnp.where(inside, cos_y * cos_x - sin_y * sin_x, 0.0)
            prop_im = jnp.where(inside, -(sin_y * cos_x + cos_y * sin_x), 0.0)
            for kind in (0, 1):
                start = block * PAIR + kind * LANES
                place = slice(first + start, first + start + LANES)
                for side in (0, 1):
                    cols = slice(side * LANES, (side + 1) * LANES)
                    real_part = result[start : start + LANES, cols]
                    imag_part = result[start : start + LANES, slice(PAIR + side * LANES, PAIR + (side + 1) * LANES)]
                    put(outs, (0, place, cols), prop_re * real_part - prop_im * imag_part)
                    put(outs, (1, place, cols), prop_re * imag_part + prop_im * real_part)

    last = pl.program_id(0) == BLOCKS - 1
    for parity in (0, 1):
        pl.when(last)(functools.partial(blocks, parity, BLOCKS - 1))
        pl.when(jnp.logical_not(last))(functools.partial(blocks, parity, BLOCKS))


def axis_factors(freq):
    angle = freq.astype(np.float64) ** 2 * (math.pi * FRESNEL / GRID)
    weight = np.where(freq == 0, 1.0, 2.0) / GRID
    return [np.cos(angle) * weight, np.sin(angle) * weight, freq.astype(np.float64) ** 2]


def row_forward(info, mine, theirs):
    rows = mine.shape[1]
    all_freqs = np.concatenate([freqs(0), freqs(1)])
    table = table_halves(paired(cos_sin(np.arange(2 * rows), all_freqs)).T)
    down = np.stack(axis_factors(all_freqs)).T.astype(np.float32)
    along = both(lambda freq: np.stack(axis_factors(freq))).astype(np.float32)
    tile = pl.BlockSpec((2, rows, PAIR), lambda j, *_: (0, 0, j))
    out = jax.ShapeDtypeStruct((2, 2 * DEPTH, DEPTH), jnp.bfloat16)
    out_spec = pl.BlockSpec((2, 2 * DEPTH, PAIR), lambda j, *_: (0, 0, j))
    table_spec = pl.BlockSpec(
        (2 * DEPTH, 2 * rows), lambda j, *_: (0, 0), pipeline_mode=pl.Buffered(1)
    )
    col_spec = pl.BlockSpec((1, FOLD, PAIR), lambda j, info: (info[2], 0, j))
    return pl.pallas_call(
        row_forward_kernel,
        out_shape=(out, out),
        grid_spec=pltpu.PrefetchScalarGridSpec(
            num_scalar_prefetch=1,
            grid=(BLOCKS,),
            in_specs=[
                tile,
                pl.BlockSpec(
                    (2, rows, FOLD), lambda j, *_: (0, 0, 0), pipeline_mode=pl.Buffered(1)
                ),
                col_spec,
                col_spec,
                table_spec,
                table_spec,
                pl.BlockSpec(down.shape, lambda j, *_: (0, 0)),
                pl.BlockSpec((1, 3, LANES), lambda j, info: (info[2], 0, j)),
            ],
            out_specs=(out_spec, out_spec),
            scratch_shapes=[pltpu.VMEM((2 * rows, 2 * PAIR), jnp.bfloat16)] * 2
            + [pltpu.VMEM((2 * rows, FOLD), jnp.bfloat16)] * 2,
        ),
        cost_estimate=pl.CostEstimate(
            flops=48 * rows * DEPTH * DEPTH,
            bytes_accessed=16 * rows * DEPTH + 16 * DEPTH * DEPTH,
            transcendentals=0,
        ),
        compiler_params=pltpu.CompilerParams(vmem_limit_bytes=VMEM_BYTES),
        name="row_forward",
    )(
        info, mine, theirs, *column_forward_table(), *table, jnp.asarray(down),
        jnp.asarray(along),
    )


def cut_slots(layout, first, info_ref, slot_ref, pos_ref, weight_ref, field, outs):
    chip_rows, waves, own, _ = layout
    height = chip_rows + WINDOW
    lane = lax.broadcasted_iota(jnp.int32, (WINDOW, WINDOW), 1)
    row_rank, wave_rank = info_ref[0], info_ref[1]

    def one(index, out_ref, place):
        target = row_rank ^ slot_ref[0, index]
        probe = (target * waves + (wave_rank ^ slot_ref[1, index])) * own + slot_ref[2, index]
        row = slot_ref[3, index] * height + lax.rem(pos_ref[probe, 0], chip_rows)
        start = lax.rem(pos_ref[probe, 1] + (GRID - HALF), GRID)
        col = lax.rem(start, FOLD)
        turned = jnp.where(start >= FOLD, sign_of(info_ref), 1.0)
        shift = lax.rem(col, LANES)
        back = lax.rem(LANES - shift, LANES)

        def cut(part):
            sides = [
                pltpu.roll(field[part, col // LANES + side, pl.ds(row, WINDOW)], back, 1)
                for side in (0, 1)
            ]
            return jnp.where(lane < LANES - shift, sides[0], sides[1])

        real_part, imag_part = cut(0), cut(1)
        weight_re, weight_im = weight_ref[0, probe] * turned, weight_ref[1, probe] * turned
        out_ref[place, 0] = weight_re * real_part - weight_im * imag_part
        out_ref[place, 1] = weight_re * imag_part + weight_im * real_part

    keep_ref, send_ref = outs
    total = slot_ref.shape[1] // 2

    @pl.loop(0, keep_ref.shape[0])
    def _(place):
        one(total + first + place, send_ref, place)
        one(first + place, keep_ref, place)


def inverse_kernel(
    layout, cuts, base, info_ref, slot_ref, pos_ref, weight_ref,
    spec_hi, spec_lo, row_hi, row_lo, col_hi, col_lo, *refs,
):
    chip_rows, _, _, segments = layout
    height = chip_rows + WINDOW
    refs = list(refs)
    outs = refs[:2]
    exports = refs[2:4] if len(refs) > 5 else None
    rows, field = refs[-3:-1], refs[-1]
    step = pl.program_id(0)
    first = 2 * BLOCKS
    last = first + 2 * cuts * COL_TILES

    def row_part(depth):
        part = step // BLOCKS
        place = pl.multiple_of(step % BLOCKS * PAIR, PAIR)
        cols = pl.ds(place, PAIR)
        count = row_hi.shape[0]
        sums = []
        for parity in (0, 1):
            freq = slice(parity * DEPTH, parity * DEPTH + depth * PAIR)
            sums.append(
                dot3((row_hi[:, freq], row_lo[:, freq]), (spec_hi[0, freq], spec_lo[0, freq]))
            )
        put(rows, (part, slice(0, count), cols), sums[0] + sums[1])
        put(rows, (part, slice(count, 2 * count), cols), sums[0] - sums[1])
        if exports is not None:
            for index in range(segments):
                start = pl.multiple_of(info_ref[base + cuts + index] * height, LANES)
                for export, source in zip(exports, rows):
                    export[0, index * height : (index + 1) * height] = source[
                        part, pl.ds(start, height), cols
                    ]

    zero_blocks = step % BLOCKS == BLOCKS - 1
    pl.when((step < first) & zero_blocks)(functools.partial(row_part, BLOCKS - 1))
    pl.when((step < first) & jnp.logical_not(zero_blocks))(functools.partial(row_part, BLOCKS))

    @pl.when((step >= first) & (step < last))
    def _():
        now = step - first
        tile = now % COL_TILES
        part = now // COL_TILES % 2
        segment = now // (2 * COL_TILES)
        source = pl.ds(pl.multiple_of(info_ref[base + segment] * height, LANES), height)
        place = pl.ds(pl.multiple_of(segment * height, LANES), height)
        value = dot3((rows[0][part, source], rows[1][part, source]), (col_hi[0], col_lo[0]))
        field[part, 2 * tile, place] = value[:, :LANES]
        field[part, 2 * tile + 1, place] = value[:, LANES:]

        @pl.when(tile == 0)
        def _():
            field[part, 2 * COL_TILES, place] = value[:, :LANES] * sign_of(info_ref)

    @pl.when(step >= last)
    def _():
        begin = (step - last) * outs[0].shape[0]
        cut_slots(layout, begin, info_ref, slot_ref, pos_ref, weight_ref, field, outs)


def window_spec(count, last):
    return pl.BlockSpec(
        (count // CUT_STEPS, 2, WINDOW, WINDOW),
        lambda i, *_: (jnp.maximum(i - last, 0), 0, 0, 0),
    )


def column_table():
    return table_halves(both(lambda freq: paired(cos_sin(np.arange(FOLD), freq)).T))


def inverse(layout, cuts, export, base, spectrum, row_list, slots, info, positions, weights):
    chip_rows, _, _, segments = layout
    height = chip_rows + WINDOW
    count = slots.shape[1] // 2
    tall = len(row_list)
    row_table = table_halves(paired(cos_sin(row_list, np.concatenate([freqs(0), freqs(1)]))))
    first = 2 * BLOCKS
    last = first + 2 * cuts * COL_TILES

    def spec_map(i, *_):
        i = jnp.minimum(i, first - 1)
        return i // BLOCKS, 0, i % BLOCKS

    def col_map(i, info, *_):
        return info[2], 0, (jnp.clip(i, first, last - 1) - first) % COL_TILES

    spec = pl.BlockSpec((1, 2 * DEPTH, PAIR), spec_map)
    row_spec = pl.BlockSpec(
        (tall, 2 * DEPTH), lambda i, *_: (0, 0), pipeline_mode=pl.Buffered(1)
    )
    col_spec = pl.BlockSpec((1, DEPTH, PAIR), col_map)
    shapes = [jax.ShapeDtypeStruct((count, 2, WINDOW, WINDOW), jnp.float32)] * 2
    specs = [window_spec(count, last)] * 2
    if export:
        shapes += [jax.ShapeDtypeStruct((2, segments * height, DEPTH), jnp.bfloat16)] * 2
        specs += [pl.BlockSpec((1, segments * height, PAIR), spec_map)] * 2
    return pl.pallas_call(
        functools.partial(inverse_kernel, layout, cuts, base),
        out_shape=shapes,
        grid_spec=pltpu.PrefetchScalarGridSpec(
            num_scalar_prefetch=4,
            grid=(last + CUT_STEPS,),
            in_specs=[spec, spec, row_spec, row_spec, col_spec, col_spec],
            out_specs=specs,
            scratch_shapes=[
                pltpu.VMEM((2, 2 * tall, DEPTH), jnp.bfloat16),
                pltpu.VMEM((2, 2 * tall, DEPTH), jnp.bfloat16),
                pltpu.VMEM((2, 2 * COL_TILES + 1, cuts * height, WINDOW), jnp.float32),
            ],
        ),
        cost_estimate=pl.CostEstimate(
            flops=24 * tall * DEPTH * DEPTH + 12 * cuts * height * DEPTH * FOLD,
            bytes_accessed=16 * DEPTH * DEPTH + 16 * tall * DEPTH,
            transcendentals=0,
        ),
        name="inverse",
    )(
        info, jnp.asarray(slots), positions, weights, *spectrum, *row_table, *column_table(),
    )


def column_inverse_kernel(
    layout, info_ref, slot_ref, pos_ref, weight_ref,
    rows_hi, rows_lo, table_hi, table_lo, keep_ref, send_ref, field,
):
    chip_rows, _, _, segments = layout
    height = chip_rows + WINDOW
    step = pl.program_id(0)
    tile = step % COL_TILES

    @pl.when(step < 2 * segments * COL_TILES)
    def _():
        part = step // COL_TILES % 2
        start = pl.multiple_of(step // (2 * COL_TILES) * height, LANES)
        rows = pl.ds(start, height)
        value = dot3((rows_hi[0], rows_lo[0]), (table_hi[0], table_lo[0]))
        field[part, 2 * tile, rows] = value[:, :LANES]
        field[part, 2 * tile + 1, rows] = value[:, LANES:]

        @pl.when(tile == 0)
        def _():
            field[part, 2 * COL_TILES, rows] = value[:, :LANES] * sign_of(info_ref)

    @pl.when(step >= 2 * segments * COL_TILES)
    def _():
        begin = (step - 2 * segments * COL_TILES) * keep_ref.shape[0]
        outs = (keep_ref, send_ref)
        cut_slots(layout, begin, info_ref, slot_ref, pos_ref, weight_ref, field, outs)


def column_inverse(layout, rows, slots, info, positions, weights):
    chip_rows, _, _, segments = layout
    count = slots.shape[1] // 2
    height = chip_rows + WINDOW
    table = column_table()
    last = 2 * segments * COL_TILES - 1

    def rows_map(i, info, *_):
        i = jnp.minimum(i, last)
        return i // COL_TILES % 2, i // (2 * COL_TILES), 0

    rows_spec = pl.BlockSpec((1, height, DEPTH), rows_map)
    table_spec = pl.BlockSpec(
        (1, DEPTH, PAIR), lambda i, info, *_: (info[2], 0, jnp.minimum(i, last) % COL_TILES)
    )
    out = jax.ShapeDtypeStruct((count, 2, WINDOW, WINDOW), jnp.float32)
    out_spec = window_spec(count, last + 1)
    return pl.pallas_call(
        functools.partial(column_inverse_kernel, layout),
        out_shape=(out, out),
        grid_spec=pltpu.PrefetchScalarGridSpec(
            num_scalar_prefetch=4,
            grid=(last + 1 + CUT_STEPS,),
            in_specs=[
                rows_spec,
                rows_spec,
                table_spec,
                table_spec,
            ],
            out_specs=(out_spec, out_spec),
            scratch_shapes=[
                pltpu.VMEM((2, 2 * COL_TILES + 1, segments * height, WINDOW), jnp.float32)
            ],
        ),
        cost_estimate=pl.CostEstimate(
            flops=12 * segments * height * DEPTH * FOLD,
            bytes_accessed=8 * segments * height * DEPTH + 16 * count * WINDOW * WINDOW,
            transcendentals=0,
        ),
        compiler_params=pltpu.CompilerParams(vmem_limit_bytes=VMEM_BYTES),
        name="column_inverse",
    )(
        info, jnp.asarray(slots), positions, weights, *rows, *table,
    )


def sum_kernel(count, halve, *refs):
    total = refs[0][0]
    for ref in refs[1:count]:
        total += ref[0]
    if halve:
        refs[count][...] = total[0]
        refs[count + 1][...] = total[1]
    else:
        refs[count][...] = total


def sum_of(terms, halve):
    tail = terms[0][0].shape[1:]
    zeros = (0,) * len(tail)
    count = terms[0][0].shape[0] // terms[0][2] // (2 if halve else 1)
    step = max(1, count // 2)
    specs, arrays = [], []
    for array, part, parts in terms:
        if halve:
            arrays.append(array.reshape((parts, 2, count) + tail))
            specs.append(
                pl.BlockSpec((1, 2, step) + tail, lambda i, part=part: (part, 0, i) + zeros)
            )
        else:
            arrays.append(array.reshape((parts, count) + tail))
            specs.append(
                pl.BlockSpec((1, step) + tail, lambda i, part=part: (part, i) + zeros)
            )
    out = jax.ShapeDtypeStruct((count,) + tail, jnp.float32)
    out_spec = pl.BlockSpec((step,) + tail, lambda i: (i,) + zeros)
    size = count * 4 * math.prod(tail) * (2 if halve else 1)
    return pl.pallas_call(
        functools.partial(sum_kernel, len(terms), halve),
        out_shape=(out, out) if halve else out,
        grid=(count // step,),
        in_specs=specs,
        out_specs=(out_spec, out_spec) if halve else out_spec,
        cost_estimate=pl.CostEstimate(
            flops=size, bytes_accessed=(len(terms) + 1) * size, transcendentals=0
        ),
        compiler_params=pltpu.CompilerParams(vmem_limit_bytes=VMEM_BYTES),
        name="sum_of",
    )(*arrays)


def spread_kernel(first_ref, second_ref, *outs):
    for index, out_ref in enumerate(outs):
        out_ref[...] = first_ref[index] + second_ref[index]


def spread_sum(first, second, count):
    tail = first.shape[1:]
    zeros = (0,) * len(tail)
    size = first.shape[0] // count
    step = max(1, size // 2)
    out = jax.ShapeDtypeStruct((size,) + tail, jnp.float32)
    spec = pl.BlockSpec((count, step) + tail, lambda i: (0, i) + zeros)
    return pl.pallas_call(
        spread_kernel,
        out_shape=[out] * count,
        grid=(size // step,),
        in_specs=[spec, spec],
        out_specs=[pl.BlockSpec((step,) + tail, lambda i: (i,) + zeros)] * count,
        cost_estimate=pl.CostEstimate(
            flops=first.size, bytes_accessed=12 * first.size, transcendentals=0
        ),
        compiler_params=pltpu.CompilerParams(vmem_limit_bytes=VMEM_BYTES),
        name="spread_sum",
    )(*(value.reshape((count, size) + tail) for value in (first, second)))


def power_kernel(count, scale, *refs):
    terms, (down_ref, along_ref, out_ref) = refs[:count], refs[count:]
    down, along = halves_of(down_ref[...]), halves_of(along_ref[...])
    total = terms[0][0, 0]
    for term in terms[1:]:
        total += term[0, 0]
    value = dot3(down, halves_of(jnp.concatenate([total[0], total[1]], axis=1)))
    cos_part, sin_part = value[:WINDOW], value[WINDOW:]
    real_part = cos_part[:, :WINDOW] + sin_part[:, WINDOW:]
    imag_part = cos_part[:, WINDOW:] - sin_part[:, :WINDOW]
    value = dot3(halves_of(jnp.concatenate([real_part, imag_part])), along)
    real_part = value[:WINDOW, :WINDOW] + value[WINDOW:, WINDOW:]
    imag_part = value[WINDOW:, :WINDOW] - value[:WINDOW, WINDOW:]
    out_ref[0] = (real_part * real_part + imag_part * imag_part) * scale


def power_of(terms, scale):
    tail = terms[0][0].shape[1:]
    count = terms[0][0].shape[0] // terms[0][2]
    table = cos_sin(np.arange(WINDOW), FACTOR * np.arange(WINDOW)).astype(np.float32)
    down, along = np.concatenate(list(table)), np.concatenate(list(table), axis=1)
    return pl.pallas_call(
        functools.partial(power_kernel, len(terms), scale),
        out_shape=jax.ShapeDtypeStruct((count, WINDOW, WINDOW), jnp.float32),
        grid=(count,),
        in_specs=[
            pl.BlockSpec((1, 1) + tail, lambda i, part=part: (part, i, 0, 0, 0))
            for _, part, _ in terms
        ]
        + [
            pl.BlockSpec(down.shape, lambda i: (0, 0)),
            pl.BlockSpec(along.shape, lambda i: (0, 0)),
        ],
        out_specs=pl.BlockSpec((1, WINDOW, WINDOW), lambda i: (i, 0, 0)),
        compiler_params=pltpu.CompilerParams(vmem_limit_bytes=VMEM_BYTES),
        name="power_of",
    )(
        *(array.reshape((parts, count) + tail) for array, _, parts in terms),
        jnp.asarray(down), jnp.asarray(along),
    )


def coefficients(positions, wave_index, wave_weight, wave_phase):
    turns = (
        FACTOR * (positions[:, 0] * wave_index[0, 0] + positions[:, 1] * wave_index[0, 1])
    ) % GRID
    angles = wave_phase[0] - turns.astype(jnp.float32) * (2.0 * math.pi / GRID)
    return wave_weight[0] * jnp.stack([jnp.cos(angles), jnp.sin(angles)])


def flip(block, axis, bit):
    count = lax.axis_size(axis)
    return lax.ppermute(block, axis, [(i, i ^ bit) for i in range(count)])


def shards(plane_waves, transmission, wave_index, wave_weight, wave_phase, probe_pos):
    rows_here = plane_waves.shape[2]
    row_count = lax.axis_size("row")
    wave_count = lax.axis_size("wave")
    row_rank = lax.axis_index("row")
    wave_rank = lax.axis_index("wave")
    core = row_rank % 2
    chip_rows = 2 * rows_here
    chips = row_count // 2
    far = chips // 2
    own = probe_pos.shape[0] // (row_count * wave_count)

    segments = far // 2
    layout = (chip_rows, wave_count, own, segments)

    def slots_of(odd, halves):
        slots = []
        for core_bit in (0, 1):
            for wave in range(wave_count):
                for at, half in enumerate(halves):
                    for index in range(segments):
                        row = ((half * segments + index) * 2 + odd) * 2 + core_bit
                        where = at * segments + index
                        slots += [(row, wave, probe, where) for probe in range(own)]
        return np.array(slots, np.int32).T

    upper, lower = 1, 0
    chip = row_rank // 2
    info = [row_rank, wave_rank, core]
    for odd in (1, 0):
        for half in (upper, lower):
            for index in range(segments):
                target = chip ^ ((half * segments + index) * 2 + odd)
                away = (target - chip) % chips
                info.append(away // far * segments + away % far // 2)
    info = jnp.stack(info)

    mine, theirs = split_columns(info, plane_waves, transmission)
    theirs = flip(theirs, "row", 1)
    weights = coefficients(probe_pos, wave_index, wave_weight, wave_phase)
    mine = column_forward(info, mine)
    mine, theirs = lax.optimization_barrier((mine, theirs))
    spectrum = row_forward(info, mine, theirs)

    def rows_of(odd):
        return np.concatenate(
            [
                chip_rows * away - HALF + np.arange(chip_rows + WINDOW)
                for away in range(odd, far, 2)
            ]
        )

    def later(value, *before):
        return lax.optimization_barrier((value,) + before)

    def over_waves(pieces):
        return [(pieces[0], 0, 1)] + [
            (flip(piece, "wave", bits), 0, 1) for bits, piece in enumerate(pieces) if bits
        ]

    common = (info, probe_pos, weights)
    keep, send = inverse(
        layout, 2 * segments, False, 3, spectrum, rows_of(1), slots_of(1, (upper, lower)), *common
    )
    arrived = flip(send, "row", 1)
    spectrum, keep = later(spectrum, keep)
    keep_upper, send, rows_hi, rows_lo = inverse(
        layout, segments, True, 3 + far, spectrum, rows_of(0), slots_of(0, (upper,)), *common
    )
    arrived_upper = flip(send, "row", 1)
    pieces = spread_sum(keep, arrived, wave_count)
    (rows_hi, rows_lo), pieces = later((rows_hi, rows_lo), pieces)
    odd_terms = over_waves(pieces)
    keep_lower, send = column_inverse(
        layout, (rows_hi, rows_lo), slots_of(0, (lower,)), *common
    )
    arrived_lower = flip(send, "row", 1)
    pieces = spread_sum(keep_upper, arrived_upper, wave_count)
    odd_arrays, pieces = later([term[0] for term in odd_terms], pieces)
    odd_terms = [(array, 0, 1) for array in odd_arrays]
    upper_terms = over_waves(pieces)
    near = flip(sum_of(odd_terms, False), "row", 2)
    pieces = spread_sum(keep_lower, arrived_lower, wave_count)
    arrays, pieces = later([term[0] for term in upper_terms], pieces)
    upper_terms = [(array, 0, 1) for array in arrays]
    lower_terms = over_waves(pieces)

    bit = row_count // 2
    send = sum_of(upper_terms + [(near, 0, 2)], False)
    terms = lower_terms + [(near, 1, 2), (flip(send, "row", bit), 0, 1)]
    while bit > 4:
        bit //= 2
        stay, send = sum_of(terms, True)
        terms = [(stay, 0, 1), (flip(send, "row", bit), 0, 1)]
    total_waves = plane_waves.shape[1] * wave_count
    power = power_of(terms, 1.0 / (WINDOW * WINDOW * total_waves))
    return lax.all_to_all(power, "wave", split_axis=1, concat_axis=0, tiled=True)


def solution(mesh):
    return jax.shard_map(
        shards,
        mesh=mesh,
        in_specs=(
            P(None, "wave", "row", None),
            P(None, None, "row", None),
            P("wave", None),
            P("wave"),
            P("wave"),
            P(),
        ),
        out_specs=P("row", "wave", None),
        check_vma=False,
    )
```

```python
import functools
import math

import jax
import jax.numpy as jnp
import numpy as np
from jax import lax
from jax.experimental import pallas as pl
from jax.experimental.pallas import tpu as pltpu
from jax.sharding import PartitionSpec as P


GRID = 2048
FACTOR = 16
WINDOW = 128
HALF = 64
FRESNEL = 0.1

FOLD = GRID // 2
BLOCKS = 3
LANES = 128
PAIR = 2 * LANES
DEPTH = BLOCKS * PAIR
FREQS = BLOCKS * LANES
COL_TILES = FOLD // PAIR
CUT_STEPS = 4
VMEM_BYTES = 67043328


def angles_of(first, second):
    return (2.0 * math.pi / GRID) * (np.outer(first, second) % GRID)


def cos_sin(first, second):
    angle = angles_of(first, second)
    return np.stack([np.cos(angle), np.sin(angle)])


def freqs(parity):
    return 2 * np.arange(FREQS) + parity


def both(function):
    return np.stack([function(freqs(0)), function(freqs(1))])


def halves_of(value):
    high = value.astype(jnp.bfloat16)
    return high, (value - high.astype(jnp.float32)).astype(jnp.bfloat16)


def dot3(left, right):
    def term(first, second):
        return jnp.dot(first, second, preferred_element_type=jnp.float32)

    return term(left[0], right[0]) + term(left[0], right[1]) + term(left[1], right[0])


def paired(values):
    blocks = values.reshape(values.shape[:-1] + (-1, LANES))
    return np.moveaxis(blocks, 0, -2).reshape(values.shape[1:-1] + (-1,))


def table_halves(table):
    high = table.astype(jnp.bfloat16)
    low = (table - high.astype(np.float64)).astype(jnp.bfloat16)
    return jnp.asarray(high), jnp.asarray(low)


def put(refs, place, value):
    high, low = halves_of(value)
    refs[0][place] = high
    refs[1][place] = low


def sign_of(info_ref):
    return 1.0 - 2.0 * info_ref[2].astype(jnp.float32)


def split_kernel(info_ref, wave_ref, trans_ref, mine_ref, theirs_ref):
    wave_re, wave_im = wave_ref[0, 0], wave_ref[1, 0]
    trans_re, trans_im = trans_ref[0, 0], trans_ref[0, 1]
    sign = sign_of(info_ref)
    for part, value in enumerate(
        (wave_re * trans_re - wave_im * trans_im, wave_re * trans_im + wave_im * trans_re)
    ):
        low, high = value[:, :FOLD], sign * value[:, FOLD:]
        mine_ref[part] = low + high
        theirs_ref[part] = low - high


def split_columns(info, plane_waves, transmission):
    rows = plane_waves.shape[2]
    step = 32
    out = jax.ShapeDtypeStruct((2, rows, FOLD), jnp.float32)
    out_spec = pl.BlockSpec((2, step, FOLD), lambda i, *_: (0, i, 0))
    return pl.pallas_call(
        split_kernel,
        out_shape=(out, out),
        grid_spec=pltpu.PrefetchScalarGridSpec(
            num_scalar_prefetch=1,
            grid=(rows // step,),
            in_specs=[
                pl.BlockSpec((2, 1, step, GRID), lambda i, *_: (0, 0, i, 0)),
                pl.BlockSpec((1, 2, step, GRID), lambda i, *_: (0, 0, i, 0)),
            ],
            out_specs=(out_spec, out_spec),
        ),
        cost_estimate=pl.CostEstimate(
            flops=20 * rows * GRID, bytes_accessed=24 * rows * GRID, transcendentals=0
        ),
        name="split_columns",
    )(info, plane_waves, transmission)


def column_forward_table():
    return table_halves(both(lambda freq: paired(cos_sin(np.arange(FOLD), freq))))


def column_forward_kernel(info_ref, field_ref, table_hi, table_lo, out_ref, *field):
    rows = field_ref.shape[1]

    @pl.when(pl.program_id(0) == 0)
    def _():
        for part in (0, 1):
            put(field, slice(part * rows, (part + 1) * rows), field_ref[part])

    result = dot3((field[0][...], field[1][...]), (table_hi[0], table_lo[0]))
    for part in (0, 1):
        out_ref[part] = result[part * rows : (part + 1) * rows]


def column_forward(info, field):
    rows = field.shape[1]
    table = column_forward_table()
    table_spec = pl.BlockSpec((1, FOLD, PAIR), lambda j, info: (info[2], 0, j))
    return pl.pallas_call(
        column_forward_kernel,
        out_shape=jax.ShapeDtypeStruct((2, rows, DEPTH), jnp.float32),
        grid_spec=pltpu.PrefetchScalarGridSpec(
            num_scalar_prefetch=1,
            grid=(BLOCKS,),
            in_specs=[
                pl.BlockSpec((2, rows, FOLD), lambda j, *_: (0, 0, 0)),
                table_spec,
                table_spec,
            ],
            out_specs=pl.BlockSpec((2, rows, PAIR), lambda j, *_: (0, 0, j)),
            scratch_shapes=[pltpu.VMEM((2 * rows, FOLD), jnp.bfloat16)] * 2,
        ),
        cost_estimate=pl.CostEstimate(
            flops=12 * rows * FOLD * DEPTH,
            bytes_accessed=8 * rows * (FOLD + DEPTH),
            transcendentals=0,
        ),
        compiler_params=pltpu.CompilerParams(vmem_limit_bytes=VMEM_BYTES),
        name="column_forward",
    )(info, field, *table)


def row_forward_kernel(
    info_ref, mine_ref, theirs_ref, col_hi, col_lo, table_hi, table_lo, down_ref, along_ref,
    out_hi, out_lo, field_hi, field_lo, theirs_hi, theirs_lo,
):
    rows = mine_ref.shape[1]
    field = (field_hi, field_lo)
    core = info_ref[2]

    @pl.when(pl.program_id(0) == 0)
    def _():
        for part in (0, 1):
            put((theirs_hi, theirs_lo), slice(part * rows, (part + 1) * rows), theirs_ref[part])

    theirs = dot3((theirs_hi[...], theirs_lo[...]), (col_hi[0], col_lo[0]))
    here = pl.ds(pl.multiple_of(core * rows, LANES), rows)
    there = pl.ds(pl.multiple_of((1 - core) * rows, LANES), rows)
    for part in (0, 1):
        cols = slice(part * PAIR, (part + 1) * PAIR)
        put(field, (here, cols), mine_ref[part])
        put(field, (there, cols), theirs[part * rows : (part + 1) * rows])
    cos_x, sin_x, square_x = (along_ref[0, i : i + 1] for i in range(3))
    outs = (out_hi, out_lo)

    def blocks(parity, count):
        first = parity * DEPTH
        part = slice(first, first + count * PAIR)
        result = dot3((table_hi[part], table_lo[part]), (field_hi[...], field_lo[...]))
        for block in range(count):
            freq = slice((parity * BLOCKS + block) * LANES, (parity * BLOCKS + block + 1) * LANES)
            cos_y, sin_y, square_y = (down_ref[freq, i : i + 1] for i in range(3))
            inside = 9.0 * (square_y + square_x) <= GRID * GRID
            prop_re = jnp.where(inside, cos_y * cos_x - sin_y * sin_x, 0.0)
            prop_im = jnp.where(inside, -(sin_y * cos_x + cos_y * sin_x), 0.0)
            for kind in (0, 1):
                start = block * PAIR + kind * LANES
                place = slice(first + start, first + start + LANES)
                for side in (0, 1):
                    cols = slice(side * LANES, (side + 1) * LANES)
                    real_part = result[start : start + LANES, cols]
                    imag_part = result[start : start + LANES, slice(PAIR + side * LANES, PAIR + (side + 1) * LANES)]
                    put(outs, (0, place, cols), prop_re * real_part - prop_im * imag_part)
                    put(outs, (1, place, cols), prop_re * imag_part + prop_im * real_part)

    last = pl.program_id(0) == BLOCKS - 1
    for parity in (0, 1):
        pl.when(last)(functools.partial(blocks, parity, BLOCKS - 1))
        pl.when(jnp.logical_not(last))(functools.partial(blocks, parity, BLOCKS))


def axis_factors(freq):
    angle = freq.astype(np.float64) ** 2 * (math.pi * FRESNEL / GRID)
    weight = np.where(freq == 0, 1.0, 2.0) / GRID
    return [np.cos(angle) * weight, np.sin(angle) * weight, freq.astype(np.float64) ** 2]


def row_forward(info, mine, theirs):
    rows = mine.shape[1]
    all_freqs = np.concatenate([freqs(0), freqs(1)])
    table = table_halves(paired(cos_sin(np.arange(2 * rows), all_freqs)).T)
    down = np.stack(axis_factors(all_freqs)).T.astype(np.float32)
    along = both(lambda freq: np.stack(axis_factors(freq))).astype(np.float32)
    tile = pl.BlockSpec((2, rows, PAIR), lambda j, *_: (0, 0, j))
    out = jax.ShapeDtypeStruct((2, 2 * DEPTH, DEPTH), jnp.bfloat16)
    out_spec = pl.BlockSpec((2, 2 * DEPTH, PAIR), lambda j, *_: (0, 0, j))
    table_spec = pl.BlockSpec(
        (2 * DEPTH, 2 * rows), lambda j, *_: (0, 0), pipeline_mode=pl.Buffered(1)
    )
    col_spec = pl.BlockSpec((1, FOLD, PAIR), lambda j, info: (info[2], 0, j))
    return pl.pallas_call(
        row_forward_kernel,
        out_shape=(out, out),
        grid_spec=pltpu.PrefetchScalarGridSpec(
            num_scalar_prefetch=1,
            grid=(BLOCKS,),
            in_specs=[
                tile,
                pl.BlockSpec(
                    (2, rows, FOLD), lambda j, *_: (0, 0, 0), pipeline_mode=pl.Buffered(1)
                ),
                col_spec,
                col_spec,
                table_spec,
                table_spec,
                pl.BlockSpec(down.shape, lambda j, *_: (0, 0)),
                pl.BlockSpec((1, 3, LANES), lambda j, info: (info[2], 0, j)),
            ],
            out_specs=(out_spec, out_spec),
            scratch_shapes=[pltpu.VMEM((2 * rows, 2 * PAIR), jnp.bfloat16)] * 2
            + [pltpu.VMEM((2 * rows, FOLD), jnp.bfloat16)] * 2,
        ),
        cost_estimate=pl.CostEstimate(
            flops=48 * rows * DEPTH * DEPTH,
            bytes_accessed=16 * rows * DEPTH + 16 * DEPTH * DEPTH,
            transcendentals=0,
        ),
        compiler_params=pltpu.CompilerParams(vmem_limit_bytes=VMEM_BYTES),
        name="row_forward",
    )(
        info, mine, theirs, *column_forward_table(), *table, jnp.asarray(down),
        jnp.asarray(along),
    )


def cut_slots(layout, first, info_ref, slot_ref, pos_ref, weight_ref, field, outs):
    chip_rows, waves, own, _ = layout
    height = chip_rows + WINDOW
    lane = lax.broadcasted_iota(jnp.int32, (WINDOW, WINDOW), 1)
    row_rank, wave_rank = info_ref[0], info_ref[1]

    def one(index, out_ref, place):
        target = row_rank ^ slot_ref[0, index]
        probe = (target * waves + (wave_rank ^ slot_ref[1, index])) * own + slot_ref[2, index]
        row = slot_ref[3, index] * height + lax.rem(pos_ref[probe, 0], chip_rows)
        start = lax.rem(pos_ref[probe, 1] + (GRID - HALF), GRID)
        col = lax.rem(start, FOLD)
        turned = jnp.where(start >= FOLD, sign_of(info_ref), 1.0)
        shift = lax.rem(col, LANES)
        back = lax.rem(LANES - shift, LANES)

        def cut(part):
            sides = [
                pltpu.roll(field[part, col // LANES + side, pl.ds(row, WINDOW)], back, 1)
                for side in (0, 1)
            ]
            return jnp.where(lane < LANES - shift, sides[0], sides[1])

        real_part, imag_part = cut(0), cut(1)
        weight_re, weight_im = weight_ref[0, probe] * turned, weight_ref[1, probe] * turned
        out_ref[place, 0] = weight_re * real_part - weight_im * imag_part
        out_ref[place, 1] = weight_re * imag_part + weight_im * real_part

    keep_ref, send_ref = outs
    total = slot_ref.shape[1] // 2

    @pl.loop(0, keep_ref.shape[0])
    def _(place):
        one(total + first + place, send_ref, place)
        one(first + place, keep_ref, place)


def inverse_kernel(
    layout, cuts, base, info_ref, slot_ref, pos_ref, weight_ref,
    spec_hi, spec_lo, row_hi, row_lo, col_hi, col_lo, *refs,
):
    chip_rows, _, _, segments = layout
    height = chip_rows + WINDOW
    refs = list(refs)
    outs = refs[:2]
    exports = refs[2:4] if len(refs) > 5 else None
    rows, field = refs[-3:-1], refs[-1]
    step = pl.program_id(0)
    first = 2 * BLOCKS
    last = first + 2 * cuts * COL_TILES

    def row_part(depth):
        part = step // BLOCKS
        place = pl.multiple_of(step % BLOCKS * PAIR, PAIR)
        cols = pl.ds(place, PAIR)
        count = row_hi.shape[0]
        sums = []
        for parity in (0, 1):
            freq = slice(parity * DEPTH, parity * DEPTH + depth * PAIR)
            sums.append(
                dot3((row_hi[:, freq], row_lo[:, freq]), (spec_hi[0, freq], spec_lo[0, freq]))
            )
        put(rows, (part, slice(0, count), cols), sums[0] + sums[1])
        put(rows, (part, slice(count, 2 * count), cols), sums[0] - sums[1])
        if exports is not None:
            for index in range(segments):
                start = pl.multiple_of(info_ref[base + cuts + index] * height, LANES)
                for export, source in zip(exports, rows):
                    export[0, index * height : (index + 1) * height] = source[
                        part, pl.ds(start, height), cols
                    ]

    zero_blocks = step % BLOCKS == BLOCKS - 1
    pl.when((step < first) & zero_blocks)(functools.partial(row_part, BLOCKS - 1))
    pl.when((step < first) & jnp.logical_not(zero_blocks))(functools.partial(row_part, BLOCKS))

    @pl.when((step >= first) & (step < last))
    def _():
        now = step - first
        tile = now % COL_TILES
        part = now // COL_TILES % 2
        segment = now // (2 * COL_TILES)
        source = pl.ds(pl.multiple_of(info_ref[base + segment] * height, LANES), height)
        place = pl.ds(pl.multiple_of(segment * height, LANES), height)
        value = dot3((rows[0][part, source], rows[1][part, source]), (col_hi[0], col_lo[0]))
        field[part, 2 * tile, place] = value[:, :LANES]
        field[part, 2 * tile + 1, place] = value[:, LANES:]

        @pl.when(tile == 0)
        def _():
            field[part, 2 * COL_TILES, place] = value[:, :LANES] * sign_of(info_ref)

    @pl.when(step >= last)
    def _():
        begin = (step - last) * outs[0].shape[0]
        cut_slots(layout, begin, info_ref, slot_ref, pos_ref, weight_ref, field, outs)


def window_spec(count, last):
    return pl.BlockSpec(
        (count // CUT_STEPS, 2, WINDOW, WINDOW),
        lambda i, *_: (jnp.maximum(i - last, 0), 0, 0, 0),
    )


def column_table():
    return table_halves(both(lambda freq: paired(cos_sin(np.arange(FOLD), freq)).T))


def inverse(layout, cuts, export, base, spectrum, row_list, slots, info, positions, weights):
    chip_rows, _, _, segments = layout
    height = chip_rows + WINDOW
    count = slots.shape[1] // 2
    tall = len(row_list)
    row_table = table_halves(paired(cos_sin(row_list, np.concatenate([freqs(0), freqs(1)]))))
    first = 2 * BLOCKS
    last = first + 2 * cuts * COL_TILES

    def spec_map(i, *_):
        i = jnp.minimum(i, first - 1)
        return i // BLOCKS, 0, i % BLOCKS

    def col_map(i, info, *_):
        return info[2], 0, (jnp.clip(i, first, last - 1) - first) % COL_TILES

    spec = pl.BlockSpec((1, 2 * DEPTH, PAIR), spec_map)
    row_spec = pl.BlockSpec(
        (tall, 2 * DEPTH), lambda i, *_: (0, 0), pipeline_mode=pl.Buffered(1)
    )
    col_spec = pl.BlockSpec((1, DEPTH, PAIR), col_map)
    shapes = [jax.ShapeDtypeStruct((count, 2, WINDOW, WINDOW), jnp.float32)] * 2
    specs = [window_spec(count, last)] * 2
    if export:
        shapes += [jax.ShapeDtypeStruct((2, segments * height, DEPTH), jnp.bfloat16)] * 2
        specs += [pl.BlockSpec((1, segments * height, PAIR), spec_map)] * 2
    return pl.pallas_call(
        functools.partial(inverse_kernel, layout, cuts, base),
        out_shape=shapes,
        grid_spec=pltpu.PrefetchScalarGridSpec(
            num_scalar_prefetch=4,
            grid=(last + CUT_STEPS,),
            in_specs=[spec, spec, row_spec, row_spec, col_spec, col_spec],
            out_specs=specs,
            scratch_shapes=[
                pltpu.VMEM((2, 2 * tall, DEPTH), jnp.bfloat16),
                pltpu.VMEM((2, 2 * tall, DEPTH), jnp.bfloat16),
                pltpu.VMEM((2, 2 * COL_TILES + 1, cuts * height, WINDOW), jnp.float32),
            ],
        ),
        cost_estimate=pl.CostEstimate(
            flops=24 * tall * DEPTH * DEPTH + 12 * cuts * height * DEPTH * FOLD,
            bytes_accessed=16 * DEPTH * DEPTH + 16 * tall * DEPTH,
            transcendentals=0,
        ),
        name="inverse",
    )(
        info, jnp.asarray(slots), positions, weights, *spectrum, *row_table, *column_table(),
    )


def column_inverse_kernel(
    layout, info_ref, slot_ref, pos_ref, weight_ref,
    rows_hi, rows_lo, table_hi, table_lo, keep_ref, send_ref, field,
):
    chip_rows, _, _, segments = layout
    height = chip_rows + WINDOW
    step = pl.program_id(0)
    tile = step % COL_TILES

    @pl.when(step < 2 * segments * COL_TILES)
    def _():
        part = step // COL_TILES % 2
        start = pl.multiple_of(step // (2 * COL_TILES) * height, LANES)
        rows = pl.ds(start, height)
        value = dot3((rows_hi[0], rows_lo[0]), (table_hi[0], table_lo[0]))
        field[part, 2 * tile, rows] = value[:, :LANES]
        field[part, 2 * tile + 1, rows] = value[:, LANES:]

        @pl.when(tile == 0)
        def _():
            field[part, 2 * COL_TILES, rows] = value[:, :LANES] * sign_of(info_ref)

    @pl.when(step >= 2 * segments * COL_TILES)
    def _():
        begin = (step - 2 * segments * COL_TILES) * keep_ref.shape[0]
        outs = (keep_ref, send_ref)
        cut_slots(layout, begin, info_ref, slot_ref, pos_ref, weight_ref, field, outs)


def column_inverse(layout, rows, slots, info, positions, weights):
    chip_rows, _, _, segments = layout
    count = slots.shape[1] // 2
    height = chip_rows + WINDOW
    table = column_table()
    last = 2 * segments * COL_TILES - 1

    def rows_map(i, info, *_):
        i = jnp.minimum(i, last)
        return i // COL_TILES % 2, i // (2 * COL_TILES), 0

    rows_spec = pl.BlockSpec((1, height, DEPTH), rows_map)
    table_spec = pl.BlockSpec(
        (1, DEPTH, PAIR), lambda i, info, *_: (info[2], 0, jnp.minimum(i, last) % COL_TILES)
    )
    out = jax.ShapeDtypeStruct((count, 2, WINDOW, WINDOW), jnp.float32)
    out_spec = window_spec(count, last + 1)
    return pl.pallas_call(
        functools.partial(column_inverse_kernel, layout),
        out_shape=(out, out),
        grid_spec=pltpu.PrefetchScalarGridSpec(
            num_scalar_prefetch=4,
            grid=(last + 1 + CUT_STEPS,),
            in_specs=[
                rows_spec,
                rows_spec,
                table_spec,
                table_spec,
            ],
            out_specs=(out_spec, out_spec),
            scratch_shapes=[
                pltpu.VMEM((2, 2 * COL_TILES + 1, segments * height, WINDOW), jnp.float32)
            ],
        ),
        cost_estimate=pl.CostEstimate(
            flops=12 * segments * height * DEPTH * FOLD,
            bytes_accessed=8 * segments * height * DEPTH + 16 * count * WINDOW * WINDOW,
            transcendentals=0,
        ),
        compiler_params=pltpu.CompilerParams(vmem_limit_bytes=VMEM_BYTES),
        name="column_inverse",
    )(
        info, jnp.asarray(slots), positions, weights, *rows, *table,
    )


def sum_kernel(count, halve, *refs):
    total = refs[0][0]
    for ref in refs[1:count]:
        total += ref[0]
    if halve:
        refs[count][...] = total[0]
        refs[count + 1][...] = total[1]
    else:
        refs[count][...] = total


def sum_of(terms, halve):
    tail = terms[0][0].shape[1:]
    zeros = (0,) * len(tail)
    count = terms[0][0].shape[0] // terms[0][2] // (2 if halve else 1)
    step = max(1, count // 2)
    specs, arrays = [], []
    for array, part, parts in terms:
        if halve:
            arrays.append(array.reshape((parts, 2, count) + tail))
            specs.append(
                pl.BlockSpec((1, 2, step) + tail, lambda i, part=part: (part, 0, i) + zeros)
            )
        else:
            arrays.append(array.reshape((parts, count) + tail))
            specs.append(
                pl.BlockSpec((1, step) + tail, lambda i, part=part: (part, i) + zeros)
            )
    out = jax.ShapeDtypeStruct((count,) + tail, jnp.float32)
    out_spec = pl.BlockSpec((step,) + tail, lambda i: (i,) + zeros)
    size = count * 4 * math.prod(tail) * (2 if halve else 1)
    return pl.pallas_call(
        functools.partial(sum_kernel, len(terms), halve),
        out_shape=(out, out) if halve else out,
        grid=(count // step,),
        in_specs=specs,
        out_specs=(out_spec, out_spec) if halve else out_spec,
        cost_estimate=pl.CostEstimate(
            flops=size, bytes_accessed=(len(terms) + 1) * size, transcendentals=0
        ),
        compiler_params=pltpu.CompilerParams(vmem_limit_bytes=VMEM_BYTES),
        name="sum_of",
    )(*arrays)


def spread_kernel(first_ref, second_ref, *outs):
    for index, out_ref in enumerate(outs):
        out_ref[...] = first_ref[index] + second_ref[index]


def spread_sum(first, second, count):
    tail = first.shape[1:]
    zeros = (0,) * len(tail)
    size = first.shape[0] // count
    step = max(1, size // 2)
    out = jax.ShapeDtypeStruct((size,) + tail, jnp.float32)
    spec = pl.BlockSpec((count, step) + tail, lambda i: (0, i) + zeros)
    return pl.pallas_call(
        spread_kernel,
        out_shape=[out] * count,
        grid=(size // step,),
        in_specs=[spec, spec],
        out_specs=[pl.BlockSpec((step,) + tail, lambda i: (i,) + zeros)] * count,
        cost_estimate=pl.CostEstimate(
            flops=first.size, bytes_accessed=12 * first.size, transcendentals=0
        ),
        compiler_params=pltpu.CompilerParams(vmem_limit_bytes=VMEM_BYTES),
        name="spread_sum",
    )(*(value.reshape((count, size) + tail) for value in (first, second)))


def power_kernel(count, scale, *refs):
    terms, (down_ref, along_ref, out_ref) = refs[:count], refs[count:]
    down, along = halves_of(down_ref[...]), halves_of(along_ref[...])
    total = terms[0][0, 0]
    for term in terms[1:]:
        total += term[0, 0]
    value = dot3(down, halves_of(jnp.concatenate([total[0], total[1]], axis=1)))
    cos_part, sin_part = value[:WINDOW], value[WINDOW:]
    real_part = cos_part[:, :WINDOW] + sin_part[:, WINDOW:]
    imag_part = cos_part[:, WINDOW:] - sin_part[:, :WINDOW]
    value = dot3(halves_of(jnp.concatenate([real_part, imag_part])), along)
    real_part = value[:WINDOW, :WINDOW] + value[WINDOW:, WINDOW:]
    imag_part = value[WINDOW:, :WINDOW] - value[:WINDOW, WINDOW:]
    out_ref[0] = (real_part * real_part + imag_part * imag_part) * scale


def power_of(terms, scale):
    tail = terms[0][0].shape[1:]
    count = terms[0][0].shape[0] // terms[0][2]
    table = cos_sin(np.arange(WINDOW), FACTOR * np.arange(WINDOW)).astype(np.float32)
    down, along = np.concatenate(list(table)), np.concatenate(list(table), axis=1)
    return pl.pallas_call(
        functools.partial(power_kernel, len(terms), scale),
        out_shape=jax.ShapeDtypeStruct((count, WINDOW, WINDOW), jnp.float32),
        grid=(count,),
        in_specs=[
            pl.BlockSpec((1, 1) + tail, lambda i, part=part: (part, i, 0, 0, 0))
            for _, part, _ in terms
        ]
        + [
            pl.BlockSpec(down.shape, lambda i: (0, 0)),
            pl.BlockSpec(along.shape, lambda i: (0, 0)),
        ],
        out_specs=pl.BlockSpec((1, WINDOW, WINDOW), lambda i: (i, 0, 0)),
        compiler_params=pltpu.CompilerParams(vmem_limit_bytes=VMEM_BYTES),
        name="power_of",
    )(
        *(array.reshape((parts, count) + tail) for array, _, parts in terms),
        jnp.asarray(down), jnp.asarray(along),
    )


def coefficients(positions, wave_index, wave_weight, wave_phase):
    turns = (
        FACTOR * (positions[:, 0] * wave_index[0, 0] + positions[:, 1] * wave_index[0, 1])
    ) % GRID
    angles = wave_phase[0] - turns.astype(jnp.float32) * (2.0 * math.pi / GRID)
    return wave_weight[0] * jnp.stack([jnp.cos(angles), jnp.sin(angles)])


def flip(block, axis, bit):
    count = lax.axis_size(axis)
    return lax.ppermute(block, axis, [(i, i ^ bit) for i in range(count)])


def diffraction(plane_waves, transmission, wave_index, wave_weight, wave_phase, probe_pos):
    rows_here = plane_waves.shape[2]
    row_count = lax.axis_size("row")
    wave_count = lax.axis_size("wave")
    row_rank = lax.axis_index("row")
    wave_rank = lax.axis_index("wave")
    core = row_rank % 2
    chip_rows = 2 * rows_here
    chips = row_count // 2
    far = chips // 2
    own = probe_pos.shape[0] // (row_count * wave_count)

    segments = far // 2
    layout = (chip_rows, wave_count, own, segments)

    def slots_of(odd, halves):
        slots = []
        for core_bit in (0, 1):
            for wave in range(wave_count):
                for at, half in enumerate(halves):
                    for index in range(segments):
                        row = ((half * segments + index) * 2 + odd) * 2 + core_bit
                        where = at * segments + index
                        slots += [(row, wave, probe, where) for probe in range(own)]
        return np.array(slots, np.int32).T

    upper, lower = 1, 0
    chip = row_rank // 2
    info = [row_rank, wave_rank, core]
    for odd in (1, 0):
        for half in (upper, lower):
            for index in range(segments):
                target = chip ^ ((half * segments + index) * 2 + odd)
                away = (target - chip) % chips
                info.append(away // far * segments + away % far // 2)
    info = jnp.stack(info)

    mine, theirs = split_columns(info, plane_waves, transmission)
    theirs = flip(theirs, "row", 1)
    weights = coefficients(probe_pos, wave_index, wave_weight, wave_phase)
    mine = column_forward(info, mine)
    mine, theirs = lax.optimization_barrier((mine, theirs))
    spectrum = row_forward(info, mine, theirs)

    def rows_of(odd):
        return np.concatenate(
            [
                chip_rows * away - HALF + np.arange(chip_rows + WINDOW)
                for away in range(odd, far, 2)
            ]
        )

    def later(value, *before):
        return lax.optimization_barrier((value,) + before)

    def over_waves(pieces):
        terms = [(pieces[0], 0, 1)]
        for bits, piece in enumerate(pieces):
            if bits:
                terms.append((flip(piece, "wave", bits), 0, 1))
        return terms

    common = (info, probe_pos, weights)
    keep, send = inverse(
        layout, 2 * segments, False, 3, spectrum, rows_of(1), slots_of(1, (upper, lower)), *common
    )
    arrived = flip(send, "row", 1)
    spectrum, keep = later(spectrum, keep)
    keep_upper, send, rows_hi, rows_lo = inverse(
        layout, segments, True, 3 + far, spectrum, rows_of(0), slots_of(0, (upper,)), *common
    )
    arrived_upper = flip(send, "row", 1)
    pieces = spread_sum(keep, arrived, wave_count)
    (rows_hi, rows_lo), pieces = later((rows_hi, rows_lo), pieces)
    odd_terms = over_waves(pieces)
    keep_lower, send = column_inverse(layout, (rows_hi, rows_lo), slots_of(0, (lower,)), *common)
    arrived_lower = flip(send, "row", 1)
    pieces = spread_sum(keep_upper, arrived_upper, wave_count)
    lower_pieces = spread_sum(keep_lower, arrived_lower, wave_count)
    odd_arrays, pieces, lower_pieces = later(
        [term[0] for term in odd_terms], pieces, lower_pieces
    )
    odd_terms = [(array, 0, 1) for array in odd_arrays]
    upper_terms = over_waves(pieces)
    near = flip(sum_of(odd_terms, False), "row", 2)
    lower_terms = over_waves(lower_pieces)

    bit = row_count // 2
    send = sum_of(upper_terms + [(near, 0, 2)], False)
    terms = lower_terms + [(near, 1, 2), (flip(send, "row", bit), 0, 1)]
    while bit > 4:
        bit //= 2
        stay, send = sum_of(terms, True)
        terms = [(stay, 0, 1), (flip(send, "row", bit), 0, 1)]
    total_waves = plane_waves.shape[1] * wave_count
    power = power_of(terms, 1.0 / (WINDOW * WINDOW * total_waves))
    return lax.all_to_all(power, "wave", split_axis=1, concat_axis=0, tiled=True)


def solution(mesh):
    return jax.shard_map(
        diffraction,
        mesh=mesh,
        in_specs=(
            P(None, "wave", "row", None),
            P(None, None, "row", None),
            P("wave", None),
            P("wave"),
            P("wave"),
            P(),
        ),
        out_specs=P("row", "wave", None),
        check_vma=False,
    )
```
